32 devices in a mesh: grp: 8 (over y, x, core), seq: 4 (over z).
Axes of the slice: x: 2, y: 2, z: 4, core: 2. Of those that a mesh axis runs over, the one named last changes fastest.
Arguments:
- frames: bfloat16 [8, 1500, 512], P('grp', 'seq'), may hold values from -6 to 6
- input_ids: int32 [8, 448], P('grp'), may hold values from 0 to 51879
- target_ids: int32 [8, 448], P('grp'), may hold values from 0 to 51879
- lengths: int32 [8], replicated, may hold values from 56 to 448, as said below
- present: int32 [8], replicated, may hold values from 0 to 1, as said below
- step_count: int32 [1], replicated, may hold values from 1 to 20
- enc_params: float32 [3392000], P(('grp', 'seq'))
- enc_moment: float32 [3392000], P(('grp', 'seq')), may hold values from -0.00012207031 to 0.00012207031
- enc_second: float32 [3392000], P(('grp', 'seq')), may hold values from 1e-11 to 1e-10
- dec_params: float32 [4194304], P(('grp', 'seq'))
- dec_moment: float32 [4194304], P(('grp', 'seq')), may hold values from -0.00012207031 to 0.00012207031
- dec_second: float32 [4194304], P(('grp', 'seq')), may hold values from 1e-11 to 1e-10
- table_params: float32 [512, 51880], P('grp', 'seq'), may hold values from -0.5 to 0.5
- table_moment: float32 [512, 51880], P('grp', 'seq'), may hold values from -0.00012207031 to 0.00012207031
- table_second: float32 [512, 51880], P('grp', 'seq'), may hold values from 1e-11 to 1e-10
Outputs:
- mean_loss: float32 [], replicated
- grad_norm: float32 [], replicated
- new_enc_params: float32 [3392000], P(('grp', 'seq'))
- new_enc_moment: float32 [3392000], P(('grp', 'seq'))
- new_enc_second: float32 [3392000], P(('grp', 'seq'))
- new_dec_params: float32 [4194304], P(('grp', 'seq'))
- new_dec_moment: float32 [4194304], P(('grp', 'seq'))
- new_dec_second: float32 [4194304], P(('grp', 'seq'))
- new_table_params: float32 [512, 51880], P('grp', 'seq')
- new_table_moment: float32 [512, 51880], P('grp', 'seq')
- new_table_second: float32 [512, 51880], P('grp', 'seq')
The draws below stay inside these ranges and needn't reach their ends.
Inputs may be any that keep to these rules, and one draw needn't show every extreme that they name: `lengths`: some clip slot has length exactly 448. `present`: at least one slot holds a clip.
All inputs are finite; a program needn't handle non-finite values.
Results may differ from the reference program's by a relative error of at most 0.00275.
The reference program's roundings to bfloat16 on the way count: a program that leaves them out, or rounds other values in their place, can miss the bound.
Values may be sent and summed in bfloat16 or wider, within the bound.
No kernel may reach another device: no remote copies, remote signals or barrier semaphores. Data moves between devices by JAX's collectives and lax.ppermute only.
A program may use at most 320 MiB of HBM per device.

```python
import math
import jax
import jax.numpy as jnp
import numpy as np
from jax import lax

D = 512
HEADS = 8
F = 2048
V = 51880
LEN = 448
FRAMES = 1500
CLIPS = 8
PE = 3392000
PD = 4194304


def draw_lengths(key, part):
    first_key, second_key = jax.random.split(jax.random.fold_in(key, 11))
    drawn = jax.random.randint(first_key, (CLIPS,), LEN // 8, LEN + 1)
    chosen = jax.random.randint(second_key, (), 0, CLIPS)
    return jnp.where(jnp.arange(CLIPS) == chosen, LEN, drawn).astype(jnp.int32)


def draw_present(key, part):
    first_key, second_key = jax.random.split(jax.random.fold_in(key, 23))
    drawn = (jax.random.randint(first_key, (CLIPS,), 0, 3) > 0).astype(jnp.int32)
    chosen = jax.random.randint(second_key, (), 0, CLIPS)
    return jnp.where(jnp.arange(CLIPS) == chosen, 1, drawn).astype(jnp.int32)


def flat_draw(key, pieces):
    scales = jnp.concatenate([jnp.full((amount,), scale_one, jnp.float32) for amount, scale_one, center_one in pieces])
    centers = jnp.concatenate([jnp.full((amount,), center_one, jnp.float32) for amount, scale_one, center_one in pieces])
    total_size = scales.shape[0]
    base_values = jax.random.normal(key, (total_size,), jnp.float32)
    return base_values * scales + centers


def draw_enc_params(key, part):
    pieces = [(3 * D * D, D ** (-0.5), 0.0), (D * D, 4.0 * D ** (-0.5), 0.0), (D * F, D ** (-0.5), 0.0), (F * D, F ** (-0.5), 0.0), (LEN * D, 0.1, 0.0), (7 * D, 0.1, 1.0), (6 * D, 0.3, 0.0), (D, 1.0, 0.0), (11 * D, 0.3, 0.0), (2 * F, 0.3, 0.0)]
    return flat_draw(jax.random.fold_in(key, 31), pieces)


def draw_dec_params(key, part):
    pieces = [(3 * D * D, D ** (-0.5), 0.0), (D * D, 4.0 * D ** (-0.5), 0.0), (D * D, D ** (-0.5), 0.0), (2 * D * D, D ** (-0.5), 0.0), (D * D, 4.0 * D ** (-0.5), 0.0), (D * F, D ** (-0.5), 0.0), (F * D, F ** (-0.5), 0.0)]
    return flat_draw(jax.random.fold_in(key, 37), pieces)


def plant(values, own_key, low, largest):
    dims = values.shape
    place = [jax.random.randint(jax.random.fold_in(own_key, axis), (), 0, dims[axis]) for axis in range(len(dims))]
    values = values.at[tuple(place)].set(low)
    longest = dims.index(max(dims))
    place[longest] = (place[longest] + 1) % dims[longest]
    return values.at[tuple(place)].set(largest)


def block_levels(stream_key, extent, shards, smallest, high):
    def one(axis_at, blocks):
        steps = jax.random.uniform(jax.random.fold_in(jax.random.fold_in(stream_key, 6), axis_at), (blocks,), jnp.float32, smallest / len(shards), high / len(shards))
        return jnp.repeat(jnp.exp(steps), extent[axis_at] // blocks).reshape((-1,) + (1,) * (len(extent) - axis_at - 1))

    level = one(*shards[0])
    for cut in shards[1:]:
        level = level * one(*cut)
    return level


def rank_table(number_of, skew):
    portions = [(1 << 20) // math.isqrt(grade ** skew) + 1 for grade in range(1, number_of + 1)]
    width = 1 + sum(portions) // (1 << 30)
    return np.cumsum(np.array([max(1, weight // width) for weight in portions]))


def ranked_ids(key, dims, count, skew):
    listing = rank_table(count, skew)
    ticket = jax.random.randint(jax.random.fold_in(key, 1), dims, 0, int(listing[count - 1]))
    rank = jnp.searchsorted(jnp.asarray(listing, jnp.int32), ticket, side="right")
    return jax.random.permutation(jax.random.fold_in(key, 2), count)[rank].astype(jnp.int32)


def gaussian(key, dims, scale, bound, cuts=(), held_as=jnp.bfloat16):
    array = jax.random.normal(key, dims, jnp.float32) * scale
    if len(cuts) > 0:
        array = block_levels(key, dims, cuts, -0.22, 0.18) * array
    return jnp.clip(array, min=-bound, max=bound).astype(held_as)


def setup_inputs(seed: int = 0) -> dict:
    key_list = jax.random.split(jax.random.key(seed), 16)
    frames = gaussian(key_list[0], (CLIPS, FRAMES, D), 1.0, 6.0, ((0, 8), (1, 4)))
    input_ids = plant(ranked_ids(key_list[1], (CLIPS, LEN), V, 2), jax.random.fold_in(key_list[1], 3), 0, V - 1).astype(jnp.int32)
    target_ids = plant(ranked_ids(key_list[2], (CLIPS, LEN), V, 2), jax.random.fold_in(key_list[2], 3), 0, V - 1).astype(jnp.int32)
    lengths = draw_lengths(jax.random.fold_in(key_list[15], 71), 0)
    present = draw_present(jax.random.fold_in(key_list[15], 71), 0)
    step_count = jax.random.randint(key_list[5], (1,), 1, 21).astype(jnp.int32)
    enc_params = draw_enc_params(jax.random.fold_in(key_list[15], 71), 0)
    enc_moment = gaussian(key_list[7], (PE,), 0.00002, 0.00012207031, ((0, 32),), jnp.float32)
    enc_second = jnp.clip(jnp.exp(math.log(1.000000013351432e-10) - 2.3025851 * jax.random.uniform(key_list[8], (PE,), jnp.float32) ** block_levels(key_list[8], (PE,), ((0, 32),), -0.2, 0.2)), 9.999999960041972e-12, 1.000000013351432e-10)
    dec_params = draw_dec_params(jax.random.fold_in(key_list[15], 71), 0)
    dec_moment = gaussian(key_list[10], (PD,), 0.00002, 0.00012207031, ((0, 32),), jnp.float32)
    dec_second = jnp.clip(jnp.exp(math.log(1.000000013351432e-10) - 2.3025851 * jax.random.uniform(key_list[11], (PD,), jnp.float32) ** block_levels(key_list[11], (PD,), ((0, 32),), -0.2, 0.2)), 9.999999960041972e-12, 1.000000013351432e-10)
    table_params = gaussian(key_list[12], (D, V), (D // 4) ** -0.5, 0.5, ((0, 8), (1, 4)), jnp.float32)
    table_moment = gaussian(key_list[13], (D, V), 0.00002, 0.00012207031, ((0, 8), (1, 4)), jnp.float32)
    table_second = jnp.clip(jnp.exp(math.log(1.000000013351432e-10) - 2.3025851 * jax.random.uniform(key_list[14], (D, V), jnp.float32) ** block_levels(key_list[14], (D, V), ((0, 8), (1, 4)), -0.2, 0.2)), 9.999999960041972e-12, 1.000000013351432e-10)
    return {"frames": frames, "input_ids": input_ids, "target_ids": target_ids, "lengths": lengths, "present": present, "step_count": step_count, "enc_params": enc_params, "enc_moment": enc_moment, "enc_second": enc_second, "dec_params": dec_params, "dec_moment": dec_moment, "dec_second": dec_second, "table_params": table_params, "table_moment": table_moment, "table_second": table_second}


highest = lax.Precision.HIGHEST
beta_one = 0.9
beta_two = 0.999
rate = 0.01
decay = 0.1
adam_eps = 1e-08
clip_limit = 1.0
norm_eps = 1e-05
masked_score = -1e+30

@jax.custom_vjp
def low(v):
    return lax.optimization_barrier(v.astype(jnp.bfloat16)).astype(jnp.float32)

@jax.custom_vjp
def low_back(v):
    return v

def low_keep(v):
    return (low(v), None)

def low_pass(kept, grad):
    return (grad,)

def back_keep(v):
    return (v, None)

def back_low(kept, grad):
    return (low(grad),)
low.defvjp(low_keep, low_pass)
low_back.defvjp(back_keep, back_low)

def layer_norm(values, norm_gain, norm_shift):
    center = values - lax.optimization_barrier(jnp.mean(values, axis=-1, keepdims=True))
    spread = lax.optimization_barrier(jnp.mean(center * center, axis=-1, keepdims=True))
    return center * lax.rsqrt(spread + norm_eps) * norm_gain + norm_shift

def sinusoid(amount, channels, offset):
    half_width = channels // 2
    stride = math.log(10000.0) / (half_width - 1)
    inverse = jnp.exp(-stride * jnp.arange(half_width, dtype=jnp.float32))
    angles = (jnp.arange(amount, dtype=jnp.float32) + offset)[:, None] * inverse[None, :]
    return jnp.concatenate([jnp.sin(angles), jnp.cos(angles)], axis=1)

def enc_layout():
    return [(D, 3 * D), (D, D), (D, F), (F, D), (LEN, D), (7, D), (7, D), (11, D), (2, F)]

def dec_layout():
    return [(D, 3 * D), (D, D), (D, D), (D, 2 * D), (D, D), (D, F), (F, D)]

def split_flat(flat_vec, layout):
    pieces = []
    offset = 0
    for matrix_dims in layout:
        amount = matrix_dims[0] * matrix_dims[1]
        pieces.append(flat_vec[offset:offset + amount].reshape(matrix_dims))
        offset += amount
    return pieces

def product(left_side, right_side):
    return jnp.dot(left_side, right_side, precision=highest)

def attend(query_raw, key_raw, value_raw, causal):
    query = low(low_back(query_raw))
    keys = low(low_back(key_raw))
    values = low(low_back(value_raw))
    query_rows = query.shape[0]
    key_rows = keys.shape[0]
    head_size = query.shape[1] // HEADS
    query_heads = query.reshape(query_rows, HEADS, head_size)
    key_heads = keys.reshape(key_rows, HEADS, head_size)
    value_heads = values.reshape(key_rows, HEADS, head_size)
    scores = jnp.einsum('qhd,khd->hqk', query_heads, key_heads, precision=highest) * head_size ** (-0.5)
    scores = low_back(scores)
    if causal:
        allowed = jnp.arange(query_rows)[:, None] >= jnp.arange(key_rows)[None, :]
        scores = jnp.where(allowed[None], scores, masked_score)
    weights = low(jax.nn.softmax(scores, axis=-1))
    mixed = jnp.einsum('hqk,khd->qhd', weights, value_heads, precision=highest).reshape(query_rows, -1)
    return low(low_back(mixed))

def feed_forward(stream, norm_gain, norm_shift, w_up, b_up, w_down, b_down):
    normed = low(layer_norm(stream, norm_gain, norm_shift))
    raised = low_back(product(normed, w_up) + b_up)
    active = low(jax.nn.gelu(raised, approximate=False))
    return low_back(product(active, w_down) + b_down)

def clip_loss(frame_rows, token_ids, target_row, length_one, present_one, enc_parts, dec_parts, table_low):
    enc_qkv, enc_wout, enc_wup, enc_wdown, positions, gains, shifts, biases, up_bias = enc_parts
    dec_qkv, dec_wout, cross_wq, cross_wkv, cross_wout, dec_wup, dec_wdown = dec_parts
    stream = frame_rows + sinusoid(FRAMES, D, 0.0)
    normed = low(layer_norm(stream, gains[0], shifts[0]))
    packed = product(normed, enc_qkv)
    mixed = attend(packed[:, :D] + biases[0], packed[:, D:2 * D], packed[:, 2 * D:] + biases[1], False)
    stream = stream + low_back(product(mixed, enc_wout) + biases[2])
    stream = stream + feed_forward(stream, gains[1], shifts[1], enc_wup, up_bias[0], enc_wdown, biases[3])
    encoded = low(layer_norm(stream, gains[2], shifts[2]))
    embedded = jnp.take(table_low, token_ids, axis=1).T
    stream = embedded + positions
    normed = low(layer_norm(stream, gains[3], shifts[3]))
    packed = product(normed, dec_qkv)
    mixed = attend(packed[:, :D] + biases[4], packed[:, D:2 * D], packed[:, 2 * D:] + biases[5], True)
    stream = stream + low_back(product(mixed, dec_wout) + biases[6])
    normed = low(layer_norm(stream, gains[4], shifts[4]))
    paired = product(encoded, cross_wkv)
    mixed = attend(product(normed, cross_wq) + biases[7], paired[:, :D], paired[:, D:] + biases[8], False)
    stream = stream + low_back(product(mixed, cross_wout) + biases[9])
    stream = stream + feed_forward(stream, gains[5], shifts[5], dec_wup, up_bias[1], dec_wdown, biases[10])
    states = low(layer_norm(stream, gains[6], shifts[6]))
    logits = low_back(product(states, table_low))
    log_total = jax.scipy.special.logsumexp(logits, axis=-1)
    picked = jnp.take_along_axis(logits, target_row[:, None], axis=1)[:, 0]
    valid = ((jnp.arange(LEN) < length_one) & (present_one > 0)).astype(jnp.float32)
    return jnp.sum((log_total - picked) * valid)

def adamw(weight_now, moment, second, gradient, factor, bias_one, bias_two):
    scaled = gradient * factor
    new_moment = beta_one * moment + (1.0 - beta_one) * scaled
    new_second = beta_two * second + (1.0 - beta_two) * scaled * scaled
    step_size = new_moment / bias_one / (jnp.sqrt(new_second / bias_two) + adam_eps) + decay * weight_now
    return (weight_now - rate * step_size, new_moment, new_second)

def reference(frames, input_ids, target_ids, lengths, present, step_count, enc_params, enc_moment, enc_second, dec_params, dec_moment, dec_second, table_params, table_moment, table_second):
    token_total = jnp.sum((lengths * present).astype(jnp.float32))
    frames_wide = frames.astype(jnp.float32)

    def total_loss(enc_flat, dec_flat, table_flat):
        enc_parts = split_flat(low(enc_flat), enc_layout())
        dec_parts = split_flat(low(dec_flat), dec_layout())
        table_low = low(table_flat)

        def clip_fn(frame_rows, token_ids, target_row, length_one, present_one):
            return clip_loss(frame_rows, token_ids, target_row, length_one, present_one, enc_parts, dec_parts, table_low)
        saved_fn = jax.checkpoint(clip_fn)

        def one_clip(running, clip_items):
            return (running + saved_fn(*clip_items), None)
        summed, unused = lax.scan(one_clip, jnp.zeros((), jnp.float32), (frames_wide, input_ids, target_ids, lengths, present))
        return summed / token_total
    mean_loss, pullback = jax.vjp(total_loss, enc_params, dec_params, table_params)
    enc_grad, dec_grad, table_grad = pullback(jnp.ones_like(mean_loss))
    squares = jnp.sum(enc_grad * enc_grad) + jnp.sum(dec_grad * dec_grad) + jnp.sum(table_grad * table_grad)
    grad_norm = jnp.sqrt(squares)
    factor = jnp.minimum(1.0, clip_limit / (grad_norm + 1e-06))
    steps_done = step_count[0].astype(jnp.float32)
    bias_one = 1.0 - beta_one ** steps_done
    bias_two = 1.0 - beta_two ** steps_done
    enc_new = adamw(enc_params, enc_moment, enc_second, enc_grad, factor, bias_one, bias_two)
    dec_new = adamw(dec_params, dec_moment, dec_second, dec_grad, factor, bias_one, bias_two)
    table_new = adamw(table_params, table_moment, table_second, table_grad, factor, bias_one, bias_two)
    return (mean_loss, grad_norm, enc_new[0], enc_new[1], enc_new[2], dec_new[0], dec_new[1], dec_new[2], table_new[0], table_new[1], table_new[2])
```

```python
from functools import partial
import math

import jax
import jax.numpy as jnp
from jax import lax
from jax.sharding import PartitionSpec as P

D = 512
HEADS = 8
F = 2048
LEN = 448
HEAD = D // HEADS


beta_one = 0.9
beta_two = 0.999
rate = 0.01
decay = 0.1
adam_eps = 1e-08
clip_limit = 1.0
norm_eps = 1e-05
masked_score = -1e30

bf16 = jnp.bfloat16
f32 = jnp.float32


def layer_norm(values, norm_gain, norm_shift):
    center = values - jnp.mean(values, axis=-1, keepdims=True)
    spread = jnp.mean(center * center, axis=-1, keepdims=True)
    return center * lax.rsqrt(spread + norm_eps) * norm_gain + norm_shift


def norm_back(grad_out, values, norm_gain, norm_shift):
    unused, pullback = jax.vjp(layer_norm, values, norm_gain, norm_shift)
    return pullback(grad_out)


def enc_layout():
    return [(D, 3 * D), (D, D), (D, F), (F, D), (LEN, D), (7, D), (7, D), (11, D), (2, F)]


def dec_layout():
    return [(D, 3 * D), (D, D), (D, D), (D, 2 * D), (D, D), (D, F), (F, D)]


def split_flat(flat_vec, layout):
    pieces = []
    offset = 0
    for matrix_dims in layout:
        amount = matrix_dims[0] * matrix_dims[1]
        pieces.append(flat_vec[offset : offset + amount].reshape(matrix_dims))
        offset += amount
    return pieces


def times(left_side, right_side):
    return jnp.dot(left_side, right_side, preferred_element_type=f32)


def times_back(left_side, right_side):
    return lax.dot_general(
        left_side, right_side, (((1,), (1,)), ((), ())), preferred_element_type=f32
    )


def over_rows(left_side, right_side):
    return lax.dot_general(
        left_side, right_side, (((0,), (0,)), ((), ())), preferred_element_type=f32
    )


def column_sum(values):
    return jnp.sum(values.astype(f32), axis=0)


def swap(value, axis, mask):
    count = lax.axis_size(axis)
    return lax.ppermute(value, axis, [(i, i ^ mask) for i in range(count)])


def reorder(items, rank):
    items = list(items)
    bit = 1
    while bit < len(items):
        odd = (rank & bit) != 0
        items = [jnp.where(odd, items[k ^ bit], items[k]) for k in range(len(items))]
        bit *= 2
    return items


def tree_join(items, join):
    items = list(items)
    while len(items) > 1:
        items = [join(items[k], items[k + 1]) for k in range(0, len(items), 2)]
    return items[0]


def all_join(value, axis, join):
    count = lax.axis_size(axis)
    return tree_join([value] + [swap(value, axis, k) for k in range(1, count)], join)


def gather_near(value, axis):
    return [value] + [swap(value, axis, k) for k in range(1, lax.axis_size(axis))]


def trade_near(items, axis):
    return [items[0]] + [swap(items[k], axis, k) for k in range(1, len(items))]


def bits_of(axis):
    count = lax.axis_size(axis)
    found = []
    bit = 1
    while bit < count:
        found.append(bit)
        bit *= 2
    return found


def group_orders():
    far = bits_of("grp")[1:]
    return far, far[::-1]


def grow(slots, bit):
    held = sorted(slots)
    sent = jnp.stack([slots[k] for k in held])
    came = swap(sent, "grp", bit)
    for place, k in enumerate(held):
        slots[k ^ bit] = came[place]
    return slots


def gather_group(value):
    half = value.shape[0] // 2
    parts = [value[:half], value[half:]]
    results = []
    for part, order in zip(parts, group_orders()):
        slots = {0: part}
        for bit in order + [1]:
            slots = grow(slots, bit)
        results.append(slots)
    count = lax.axis_size("grp")
    return jnp.stack([jnp.concatenate([r[k] for r in results]) for k in range(count)])


def reduce_group(slots, wire, hold=f32):
    count = lax.axis_size("grp")
    sent = jnp.stack([slots[k] for k in range(count) if k & 1]).astype(wire)
    came = swap(sent, "grp", 1)
    held = {k: slots[k].astype(hold) + came[k // 2].astype(hold) for k in range(0, count, 2)}
    half = slots[0].shape[0] // 2
    results = []
    for low, order in zip((0, half), group_orders()):
        part = {k: v[low : low + half] for k, v in held.items()}
        for bit in order:
            gone = [k for k in sorted(part) if k & bit]
            came = swap(jnp.stack([part[k] for k in gone]).astype(wire), "grp", bit)
            part = {
                k: v + came[gone.index(k ^ bit)].astype(hold)
                for k, v in part.items()
                if not k & bit
            }
        results.append(part[0])
    return jnp.concatenate(results)


def gather_flat(shard):
    seq_rank = lax.axis_index("seq")
    group_rank = lax.axis_index("grp")
    half = shard.shape[0] // 2
    parts = []
    far, back = group_orders()
    bits = bits_of("grp")
    for low, order in zip((0, half), (far, back)):
        part = shard[low : low + half]
        whole = jnp.stack(reorder(gather_near(part, "seq"), seq_rank))
        whole = whole.reshape((1,) * len(bits) + whole.shape)
        for bit in order + [1]:
            came = swap(whole, "grp", bit)
            upper = (group_rank & bit) != 0
            place = len(bits) - 1 - bits.index(bit)
            whole = jnp.concatenate(
                [jnp.where(upper, came, whole), jnp.where(upper, whole, came)], axis=place
            )
        parts.append(whole.reshape(-1, half))
    return jnp.concatenate(parts, axis=1).reshape(-1)


def reduce_blocks(blocks, wire=f32):
    group_rank = lax.axis_index("grp")
    bits = bits_of("grp")
    count = lax.axis_size("grp")
    rest = blocks.shape[1:]
    blocks = blocks.reshape((2,) * len(bits) + rest)

    def step(value, bit):
        place = len(bits) - 1 - bits.index(bit)
        mine = (group_rank & bit) // bit
        sent = lax.dynamic_slice_in_dim(value, 1 - mine, 1, place)
        kept = lax.dynamic_slice_in_dim(value, mine, 1, place)
        return kept + swap(sent.astype(wire), "grp", bit).astype(f32)

    blocks = step(blocks, 1)
    half = rest[-1] // 2
    results = []
    for low, order in zip((0, half), group_orders()):
        part = lax.slice_in_dim(blocks, low, low + half, axis=blocks.ndim - 1)
        for bit in order:
            part = step(part, bit)
        results.append(part.reshape(rest[:-1] + (half,)))
    return jnp.concatenate(results, axis=-1)


def scatter_near(items, axis, wire):
    came = [swap(items[k].astype(wire), axis, k).astype(f32) for k in range(1, len(items))]
    return tree_join([items[0].astype(f32)] + came, jnp.add)


def heads_of(values):
    return values.reshape(values.shape[0], values.shape[1] // HEAD, HEAD)


def scores_of(query, keys, allowed):
    scores = jnp.einsum(
        "qhd,khd->hqk", heads_of(query), heads_of(keys), preferred_element_type=f32
    ) * HEAD ** (-0.5)
    return jnp.where(allowed, scores, masked_score)


def attend_forward(query, keys, values, allowed):
    scores = scores_of(query, keys, allowed)
    highest = jnp.max(scores, axis=-1, keepdims=True)
    log_total = highest + jnp.log(jnp.sum(jnp.exp(scores - highest), axis=-1, keepdims=True))
    weights = jnp.exp(scores - log_total).astype(bf16)
    mixed = jnp.einsum("hqk,khd->qhd", weights, heads_of(values), preferred_element_type=f32)
    return mixed.reshape(query.shape).astype(bf16), log_total


def attend_backward(grad_mixed, query, keys, values, log_total, allowed):
    scores = scores_of(query, keys, allowed)
    weights = jnp.exp(scores - log_total)
    grad_heads = heads_of(grad_mixed)
    grad_weights = jnp.einsum(
        "qhd,khd->hqk", grad_heads, heads_of(values), preferred_element_type=f32
    )
    grad_values = jnp.einsum(
        "hqk,qhd->khd", weights.astype(bf16), grad_heads, preferred_element_type=f32
    )
    inner = jnp.sum(weights * grad_weights, axis=-1, keepdims=True)
    grad_scores = (weights * (grad_weights - inner)).astype(bf16)
    grad_query = jnp.einsum(
        "hqk,khd->qhd", grad_scores, heads_of(keys), preferred_element_type=f32
    ) * HEAD ** (-0.5)
    grad_keys = jnp.einsum(
        "hqk,qhd->khd", grad_scores, heads_of(query), preferred_element_type=f32
    ) * HEAD ** (-0.5)
    return (
        grad_query.reshape(query.shape).astype(bf16),
        grad_keys.reshape(keys.shape).astype(bf16),
        grad_values.reshape(values.shape).astype(bf16),
    )


def mlp_forward(stream, norm_gain, norm_shift, w_up, b_up, w_down, b_down):
    normed = layer_norm(stream, norm_gain, norm_shift).astype(bf16)
    raised = times(normed, w_up) + b_up
    active = jax.nn.gelu(raised, approximate=False).astype(bf16)
    return (stream + times(active, w_down) + b_down, normed, raised, active)


def mlp_backward(grad_stream, stream, norm_gain, norm_shift, normed, raised, active, w_up, w_down):
    grad_branch = grad_stream.astype(bf16)
    grad_wdown = over_rows(active, grad_branch)
    grad_bdown = column_sum(grad_branch)
    grad_active = times_back(grad_branch, w_down)
    unused, gelu_pull = jax.vjp(partial(jax.nn.gelu, approximate=False), raised)
    grad_raised = gelu_pull(grad_active)[0].astype(bf16)
    grad_wup = over_rows(normed, grad_raised)
    grad_bup = column_sum(grad_raised)
    grad_normed = times_back(grad_raised, w_up)
    grad_in, grad_gain, grad_shift = norm_back(grad_normed, stream, norm_gain, norm_shift)
    return (
        grad_stream + grad_in,
        grad_wup,
        grad_bup,
        grad_wdown,
        grad_bdown,
        grad_gain,
        grad_shift,
    )


def merge_stats(first_stats, second_stats):
    biggest = jnp.maximum(first_stats[0], second_stats[0])
    summed = first_stats[1] * jnp.exp(first_stats[0] - biggest) + second_stats[1] * jnp.exp(
        second_stats[0] - biggest
    )
    return jnp.stack([biggest, summed, first_stats[2] + second_stats[2]])


def adamw(weight_now, moment, second, gradient, factor, bias_one, bias_two):
    scaled = gradient * factor
    new_moment = beta_one * moment + (1.0 - beta_one) * scaled
    new_second = beta_two * second + (1.0 - beta_two) * scaled * scaled
    step_size = (
        new_moment / bias_one / (jnp.sqrt(new_second / bias_two) + adam_eps) + decay * weight_now
    )
    return (weight_now - rate * step_size, new_moment, new_second)


def round_up(amount, unit):
    return -(-amount // unit) * unit


def on_device(
    frames,
    input_ids,
    target_ids,
    lengths,
    present,
    step_count,
    enc_params,
    enc_moment,
    enc_second,
    dec_params,
    dec_moment,
    dec_second,
    table_params,
    table_moment,
    table_second,
):
    seq_size = lax.axis_size("seq")
    grp_size = lax.axis_size("grp")
    seq_rank = lax.axis_index("seq")
    group_rank = lax.axis_index("grp")
    lead = (seq_rank == 0).astype(f32)

    frame_rows = frames.shape[1]
    rows = round_up(frame_rows, 128)
    frames_here = jnp.pad(frames[0], ((0, rows - frame_rows), (0, 0)))
    frame_slots = gather_near(frames_here, "seq")
    enc_full = gather_flat(enc_params.astype(bf16))
    dec_full = gather_flat(dec_params.astype(bf16))
    vocab = table_params.shape[1]
    width = round_up(round_up(vocab, grp_size) // grp_size, 128)
    table_wide = jnp.pad(table_params.astype(bf16), ((0, 0), (0, width * grp_size - vocab)))
    table_sent = [
        lax.dynamic_slice_in_dim(table_wide, (group_rank ^ k) * width, width, 1)
        for k in range(grp_size)
    ]
    table = jnp.concatenate(reorder(trade_near(table_sent, "grp"), group_rank))
    vocab_first = seq_rank * vocab + group_rank * width
    vocab_here = jnp.clip(vocab - group_rank * width, 0, width)
    ids_slots = jnp.stack(gather_near(jnp.stack([input_ids[0], target_ids[0]]), "grp"))

    enc_qkv, enc_wout, enc_wup, enc_wdown, positions, gains, shifts, biases, up_bias = split_flat(
        enc_full, enc_layout()
    )
    dec_qkv, dec_wout, cross_wq, cross_wkv, cross_wout, dec_wup, dec_wdown = split_flat(
        dec_full, dec_layout()
    )
    gains = gains.astype(f32)
    shifts = shifts.astype(f32)
    biases = biases.astype(f32)
    up_bias = up_bias.astype(f32)
    positions = positions.astype(f32)
    span = D // seq_size

    def own(matrix, parts):
        return jnp.concatenate(
            [
                lax.dynamic_slice_in_dim(matrix, part * D + seq_rank * span, span, matrix.ndim - 1)
                for part in range(parts)
            ],
            axis=-1,
        )

    def own_bias(row):
        return lax.dynamic_slice_in_dim(biases[row], seq_rank * span, span, 0)

    half_width = D // 2
    stride = math.log(10000.0) / (half_width - 1)
    inverse = jnp.exp(-stride * jnp.arange(half_width, dtype=f32))
    x_slots = []
    for k in range(seq_size):
        offset = ((seq_rank ^ k) * frame_rows).astype(f32)
        angles = (jnp.arange(rows, dtype=f32) + offset)[:, None] * inverse[None, :]
        wave = jnp.concatenate([jnp.sin(angles), jnp.cos(angles)], axis=1)
        x_slots.append(frame_slots[k].astype(f32) + wave)
    x_all = jnp.concatenate(x_slots)
    x_enc0 = x_slots[0]
    h_enc1 = layer_norm(x_all, gains[0], shifts[0]).astype(bf16)
    own_enc_qkv = own(enc_qkv, 3)
    packed = times(h_enc1, own_enc_qkv)
    q_enc = (packed[:, :span] + own_bias(0)).astype(bf16)
    k_enc = packed[:, span : 2 * span].astype(bf16)
    v_enc = (packed[:, 2 * span :] + own_bias(1)).astype(bf16)
    frame_allowed = (jnp.arange(rows * seq_size) % rows < frame_rows)[None, None, :]
    o_own, lse_enc = attend_forward(q_enc, k_enc, v_enc, frame_allowed)

    def to_rows(value):
        pieces = [value[k * rows : (k + 1) * rows] for k in range(seq_size)]
        return jnp.concatenate(reorder(trade_near(pieces, "seq"), seq_rank), axis=1)

    def to_heads(value):
        pieces = reorder([value[:, k * span : (k + 1) * span] for k in range(seq_size)], seq_rank)
        return jnp.concatenate(trade_near(pieces, "seq"), axis=0)

    o_enc = to_rows(o_own)
    x_enc1 = x_enc0 + times(o_enc, enc_wout) + biases[2]
    x_enc2, h_enc2, up_enc, act_enc = mlp_forward(
        x_enc1, gains[1], shifts[1], enc_wup, up_bias[0], enc_wdown, biases[3]
    )
    enc_out = layer_norm(x_enc2, gains[2], shifts[2]).astype(bf16)
    paired = times(enc_out, cross_wkv)
    k_rows = paired[:, :D].astype(bf16)
    v_rows = (paired[:, D:] + biases[8]).astype(bf16)
    k_cross = to_heads(k_rows)
    v_cross = to_heads(v_rows)

    ids = ids_slots[:, 0].reshape(-1)
    targets = ids_slots[:, 1].reshape(-1)
    columns = jnp.arange(width)[None, :]
    inside = columns < vocab_here
    id_hot = ((ids[:, None] - vocab_first == columns) & inside).astype(bf16)
    looked = times_back(id_hot, table).astype(bf16).reshape(grp_size, LEN, D)
    part_rows = LEN // seq_size

    def share_rows(value, wire):
        pieces = [value[k * part_rows : (k + 1) * part_rows] for k in range(seq_size)]
        mine = scatter_near(reorder(pieces, seq_rank), "seq", wire)
        return jnp.concatenate(reorder(gather_near(mine.astype(wire), "seq"), seq_rank))

    token_emb = share_rows(reduce_group(looked, bf16, bf16), bf16).astype(f32)

    def all_heads(value):
        return reorder(gather_near(value, "seq"), seq_rank)

    x_dec0 = token_emb + positions
    h_dec1 = layer_norm(x_dec0, gains[3], shifts[3]).astype(bf16)
    packed = times(h_dec1, own(dec_qkv, 3))
    q_dec = (packed[:, :span] + own_bias(4)).astype(bf16)
    k_dec = packed[:, span : 2 * span].astype(bf16)
    v_dec = (packed[:, 2 * span :] + own_bias(5)).astype(bf16)
    causal = (jnp.arange(LEN)[:, None] >= jnp.arange(LEN)[None, :])[None]
    o_own_dec, lse_dec = attend_forward(q_dec, k_dec, v_dec, causal)
    o_dec = jnp.concatenate(all_heads(o_own_dec), axis=1)
    x_dec1 = x_dec0 + times(o_dec, dec_wout) + biases[6]
    h_dec2 = layer_norm(x_dec1, gains[4], shifts[4]).astype(bf16)
    q_cross = (times(h_dec2, own(cross_wq, 1)) + own_bias(7)).astype(bf16)
    o_own_cross, lse_cross = attend_forward(q_cross, k_cross, v_cross, frame_allowed)
    o_cross = jnp.concatenate(all_heads(o_own_cross), axis=1)
    x_dec2 = x_dec1 + times(o_cross, cross_wout) + biases[9]
    x_dec3, h_dec3, up_dec, act_dec = mlp_forward(
        x_dec2, gains[5], shifts[5], dec_wup, up_bias[1], dec_wdown, biases[10]
    )
    states = layer_norm(x_dec3, gains[6], shifts[6]).astype(bf16)

    all_states = gather_group(states).reshape(-1, D)
    logits = jnp.where(inside, times(all_states, table), masked_score)
    target_hot = (targets[:, None] - vocab_first == columns) & inside
    top_local = jnp.max(logits, axis=-1)
    total_local = jnp.sum(jnp.exp(logits - top_local[:, None]), axis=-1)
    picked_local = jnp.sum(jnp.where(target_hot, logits, 0.0), axis=-1)
    stats = jnp.stack([top_local, total_local, picked_local])
    by_slot = stats.reshape(3, grp_size, LEN)
    came = [
        swap(jnp.stack([by_slot[:, k ^ j] for k in range(grp_size)], axis=1), "grp", j)
        for j in range(1, grp_size)
    ]
    stats = tree_join([stats] + [piece.reshape(stats.shape) for piece in came], merge_stats)
    stats = all_join(stats, "seq", merge_stats)
    log_total = stats[0] + jnp.log(stats[1])
    clips = group_rank ^ jnp.arange(grp_size)
    valid = (
        (jnp.arange(LEN)[None, :] < lengths[clips][:, None]) & (present[clips][:, None] > 0)
    ).astype(f32)
    token_total = jnp.sum((lengths * present).astype(f32))
    loss_part = jnp.sum((log_total - stats[2])[:LEN] * valid[0]) * lead
    row_weight = (valid / token_total).reshape(-1)
    soft = jnp.where(inside, jnp.exp(logits - log_total[:, None]), 0.0)
    grad_logits = ((soft - target_hot.astype(f32)) * row_weight[:, None]).astype(bf16)
    grad_states_all = times_back(grad_logits, table).reshape(grp_size, LEN, D)
    grad_states = share_rows(reduce_group(grad_states_all, bf16), bf16).astype(f32)

    grad_x3, grad_g6, grad_s6 = norm_back(grad_states, x_dec3, gains[6], shifts[6])
    grad_x2, grad_dec_up, grad_dec_bup, grad_dec_down, grad_b10, grad_g5, grad_s5 = mlp_backward(
        grad_x3, x_dec2, gains[5], shifts[5], h_dec3, up_dec, act_dec, dec_wup, dec_wdown
    )
    grad_branch = grad_x2.astype(bf16)
    grad_cross_wout = over_rows(o_cross, grad_branch)
    grad_b9 = column_sum(grad_branch)
    own_cross_wout = lax.dynamic_slice_in_dim(cross_wout, seq_rank * span, span, 0)
    grad_mixed = times_back(grad_branch, own_cross_wout).astype(bf16)
    grad_qc_own, grad_kc_own, grad_vc_own = attend_backward(
        grad_mixed, q_cross, k_cross, v_cross, lse_cross, frame_allowed
    )
    grad_qc = jnp.concatenate(all_heads(grad_qc_own), axis=1)
    grad_kc = to_rows(grad_kc_own)
    grad_vc = to_rows(grad_vc_own)
    grad_cross_wq = over_rows(h_dec2, grad_qc)
    grad_b7 = column_sum(grad_qc)
    grad_in, grad_g4, grad_s4 = norm_back(
        times_back(grad_qc, cross_wq), x_dec1, gains[4], shifts[4]
    )
    grad_x1 = grad_x2 + grad_in
    grad_branch = grad_x1.astype(bf16)
    grad_dec_wout = over_rows(o_dec, grad_branch)
    grad_b6 = column_sum(grad_branch)
    own_dec_wout = lax.dynamic_slice_in_dim(dec_wout, seq_rank * span, span, 0)
    grad_mixed = times_back(grad_branch, own_dec_wout).astype(bf16)
    grad_qkv_own = jnp.concatenate(
        attend_backward(grad_mixed, q_dec, k_dec, v_dec, lse_dec, causal), axis=1
    )
    grad_qkv_all = all_heads(grad_qkv_own)
    grad_packed = jnp.concatenate(
        [
            piece[:, part * span : (part + 1) * span]
            for part in range(3)
            for piece in grad_qkv_all
        ],
        axis=1,
    )
    grad_dec_qkv = over_rows(h_dec1, grad_packed)
    sums = column_sum(grad_packed)
    grad_b4 = sums[:D]
    grad_b5 = sums[2 * D :]
    grad_in, grad_g3, grad_s3 = norm_back(
        times_back(grad_packed, dec_qkv), x_dec0, gains[3], shifts[3]
    )
    grad_x0 = grad_x1 + grad_in

    grad_embed_all = gather_group(grad_x0.astype(bf16)).reshape(-1, D)
    grad_table = over_rows(all_states, grad_logits) + over_rows(grad_embed_all, id_hot)
    chans = D // grp_size
    table_back = [
        lax.dynamic_slice_in_dim(grad_table, (group_rank ^ k) * chans, chans, 0)
        for k in range(grp_size)
    ]
    table_grad = jnp.concatenate(reorder(trade_near(table_back, "grp"), group_rank), axis=1)
    table_grad = table_grad[:, :vocab]

    grad_pair = jnp.concatenate([grad_kc, grad_vc], axis=1)
    grad_cross_wkv = over_rows(enc_out, grad_pair)
    grad_b8 = column_sum(grad_vc)
    grad_enc2, grad_g2, grad_s2 = norm_back(
        times_back(grad_pair, cross_wkv), x_enc2, gains[2], shifts[2]
    )

    block = dec_params.shape[0]
    wkv_at = (3 * D + D + D) * D
    dec_flat = jnp.concatenate(
        [
            grad_dec_qkv.reshape(-1),
            grad_dec_wout.reshape(-1),
            grad_cross_wq.reshape(-1),
            jnp.zeros((2 * D * D,), f32),
            grad_cross_wout.reshape(-1),
            grad_dec_up.reshape(-1),
            grad_dec_down.reshape(-1),
        ]
    ).reshape(grp_size, seq_size, block)
    dec_mine = lax.dynamic_index_in_dim(dec_flat, seq_rank, 1, False)
    first_block = wkv_at // block
    turn = first_block % seq_size
    wkv_blocks = grad_cross_wkv.reshape(-1, seq_size, block)
    wkv_sent = [
        lax.dynamic_index_in_dim(wkv_blocks, (seq_rank ^ k) ^ turn, 1, False)
        for k in range(seq_size)
    ]
    wkv_mine = scatter_near(wkv_sent, "seq", f32)
    dec_mine = lax.dynamic_update_slice_in_dim(
        dec_mine,
        wkv_mine
        + lax.dynamic_slice_in_dim(
            dec_mine, (first_block + (seq_rank ^ turn)) // seq_size, wkv_mine.shape[0], 0
        ),
        (first_block + (seq_rank ^ turn)) // seq_size,
        0,
    )
    dec_grad = reduce_blocks(dec_mine)

    grad_enc1, grad_enc_up, grad_enc_bup, grad_enc_down, grad_b3, grad_g1, grad_s1 = mlp_backward(
        grad_enc2, x_enc1, gains[1], shifts[1], h_enc2, up_enc, act_enc, enc_wup, enc_wdown
    )
    grad_branch = grad_enc1.astype(bf16)
    grad_enc_wout = over_rows(o_enc, grad_branch)
    grad_b2 = column_sum(grad_branch)
    grad_mixed = to_heads(times_back(grad_branch, enc_wout).astype(bf16))
    grad_q, grad_k, grad_v = attend_backward(
        grad_mixed, q_enc, k_enc, v_enc, lse_enc, frame_allowed
    )
    grad_packed = jnp.concatenate([grad_q, grad_k, grad_v], axis=1)
    own_grad = over_rows(h_enc1, grad_packed)
    grad_enc_qkv = jnp.zeros((D, 3 * D), f32)
    for part in range(3):
        grad_enc_qkv = lax.dynamic_update_slice(
            grad_enc_qkv,
            own_grad[:, part * span : (part + 1) * span],
            (0, part * D + seq_rank * span),
        )
    sums = column_sum(grad_packed)

    def placed(values):
        return lax.dynamic_update_slice(jnp.zeros((D,), f32), values, (seq_rank * span,))

    grad_b0 = placed(sums[:span])
    grad_b1 = placed(sums[2 * span :])
    unused, grad_g0, grad_s0 = norm_back(
        times_back(grad_packed, own_enc_qkv), x_all, gains[0], shifts[0]
    )
    once = lead
    grad_gains = jnp.stack(
        [grad_g0, grad_g1, grad_g2, grad_g3 * once, grad_g4 * once, grad_g5 * once, grad_g6 * once]
    )
    grad_shifts = jnp.stack(
        [grad_s0, grad_s1, grad_s2, grad_s3 * once, grad_s4 * once, grad_s5 * once, grad_s6 * once]
    )
    grad_biases = jnp.stack(
        [
            grad_b0,
            grad_b1,
            grad_b2,
            grad_b3,
            grad_b4 * once,
            grad_b5 * once,
            grad_b6 * once,
            grad_b7 * once,
            grad_b8,
            grad_b9 * once,
            grad_b10 * once,
        ]
    )
    grad_up_bias = jnp.stack([grad_enc_bup, grad_dec_bup * once])
    enc_block = enc_params.shape[0]
    enc_flat = jnp.concatenate(
        [
            grad_enc_qkv.reshape(-1),
            grad_enc_wout.reshape(-1),
            grad_enc_up.reshape(-1),
            grad_enc_down.reshape(-1),
            (grad_x0 * once).reshape(-1),
            grad_gains.reshape(-1),
            grad_shifts.reshape(-1),
            grad_biases.reshape(-1),
            grad_up_bias.reshape(-1),
        ]
    ).reshape(grp_size, seq_size, enc_block)
    enc_sums = reduce_blocks(enc_flat)
    enc_grad = scatter_near(
        [
            lax.dynamic_index_in_dim(enc_sums, seq_rank ^ k, 0, False)
            for k in range(seq_size)
        ],
        "seq",
        f32,
    )

    squares = (
        jnp.sum(enc_grad * enc_grad)
        + jnp.sum(dec_grad * dec_grad)
        + jnp.sum(table_grad * table_grad)
    )
    totals = jnp.stack([loss_part, squares])
    totals = all_join(all_join(totals, "grp", jnp.add), "seq", jnp.add)
    mean_loss = totals[0] / token_total
    grad_norm = jnp.sqrt(totals[1])
    factor = jnp.minimum(1.0, clip_limit / (grad_norm + 1e-06))
    steps_done = step_count[0].astype(f32)
    bias_one = 1.0 - beta_one**steps_done
    bias_two = 1.0 - beta_two**steps_done
    enc_new = adamw(enc_params, enc_moment, enc_second, enc_grad, factor, bias_one, bias_two)
    dec_new = adamw(dec_params, dec_moment, dec_second, dec_grad, factor, bias_one, bias_two)
    table_new = adamw(
        table_params, table_moment, table_second, table_grad, factor, bias_one, bias_two
    )
    return (mean_loss, grad_norm, *enc_new, *dec_new, *table_new)


def wide_joined_2(value, axis, join):
    pieces = jax.tree.map(lambda part: lax.all_gather(part, axis), value)
    head = jax.tree.map(lambda part: part[0], pieces)
    tail = jax.tree.map(lambda part: part[1:], pieces)
    total, _ = lax.scan(lambda total, piece: (join(total, piece), None), head, tail)
    return total


def wide_sinusoid(amount, channels, offset):
    half_width = channels // 2
    stride = math.log(10000.0) / (half_width - 1)
    inverse = jnp.exp(-stride * jnp.arange(half_width, dtype=jnp.float32))
    angles = (jnp.arange(amount, dtype=jnp.float32) + offset)[:, None] * inverse[None, :]
    return jnp.concatenate([jnp.sin(angles), jnp.cos(angles)], axis=1)


def wide_times_rows(left_side, right_side):
    return lax.dot_general(
        left_side,
        right_side,
        (((left_side.ndim - 1,), (0,)), ((), ())),
        preferred_element_type=jnp.float32,
    )


def wide_times_back(left_side, right_side):
    return lax.dot_general(
        left_side,
        right_side,
        (((left_side.ndim - 1,), (1,)), ((), ())),
        preferred_element_type=jnp.float32,
    )


def wide_over_rows(left_side, right_side):
    return lax.dot_general(
        left_side, right_side, (((0, 1), (0, 1)), ((), ())), preferred_element_type=jnp.float32
    )


def wide_column_sum(values):
    return jnp.sum(values.astype(jnp.float32), axis=(0, 1))


def wide_split_heads(values):
    return values.reshape(values.shape[0], values.shape[1], HEADS, values.shape[2] // HEADS)


def wide_score_block(query, keys, first_row):
    head_size = query.shape[2] // HEADS
    scores = jnp.einsum(
        "cqhd,ckhd->chqk", wide_split_heads(query), wide_split_heads(keys), preferred_element_type=jnp.float32
    ) * head_size ** (-0.5)
    if first_row is not None:
        allowed = (first_row + jnp.arange(query.shape[1]))[:, None] >= jnp.arange(keys.shape[1])[
            None, :
        ]
        scores = jnp.where(allowed[None, None], scores, masked_score)
    return scores


def wide_attend_forward(query, keys, values, first_row):
    scores = wide_score_block(query, keys, first_row)
    highest_score = jnp.max(scores, axis=-1, keepdims=True)
    log_total = highest_score + jnp.log(
        jnp.sum(jnp.exp(scores - highest_score), axis=-1, keepdims=True)
    )
    weights = jnp.exp(scores - log_total).astype(jnp.bfloat16)
    mixed = jnp.einsum(
        "chqk,ckhd->cqhd", weights, wide_split_heads(values), preferred_element_type=jnp.float32
    )
    return (mixed.reshape(query.shape).astype(jnp.bfloat16), log_total)


def wide_attend_backward(grad_mixed, query, keys, values, log_total, first_row):
    head_size = query.shape[2] // HEADS
    scores = wide_score_block(query, keys, first_row)
    weights = jnp.exp(scores - log_total)
    grad_heads = wide_split_heads(grad_mixed)
    grad_weights = jnp.einsum(
        "cqhd,ckhd->chqk", grad_heads, wide_split_heads(values), preferred_element_type=jnp.float32
    )
    grad_values = jnp.einsum(
        "chqk,cqhd->ckhd",
        weights.astype(jnp.bfloat16),
        grad_heads,
        preferred_element_type=jnp.float32,
    )
    inner = jnp.sum(weights * grad_weights, axis=-1, keepdims=True)
    grad_scores = (weights * (grad_weights - inner)).astype(jnp.bfloat16)
    grad_query = jnp.einsum(
        "chqk,ckhd->cqhd", grad_scores, wide_split_heads(keys), preferred_element_type=jnp.float32
    ) * head_size ** (-0.5)
    grad_keys = jnp.einsum(
        "chqk,cqhd->ckhd", grad_scores, wide_split_heads(query), preferred_element_type=jnp.float32
    ) * head_size ** (-0.5)
    return (
        grad_query.reshape(query.shape),
        grad_keys.reshape(keys.shape),
        grad_values.reshape(values.shape),
    )


def wide_mlp_forward(stream, norm_gain, norm_shift, w_up, b_up, w_down, b_down):
    normed = layer_norm(stream, norm_gain, norm_shift).astype(jnp.bfloat16)
    raised = wide_times_rows(normed, w_up) + b_up
    active = jax.nn.gelu(raised, approximate=False).astype(jnp.bfloat16)
    return (stream + wide_times_rows(active, w_down) + b_down, normed, raised, active)


def wide_mlp_backward(grad_stream, stream, norm_gain, norm_shift, normed, raised, active, w_up, w_down):
    grad_branch = grad_stream.astype(jnp.bfloat16)
    grad_wdown = wide_over_rows(active, grad_branch)
    grad_bdown = wide_column_sum(grad_branch)
    grad_active = wide_times_back(grad_branch, w_down)
    unused, gelu_pull = jax.vjp(partial(jax.nn.gelu, approximate=False), raised)
    grad_raised = gelu_pull(grad_active)[0].astype(jnp.bfloat16)
    grad_wup = wide_over_rows(normed, grad_raised)
    grad_bup = wide_column_sum(grad_raised)
    grad_normed = wide_times_back(grad_raised, w_up)
    grad_in, grad_gain, grad_shift = norm_back(grad_normed, stream, norm_gain, norm_shift)
    return (
        grad_stream + grad_in,
        grad_wup,
        grad_bup,
        grad_wdown,
        grad_bdown,
        grad_gain,
        grad_shift,
    )


def wide_merge_stats(first_stats, second_stats):
    biggest = jnp.maximum(first_stats[0], second_stats[0])
    summed = first_stats[1] * jnp.exp(first_stats[0] - biggest) + second_stats[1] * jnp.exp(
        second_stats[0] - biggest
    )
    return (biggest, summed, first_stats[2] + second_stats[2])


def wide_spread_grads(grad_matrix):
    return lax.psum_scatter(grad_matrix, ("grp", "seq"), scatter_dimension=0, tiled=True)


def wide_on_device(
    frames,
    input_ids,
    target_ids,
    lengths,
    present,
    step_count,
    enc_params,
    enc_moment,
    enc_second,
    dec_params,
    dec_moment,
    dec_second,
    table_params,
    table_moment,
    table_second,
):
    enc_full, dec_full = (
        lax.all_gather(enc_params.astype(jnp.bfloat16), ("grp", "seq"), axis=0, tiled=True),
        lax.all_gather(dec_params.astype(jnp.bfloat16), ("grp", "seq"), axis=0, tiled=True),
    )
    table_local = lax.all_gather(table_params.astype(jnp.bfloat16), "grp", axis=0, tiled=True)
    enc_qkv, enc_wout, enc_wup, enc_wdown, positions, gains, shifts, biases, up_bias = split_flat(
        enc_full, enc_layout()
    )
    dec_qkv, dec_wout, cross_wq, cross_wkv, cross_wout, dec_wup, dec_wdown = split_flat(
        dec_full, dec_layout()
    )
    gains = gains.astype(jnp.float32)
    shifts = shifts.astype(jnp.float32)
    biases = biases.astype(jnp.float32)
    up_bias = up_bias.astype(jnp.float32)
    positions = positions.astype(jnp.float32)
    seq_size = lax.axis_size("seq")
    seq_rank = lax.axis_index("seq")
    group_rank = lax.axis_index("grp")
    clip_count = frames.shape[0]
    enc_rows = frames.shape[1]
    dec_rows = LEN // seq_size
    vocab_rows = table_local.shape[1]
    dec_first = seq_rank * dec_rows
    vocab_first = seq_rank * vocab_rows
    x_enc0 = (
        frames.astype(jnp.float32)
        + wide_sinusoid(enc_rows, D, (seq_rank * enc_rows).astype(jnp.float32))[None]
    )
    h_enc1 = layer_norm(x_enc0, gains[0], shifts[0]).astype(jnp.bfloat16)
    packed = wide_times_rows(h_enc1, enc_qkv)
    q_enc = (packed[..., :D] + biases[0]).astype(jnp.bfloat16)
    k_enc = packed[..., D : 2 * D].astype(jnp.bfloat16)
    v_enc = (packed[..., 2 * D :] + biases[1]).astype(jnp.bfloat16)
    keys_enc, vals_enc = (
        lax.all_gather(k_enc, "seq", axis=1, tiled=True),
        lax.all_gather(v_enc, "seq", axis=1, tiled=True),
    )
    o_enc, lse_enc = wide_attend_forward(q_enc, keys_enc, vals_enc, None)
    x_enc1 = x_enc0 + wide_times_rows(o_enc, enc_wout) + biases[2]
    x_enc2, h_enc2, up_enc, act_enc = wide_mlp_forward(
        x_enc1, gains[1], shifts[1], enc_wup, up_bias[0], enc_wdown, biases[3]
    )
    enc_out = layer_norm(x_enc2, gains[2], shifts[2]).astype(jnp.bfloat16)
    local_ids = input_ids - vocab_first
    inside = (local_ids >= 0) & (local_ids < vocab_rows)
    safe_ids = jnp.clip(local_ids, 0, vocab_rows - 1).reshape(-1)
    looked = jnp.take(table_local, safe_ids, axis=1).astype(jnp.float32).T
    looked = jnp.where(inside.reshape(-1)[:, None], looked, 0.0).reshape(clip_count, LEN, D)
    token_emb = lax.psum_scatter(
        looked.astype(jnp.bfloat16), "seq", scatter_dimension=1, tiled=True
    ).astype(jnp.float32)
    x_dec0 = token_emb + lax.dynamic_slice_in_dim(positions, dec_first, dec_rows, 0)[None]
    h_dec1 = layer_norm(x_dec0, gains[3], shifts[3]).astype(jnp.bfloat16)
    packed = wide_times_rows(h_dec1, dec_qkv)
    q_dec = (packed[..., :D] + biases[4]).astype(jnp.bfloat16)
    k_dec = packed[..., D : 2 * D].astype(jnp.bfloat16)
    v_dec = (packed[..., 2 * D :] + biases[5]).astype(jnp.bfloat16)
    paired = wide_times_rows(enc_out, cross_wkv)
    k_cross = paired[..., :D].astype(jnp.bfloat16)
    v_cross = (paired[..., D:] + biases[8]).astype(jnp.bfloat16)
    keys_dec, vals_dec, keys_cross, vals_cross = (
        lax.all_gather(k_dec, "seq", axis=1, tiled=True),
        lax.all_gather(v_dec, "seq", axis=1, tiled=True),
        lax.all_gather(k_cross, "seq", axis=1, tiled=True),
        lax.all_gather(v_cross, "seq", axis=1, tiled=True),
    )
    o_dec, lse_dec = wide_attend_forward(q_dec, keys_dec, vals_dec, dec_first)
    x_dec1 = x_dec0 + wide_times_rows(o_dec, dec_wout) + biases[6]
    h_dec2 = layer_norm(x_dec1, gains[4], shifts[4]).astype(jnp.bfloat16)
    q_cross = (wide_times_rows(h_dec2, cross_wq) + biases[7]).astype(jnp.bfloat16)
    o_cross, lse_cross = wide_attend_forward(q_cross, keys_cross, vals_cross, None)
    x_dec2 = x_dec1 + wide_times_rows(o_cross, cross_wout) + biases[9]
    x_dec3, h_dec3, up_dec, act_dec = wide_mlp_forward(
        x_dec2, gains[5], shifts[5], dec_wup, up_bias[1], dec_wdown, biases[10]
    )
    states = layer_norm(x_dec3, gains[6], shifts[6]).astype(jnp.bfloat16)
    all_states = lax.all_gather(states, "seq", axis=1, tiled=True)
    logits = wide_times_rows(all_states, table_local)
    target_local = target_ids - vocab_first
    has_target = (target_local >= 0) & (target_local < vocab_rows)
    top_local = jnp.max(logits, axis=-1)
    total_local = jnp.sum(jnp.exp(logits - top_local[..., None]), axis=-1)
    picked_local = jnp.take_along_axis(
        logits, jnp.clip(target_local, 0, vocab_rows - 1)[..., None], axis=-1
    )[..., 0]
    picked_local = jnp.where(has_target, picked_local, 0.0)
    top_all, total_all, picked_all = wide_joined_2(
        (top_local, total_local, picked_local), "seq", wide_merge_stats
    )
    log_total = top_all + jnp.log(total_all)
    my_lengths = lax.dynamic_slice_in_dim(lengths, group_rank * clip_count, clip_count)
    my_present = lax.dynamic_slice_in_dim(present, group_rank * clip_count, clip_count)
    valid = ((jnp.arange(LEN)[None, :] < my_lengths[:, None]) & (my_present[:, None] > 0)).astype(
        jnp.float32
    )
    token_total = jnp.sum((lengths * present).astype(jnp.float32))
    token_loss = (log_total - picked_all) * valid
    loss_part = jnp.sum(lax.dynamic_slice_in_dim(token_loss, dec_first, dec_rows, 1))
    row_weight = valid / token_total
    onehot = (jnp.arange(vocab_rows)[None, None, :] == target_local[..., None]).astype(jnp.float32)
    grad_logits = (
        (jnp.exp(logits - log_total[..., None]) - onehot) * row_weight[..., None]
    ).astype(jnp.bfloat16)
    grad_states_all = wide_times_back(grad_logits, table_local)
    grad_table = wide_over_rows(all_states, grad_logits)
    grad_states = lax.psum_scatter(
        grad_states_all.astype(jnp.bfloat16), "seq", scatter_dimension=1, tiled=True
    ).astype(jnp.float32)
    grad_x3, grad_g6, grad_s6 = norm_back(grad_states, x_dec3, gains[6], shifts[6])
    grad_x2, grad_dec_up, grad_dec_bup, grad_dec_down, grad_b10, grad_g5, grad_s5 = wide_mlp_backward(
        grad_x3, x_dec2, gains[5], shifts[5], h_dec3, up_dec, act_dec, dec_wup, dec_wdown
    )
    grad_branch = grad_x2.astype(jnp.bfloat16)
    grad_cross_wout = wide_over_rows(o_cross, grad_branch)
    grad_b9 = wide_column_sum(grad_branch)
    grad_mixed = wide_times_back(grad_branch, cross_wout).astype(jnp.bfloat16)
    grad_qc, grad_kc, grad_vc = wide_attend_backward(
        grad_mixed, q_cross, keys_cross, vals_cross, lse_cross, None
    )
    grad_qc = grad_qc.astype(jnp.bfloat16)
    grad_cross_wq = wide_over_rows(h_dec2, grad_qc)
    grad_b7 = wide_column_sum(grad_qc)
    grad_in, grad_g4, grad_s4 = norm_back(
        wide_times_back(grad_qc, cross_wq), x_dec1, gains[4], shifts[4]
    )
    grad_x1 = grad_x2 + grad_in
    grad_branch = grad_x1.astype(jnp.bfloat16)
    grad_dec_wout = wide_over_rows(o_dec, grad_branch)
    grad_b6 = wide_column_sum(grad_branch)
    grad_mixed = wide_times_back(grad_branch, dec_wout).astype(jnp.bfloat16)
    grad_qd, grad_kd, grad_vd = wide_attend_backward(
        grad_mixed, q_dec, keys_dec, vals_dec, lse_dec, dec_first
    )
    grad_kd, grad_vd, grad_kc, grad_vc = (
        lax.psum_scatter(
            grad_kd.astype(jnp.bfloat16), "seq", scatter_dimension=1, tiled=True
        ).astype(jnp.float32),
        lax.psum_scatter(
            grad_vd.astype(jnp.bfloat16), "seq", scatter_dimension=1, tiled=True
        ).astype(jnp.float32),
        lax.psum_scatter(
            grad_kc.astype(jnp.bfloat16), "seq", scatter_dimension=1, tiled=True
        ).astype(jnp.float32),
        lax.psum_scatter(
            grad_vc.astype(jnp.bfloat16), "seq", scatter_dimension=1, tiled=True
        ).astype(jnp.float32),
    )
    grad_qd = grad_qd.astype(jnp.bfloat16)
    grad_vd = grad_vd.astype(jnp.bfloat16)
    grad_packed = jnp.concatenate([grad_qd, grad_kd.astype(jnp.bfloat16), grad_vd], axis=-1)
    grad_dec_qkv = wide_over_rows(h_dec1, grad_packed)
    grad_b4 = wide_column_sum(grad_qd)
    grad_b5 = wide_column_sum(grad_vd)
    grad_in, grad_g3, grad_s3 = norm_back(
        wide_times_back(grad_packed, dec_qkv), x_dec0, gains[3], shifts[3]
    )
    grad_x0 = grad_x1 + grad_in
    grad_positions = lax.dynamic_update_slice_in_dim(
        jnp.zeros((LEN, D), jnp.float32), jnp.sum(grad_x0, axis=0), dec_first, 0
    )
    grad_embed_all = lax.all_gather(grad_x0.astype(jnp.bfloat16), "seq", axis=1, tiled=True).astype(
        grad_x0.dtype
    )
    grad_embed_all = jnp.where(inside.reshape(-1)[:, None], grad_embed_all.reshape(-1, D), 0.0)
    grad_table = grad_table.at[:, safe_ids].add(grad_embed_all.T)
    grad_vc = grad_vc.astype(jnp.bfloat16)
    grad_pair = jnp.concatenate([grad_kc.astype(jnp.bfloat16), grad_vc], axis=-1)
    grad_cross_wkv = wide_over_rows(enc_out, grad_pair)
    grad_b8 = wide_column_sum(grad_vc)
    grad_enc2, grad_g2, grad_s2 = norm_back(
        wide_times_back(grad_pair, cross_wkv), x_enc2, gains[2], shifts[2]
    )
    device_count = lax.axis_size(("grp", "seq"))
    dec_flat = jnp.concatenate(
        [
            grad_dec_qkv.reshape(-1),
            grad_dec_wout.reshape(-1),
            grad_cross_wq.reshape(-1),
            grad_cross_wkv.reshape(-1),
            grad_cross_wout.reshape(-1),
            grad_dec_up.reshape(-1),
            grad_dec_down.reshape(-1),
        ]
    )
    dec_matrix = dec_flat.reshape(device_count, -1)
    dec_columns = dec_matrix.shape[1]
    grad_enc1, grad_enc_up, grad_enc_bup, grad_enc_down, grad_b3, grad_g1, grad_s1 = wide_mlp_backward(
        grad_enc2, x_enc1, gains[1], shifts[1], h_enc2, up_enc, act_enc, enc_wup, enc_wdown
    )
    grad_branch = grad_enc1.astype(jnp.bfloat16)
    grad_enc_wout = wide_over_rows(o_enc, grad_branch)
    grad_b2 = wide_column_sum(grad_branch)
    grad_mixed = wide_times_back(grad_branch, enc_wout).astype(jnp.bfloat16)
    grad_qe, grad_ke, grad_ve = wide_attend_backward(
        grad_mixed, q_enc, keys_enc, vals_enc, lse_enc, None
    )
    grad_ke, grad_ve = (
        lax.psum_scatter(
            grad_ke.astype(jnp.bfloat16), "seq", scatter_dimension=1, tiled=True
        ).astype(jnp.float32),
        lax.psum_scatter(
            grad_ve.astype(jnp.bfloat16), "seq", scatter_dimension=1, tiled=True
        ).astype(jnp.float32),
    )
    grad_qe = grad_qe.astype(jnp.bfloat16)
    grad_ve = grad_ve.astype(jnp.bfloat16)
    grad_packed = jnp.concatenate([grad_qe, grad_ke.astype(jnp.bfloat16), grad_ve], axis=-1)
    grad_enc_qkv = wide_over_rows(h_enc1, grad_packed)
    grad_b0 = wide_column_sum(grad_qe)
    grad_b1 = wide_column_sum(grad_ve)
    unused, grad_g0, grad_s0 = norm_back(
        wide_times_back(grad_packed, enc_qkv), x_enc0, gains[0], shifts[0]
    )
    grad_gains = jnp.stack([grad_g0, grad_g1, grad_g2, grad_g3, grad_g4, grad_g5, grad_g6])
    grad_shifts = jnp.stack([grad_s0, grad_s1, grad_s2, grad_s3, grad_s4, grad_s5, grad_s6])
    grad_biases = jnp.stack(
        [
            grad_b0,
            grad_b1,
            grad_b2,
            grad_b3,
            grad_b4,
            grad_b5,
            grad_b6,
            grad_b7,
            grad_b8,
            grad_b9,
            grad_b10,
        ]
    )
    grad_up_bias = jnp.stack([grad_enc_bup, grad_dec_bup])
    enc_flat = jnp.concatenate(
        [
            grad_enc_qkv.reshape(-1),
            grad_enc_wout.reshape(-1),
            grad_enc_up.reshape(-1),
            grad_enc_down.reshape(-1),
            grad_positions.reshape(-1),
            grad_gains.reshape(-1),
            grad_shifts.reshape(-1),
            grad_biases.reshape(-1),
            grad_up_bias.reshape(-1),
        ]
    )
    enc_matrix = enc_flat.reshape(device_count, -1)
    joined = wide_spread_grads(jnp.concatenate([dec_matrix, enc_matrix], axis=1))
    dec_grad = joined[:, :dec_columns].reshape(-1)
    enc_grad = joined[:, dec_columns:].reshape(-1)
    table_grad = lax.psum_scatter(grad_table, "grp", scatter_dimension=0, tiled=True)
    squares = (
        jnp.sum(enc_grad * enc_grad)
        + jnp.sum(dec_grad * dec_grad)
        + jnp.sum(table_grad * table_grad)
    )
    loss_sum, square_sum = lax.psum((loss_part, squares), ("grp", "seq"))
    mean_loss = loss_sum / token_total
    grad_norm = jnp.sqrt(square_sum)
    factor = jnp.minimum(1.0, clip_limit / (grad_norm + 1e-06))
    steps_done = step_count[0].astype(jnp.float32)
    bias_one = 1.0 - beta_one**steps_done
    bias_two = 1.0 - beta_two**steps_done
    enc_new = adamw(enc_params, enc_moment, enc_second, enc_grad, factor, bias_one, bias_two)
    dec_new = adamw(dec_params, dec_moment, dec_second, dec_grad, factor, bias_one, bias_two)
    table_new = adamw(
        table_params, table_moment, table_second, table_grad, factor, bias_one, bias_two
    )
    return (
        mean_loss,
        grad_norm,
        enc_new[0],
        enc_new[1],
        enc_new[2],
        dec_new[0],
        dec_new[1],
        dec_new[2],
        table_new[0],
        table_new[1],
        table_new[2],
    )


def solution(mesh):
    flat = P(("grp", "seq"))
    both = P("grp", "seq")
    in_specs = (
        P("grp", "seq", None),
        P("grp", None),
        P("grp", None),
        P(),
        P(),
        P(),
        flat,
        flat,
        flat,
        flat,
        flat,
        flat,
        both,
        both,
        both,
    )
    out_specs = (P(), P(), flat, flat, flat, flat, flat, flat, both, both, both)
    return jax.shard_map(
        on_device if mesh.shape["grp"] <= 8 else wide_on_device,
        mesh=mesh,
        in_specs=in_specs,
        out_specs=out_specs,
        check_vma=False,
    )
```

```python
from functools import partial
import math

import jax
import jax.numpy as jnp
from jax import lax
from jax.experimental import pallas as pl
from jax.experimental.pallas import tpu as pltpu
from jax.sharding import PartitionSpec as P


D = 512
HEADS = 8
F = 2048
LEN = 448
HEAD = D // HEADS
LANES = 128


beta_one = 0.9
beta_two = 0.999
rate = 0.01
decay = 0.1
adam_eps = 1e-08
clip_limit = 1.0
norm_eps = 1e-05
masked_score = -1e30

bf16 = jnp.bfloat16
f32 = jnp.float32


def layer_norm(values, norm_gain, norm_shift):
    center = values - jnp.mean(values, axis=-1, keepdims=True)
    spread = jnp.mean(center * center, axis=-1, keepdims=True)
    return center * lax.rsqrt(spread + norm_eps) * norm_gain + norm_shift


def norm_back(grad_out, values, norm_gain, norm_shift):
    _, pullback = jax.vjp(layer_norm, values, norm_gain, norm_shift)
    return pullback(grad_out)


def enc_layout():
    return [(D, 3 * D), (D, D), (D, F), (F, D), (LEN, D), (7, D), (7, D), (11, D), (2, F)]


def dec_layout():
    return [(D, 3 * D), (D, D), (D, D), (D, 2 * D), (D, D), (D, F), (F, D)]


def split_flat(flat_vec, layout):
    pieces = []
    offset = 0
    for matrix_dims in layout:
        amount = matrix_dims[0] * matrix_dims[1]
        pieces.append(flat_vec[offset : offset + amount].reshape(matrix_dims))
        offset += amount
    return pieces


def times(left_side, right_side):
    return jnp.dot(left_side, right_side, preferred_element_type=f32)


def times_back(left_side, right_side):
    return lax.dot_general(
        left_side, right_side, (((1,), (1,)), ((), ())), preferred_element_type=f32
    )


def over_rows(left_side, right_side):
    return lax.dot_general(
        left_side, right_side, (((0,), (0,)), ((), ())), preferred_element_type=f32
    )


def column_sum(values):
    return jnp.sum(values.astype(f32), axis=0)


def swap(value, axis, mask):
    count = lax.axis_size(axis)
    return lax.ppermute(value, axis, [(i, i ^ mask) for i in range(count)])


def reorder(items, rank):
    items = list(items)
    bit = 1
    while bit < len(items):
        odd = (rank & bit) != 0
        items = [jnp.where(odd, items[k ^ bit], items[k]) for k in range(len(items))]
        bit *= 2
    return items


def tree_join(items, join):
    items = list(items)
    while len(items) > 1:
        items = [join(items[k], items[k + 1]) for k in range(0, len(items), 2)]
    return items[0]


def pair_join(value, axis, join):
    for bit in bits_of(axis):
        value = join(value, swap(value, axis, bit))
    return value


def all_join(value, axis, join):
    count = lax.axis_size(axis)
    return tree_join([value] + [swap(value, axis, k) for k in range(1, count)], join)


def gather_near(value, axis):
    return [value] + [swap(value, axis, k) for k in range(1, lax.axis_size(axis))]


def trade_near(items, axis):
    return [items[0]] + [swap(items[k], axis, k) for k in range(1, len(items))]


def bits_of(axis):
    count = lax.axis_size(axis)
    found = []
    bit = 1
    while bit < count:
        found.append(bit)
        bit *= 2
    return found


def group_orders():
    far = bits_of("grp")[1:]
    return far, far[::-1]


def grow(slots, bit):
    held = sorted(slots)
    sent = jnp.stack([slots[k] for k in held])
    came = swap(sent, "grp", bit)
    for place, k in enumerate(held):
        slots[k ^ bit] = came[place]
    return slots


def gather_group(value):
    half = value.shape[0] // 2
    parts = [value[:half], value[half:]]
    results = []
    for part, order in zip(parts, group_orders()):
        slots = {0: part}
        for bit in order + [1]:
            slots = grow(slots, bit)
        results.append(slots)
    count = lax.axis_size("grp")
    return jnp.stack([jnp.concatenate([r[k] for r in results]) for k in range(count)])


def reduce_group(slots, wire, hold=f32):
    count = lax.axis_size("grp")
    sent = jnp.stack([slots[k] for k in range(count) if k & 1]).astype(wire)
    came = swap(sent, "grp", 1)
    held = {k: slots[k].astype(hold) + came[k // 2].astype(hold) for k in range(0, count, 2)}
    half = slots[0].shape[0] // 2
    results = []
    for low, order in zip((0, half), group_orders()):
        part = {k: v[low : low + half] for k, v in held.items()}
        for bit in order:
            gone = [k for k in sorted(part) if k & bit]
            came = swap(jnp.stack([part[k] for k in gone]).astype(wire), "grp", bit)
            part = {
                k: v + came[gone.index(k ^ bit)].astype(hold)
                for k, v in part.items()
                if not k & bit
            }
        results.append(part[0])
    return jnp.concatenate(results)


def gather_near_lines(block):
    half = block.shape[0] // 2
    near = gather_near(block, "seq")
    return [jnp.stack([piece[low : low + half] for piece in near])[None] for low in (0, half)]


def gather_far_lines(parts, stage):
    return [
        jnp.concatenate([part, swap(part, "grp", order[stage])])
        for part, order in zip(parts, group_orders())
    ]


def lay_out_kernel(shapes, block, rank_ref, own_a, own_b, came_a, came_b, *refs):
    outs, (lines, wide, sems) = refs[: len(shapes)], refs[len(shapes) :]
    half = block // 2
    rank = rank_ref[0]

    def copies(index, start):
        slot = index ^ rank
        far_z = slot & 3
        mate = (slot >> 2) & 1
        far_x = (slot >> 3) & 1
        far_y = (slot >> 4) & 1
        for side, place, own_ref, came_ref in (
            (0, 2 * far_y + far_x, own_a, came_a),
            (1, 2 * far_x + far_y, own_b, came_b),
        ):
            target = lines.at[pl.ds(index * block + side * half, half), :]
            sem = sems.at[2 * index + side]
            if not start:
                pltpu.make_async_copy(own_ref.at[0, 0], target, sem).wait()
                continue

            @pl.when(mate == 0)
            def _():
                pltpu.make_async_copy(own_ref.at[place, far_z], target, sem).start()

            @pl.when(mate == 1)
            def _():
                pltpu.make_async_copy(came_ref.at[place, far_z], target, sem).start()

    lax.fori_loop(0, 32, lambda index, carry: (copies(index, True), carry)[1], 0)
    lax.fori_loop(0, 32, lambda index, carry: (copies(index, False), carry)[1], 0)
    first = 0
    for out, (height, across) in zip(outs, shapes):
        step = 64
        while height % step:
            step //= 2
        if across == 1:
            out[...] = lines[first : first + height, :]
        else:

            def unfold(index, carry, out=out, across=across, step=step, first=first):
                count = step * across
                start = pl.multiple_of(first + index * count, 16)
                wide[pl.ds(0, count), :] = lines[pl.ds(start, count), :].astype(f32)
                low = pl.multiple_of(index * step, step)
                for column in range(across):
                    out[pl.ds(low, step), column * LANES : (column + 1) * LANES] = wide[
                        pl.ds(column, step, stride=across), :
                    ].astype(bf16)
                return carry

            lax.fori_loop(0, height // step, unfold, 0)
        first += height * across


def lay_out(held, came, shapes, rank):
    block = 2 * held[0].shape[2]
    total = 8 * block * held[0].shape[1]
    vmem = pl.BlockSpec(memory_space=pltpu.VMEM)
    hbm = pl.BlockSpec(memory_space=pl.ANY)
    return pl.pallas_call(
        partial(lay_out_kernel, shapes, block),
        out_shape=[jax.ShapeDtypeStruct((h, a * LANES), bf16) for h, a in shapes],
        in_specs=[pl.BlockSpec(memory_space=pltpu.SMEM)] + [hbm] * 4,
        out_specs=[vmem] * len(shapes),
        scratch_shapes=[
            pltpu.VMEM((total, LANES), bf16),
            pltpu.VMEM((64 * 16, LANES), f32),
            pltpu.SemaphoreType.DMA((64,)),
        ],
        name="lay_out",
    )(rank.reshape(1), *held, *came)


def write_lines(buffer, left, right, total, first, step, own=None):
    tall, height = left.shape
    across = (right.shape[1] if own is None else 3 * D) // LANES
    rows = step * across
    assert first % rows == 0 and height % step == 0

    def kernel(*refs):
        left_ref, right_ref, out_ref = refs[0], refs[1], refs[-1]
        got = lax.dot_general(
            left_ref[...], right_ref[...], (((0,), (0,)), ((), ())), preferred_element_type=f32
        )
        for column in range(across):
            if own is None:
                piece = got[:, column * LANES : (column + 1) * LANES]
            else:
                per = D // LANES
                source = column // per
                piece = jnp.where(
                    refs[2][0] == column % per, got[:, source * LANES : (source + 1) * LANES], 0.0
                )
            out_ref[pl.ds(column, step, stride=across), :] = piece

    specs = [
        pl.BlockSpec((tall, step), lambda i: (0, i)),
        pl.BlockSpec(right.shape, lambda i: (0, 0)),
    ]
    args = [left, right]
    if own is not None:
        specs.append(pl.BlockSpec(memory_space=pltpu.SMEM))
        args.append(own.reshape(1))
    aliases = {}
    if buffer is not None:
        specs.append(pl.BlockSpec(memory_space=pl.ANY))
        aliases = {len(args): 0}
        args.append(buffer)
    return pl.pallas_call(
        kernel,
        grid=(height // step,),
        in_specs=specs,
        out_specs=pl.BlockSpec((rows, LANES), lambda i: (first // rows + i, 0)),
        out_shape=jax.ShapeDtypeStruct((total, LANES), f32),
        input_output_aliases=aliases,
        name="write_lines",
    )(*args)


def write_rest(buffer, matrix, rest, first):
    height = matrix.shape[0]
    across = D // LANES
    rows = height * across + rest.shape[0]

    def kernel(matrix_ref, rest_ref, buffer_ref, out_ref):
        for column in range(across):
            out_ref[pl.ds(column, height, stride=across), :] = matrix_ref[
                :, column * LANES : (column + 1) * LANES
            ]
        out_ref[height * across :, :] = rest_ref[...]

    return pl.pallas_call(
        kernel,
        grid=(1,),
        in_specs=[
            pl.BlockSpec(matrix.shape, lambda i: (0, 0)),
            pl.BlockSpec(rest.shape, lambda i: (0, 0)),
            pl.BlockSpec(memory_space=pl.ANY),
        ],
        out_specs=pl.BlockSpec((rows, LANES), lambda i: (first // rows, 0)),
        out_shape=jax.ShapeDtypeStruct(buffer.shape, f32),
        input_output_aliases={2: 0},
        name="write_rest",
    )(matrix, rest, buffer)


def reduce_blocks(blocks, pick):
    group_rank = lax.axis_index("grp")
    rest = blocks.shape[2:]
    blocks = blocks.reshape((4, 2) + blocks.shape[1:])
    mine = group_rank & 1

    def entry(core):
        zero = jnp.int32(0)
        start = (zero, core, pick) + (zero,) * len(rest)
        return lax.dynamic_slice(blocks, start, (4, 1, 1) + rest).reshape((2, 2) + rest)

    def step(value, place, bit):
        mine = (group_rank & bit) // bit
        sent = lax.dynamic_slice_in_dim(value, 1 - mine, 1, place)
        kept = lax.dynamic_slice_in_dim(value, mine, 1, place)
        return kept + swap(sent, "grp", bit)

    blocks = entry(mine) + swap(entry(1 - mine), "grp", 1)
    half = rest[-2] // 2
    results = []
    for low, order in zip((0, half), group_orders()):
        part = lax.slice_in_dim(blocks, low, low + half, axis=blocks.ndim - 2)
        for bit in order:
            part = step(part, 0 if bit == 4 else 1, bit)
        results.append(part.reshape(rest[:-2] + (half, LANES)))
    return jnp.concatenate(results, axis=-2)


def scatter_near(items, axis, wire):
    came = [swap(items[k].astype(wire), axis, k).astype(f32) for k in range(1, len(items))]
    return tree_join([items[0].astype(f32)] + came, jnp.add)


def head_scores(query_ref, key_ref, bias_ref, head, causal):
    query = query_ref[...]
    lane = lax.broadcasted_iota(jnp.int32, query.shape, 1)
    query = jnp.where(lane // HEAD == head, query * jnp.bfloat16(HEAD ** (-0.5)), jnp.bfloat16(0))
    scores = times_back(key_ref[...], query)
    if causal:
        key_at = lax.broadcasted_iota(jnp.int32, scores.shape, 0)
        query_at = lax.broadcasted_iota(jnp.int32, scores.shape, 1)
        return query, jnp.where(query_at >= key_at, scores, masked_score)
    return query, scores + bias_ref[...]


def head_rows(parts):
    row = lax.broadcasted_iota(jnp.int32, parts[0].shape, 0)
    joined = parts[-1]
    for head in range(len(parts) - 2, -1, -1):
        joined = jnp.where(row < (head + 1) * HEAD, parts[head], joined)
    return joined.T


def attend_forward_kernel(causal, query_ref, key_ref, value_ref, bias_ref, out_ref, total_ref):
    parts = []
    for head in range(query_ref.shape[1] // HEAD):
        _, scores = head_scores(query_ref, key_ref, bias_ref, head, causal)
        highest = jnp.max(scores, axis=0, keepdims=True)
        weights = jnp.exp(scores - highest)
        total = jnp.sum(weights, axis=0, keepdims=True)
        weights = (weights * (1.0 / total)).astype(bf16)
        parts.append(over_rows(value_ref[...], weights))
        total_ref[head : head + 1, :] = highest + jnp.log(total)
    out_ref[...] = head_rows(parts).astype(bf16)


def query_tile(rows):
    return 256 if rows % 256 == 0 else rows


def attend_forward(query, keys, values, bias, causal=False):
    rows, wide = query.shape
    tile = query_tile(rows)
    whole = pl.BlockSpec(keys.shape, lambda i: (0, 0))
    return pl.pallas_call(
        partial(attend_forward_kernel, causal),
        grid=(rows // tile,),
        in_specs=[
            pl.BlockSpec((tile, wide), lambda i: (i, 0)),
            whole,
            whole,
            pl.BlockSpec(bias.shape, lambda i: (0, 0)),
        ],
        out_specs=[
            pl.BlockSpec((tile, wide), lambda i: (i, 0)),
            pl.BlockSpec((wide // HEAD, tile), lambda i: (0, i)),
        ],
        out_shape=[
            jax.ShapeDtypeStruct((rows, wide), bf16),
            jax.ShapeDtypeStruct((wide // HEAD, rows), f32),
        ],
        name="attend_forward",
    )(query, keys, values, bias)


def attend_backward_kernel(
    causal,
    grad_ref,
    query_ref,
    key_ref,
    value_ref,
    total_ref,
    bias_ref,
    grad_query_ref,
    grad_key_ref,
    grad_value_ref,
    key_sum,
    value_sum,
):
    @pl.when(pl.program_id(0) == 0)
    def _():
        key_sum[...] = jnp.zeros_like(key_sum)
        value_sum[...] = jnp.zeros_like(value_sum)

    grad = grad_ref[...]
    lane = lax.broadcasted_iota(jnp.int32, grad.shape, 1)
    parts = []
    for head in range(grad.shape[1] // HEAD):
        query, scores = head_scores(query_ref, key_ref, bias_ref, head, causal)
        weights = jnp.exp(scores - total_ref[head : head + 1, :])
        grad_head = jnp.where(lane // HEAD == head, grad, jnp.bfloat16(0))
        grad_weights = times_back(value_ref[...], grad_head)
        inner = jnp.sum(weights * grad_weights, axis=0, keepdims=True)
        grad_scores = (weights * (grad_weights - inner)).astype(bf16)
        value_sum[...] += times(weights.astype(bf16), grad_head)
        key_sum[...] += times(grad_scores, query)
        parts.append(over_rows(key_ref[...], grad_scores))
    grad_query_ref[...] = (head_rows(parts) * HEAD ** (-0.5)).astype(bf16)

    @pl.when(pl.program_id(0) == pl.num_programs(0) - 1)
    def _():
        grad_key_ref[...] = key_sum[...].astype(bf16)
        grad_value_ref[...] = value_sum[...].astype(bf16)


def attend_backward(grad_mixed, query, keys, values, log_total, bias, causal=False):
    rows, wide = query.shape
    tile = query_tile(rows)
    some = pl.BlockSpec((tile, wide), lambda i: (i, 0))
    whole = pl.BlockSpec(keys.shape, lambda i: (0, 0))
    return pl.pallas_call(
        partial(attend_backward_kernel, causal),
        grid=(rows // tile,),
        in_specs=[
            some,
            some,
            whole,
            whole,
            pl.BlockSpec((wide // HEAD, tile), lambda i: (0, i)),
            pl.BlockSpec(bias.shape, lambda i: (0, 0)),
        ],
        out_specs=[some, whole, whole],
        out_shape=[
            jax.ShapeDtypeStruct((rows, wide), bf16),
            jax.ShapeDtypeStruct(keys.shape, bf16),
            jax.ShapeDtypeStruct(keys.shape, bf16),
        ],
        scratch_shapes=[pltpu.VMEM(keys.shape, f32), pltpu.VMEM(keys.shape, f32)],
        name="attend_backward",
    )(grad_mixed, query, keys, values, log_total, bias)


def stand_up(rows):
    blank = jnp.zeros((LANES - rows.shape[0], rows.shape[1]), rows.dtype)
    return jnp.concatenate([rows, blank]).T


def loss_forward_kernel(last, rank_ref, here_ref, states_ref, table_ref, target_ref, out_ref):
    target = stand_up(jnp.broadcast_to(target_ref[0].astype(f32), (8, target_ref.shape[2])))
    target = target[:, 0:1].astype(jnp.int32)

    def work(columns, short):
        logits = times(states_ref[0], table_ref[:, :columns])
        column = lax.broadcasted_iota(jnp.int32, logits.shape, 1)
        if short:
            logits = jnp.where(column < here_ref[0], logits, masked_score)
        highest = jnp.max(logits, axis=1, keepdims=True)
        total = jnp.sum(jnp.exp(logits - highest), axis=1, keepdims=True)
        picked = jnp.sum(jnp.where(column == target, logits, 0.0), axis=1, keepdims=True)
        lane = lax.broadcasted_iota(jnp.int32, (logits.shape[0], LANES), 1)
        packed = jnp.where(lane == 0, highest, jnp.where(lane == 1, total, picked))
        out_ref[0] = packed.T[:8]

    width = table_ref.shape[1]

    @pl.when(here_ref[0] == width)
    def _():
        work(width, False)

    @pl.when(here_ref[0] != width)
    def _():
        work(round_up(last, LANES), True)


def loss_forward(states, table, targets, here, rank, last):
    count, tile, deep = states.shape
    return pl.pallas_call(
        partial(loss_forward_kernel, last),
        grid_spec=pltpu.PrefetchScalarGridSpec(
            num_scalar_prefetch=2,
            grid=(count,),
            in_specs=[
                pl.BlockSpec((1, tile, deep), lambda i, rank, here: (i, 0, 0)),
                pl.BlockSpec(table.shape, lambda i, rank, here: (0, 0)),
                pl.BlockSpec((1, 1, tile), lambda i, rank, here: (i, 0, 0)),
            ],
            out_specs=pl.BlockSpec((1, 8, tile), lambda i, rank, here: (i ^ rank[0], 0, 0)),
        ),
        out_shape=jax.ShapeDtypeStruct((count, 8, tile), f32),
        name="loss_forward",
    )(rank.reshape(1), here.reshape(1), states, table, targets)


def join_stats_kernel(*refs):
    parts, out_ref = [ref[...] for ref in refs[:-1]], refs[-1]
    while len(parts) > 1:
        pairs = []
        for first, second in zip(parts[::2], parts[1::2]):
            biggest = jnp.maximum(first[:, 0:1], second[:, 0:1])
            summed = first[:, 1:2] * jnp.exp(first[:, 0:1] - biggest) + second[:, 1:2] * jnp.exp(
                second[:, 0:1] - biggest
            )
            picked = first[:, 2:3] + second[:, 2:3]
            pairs.append(jnp.concatenate([biggest, summed, picked, first[:, 3:]], axis=1))
        parts = pairs
    out_ref[...] = parts[0]


def join_stats(parts):
    vmem = pl.BlockSpec(memory_space=pltpu.VMEM)
    return pl.pallas_call(
        join_stats_kernel,
        in_specs=[vmem] * len(parts),
        out_specs=vmem,
        out_shape=jax.ShapeDtypeStruct(parts[0].shape, f32),
        name="join_stats",
    )(*parts)


def loss_backward_kernel(
    last, rank_ref, here_ref, states_ref, table_ref, target_ref, scale_ref, grad_ref, out_ref
):
    target = stand_up(jnp.broadcast_to(target_ref[0].astype(f32), (8, target_ref.shape[2])))
    target = target[:, 0:1].astype(jnp.int32)
    scale = stand_up(scale_ref[0])

    def work(columns, short):
        logits = times(states_ref[0], table_ref[:, :columns])
        column = lax.broadcasted_iota(jnp.int32, logits.shape, 1)
        soft = jnp.exp(logits - scale[:, 0:1])
        grad = jnp.where(column == target, soft - 1.0, soft) * scale[:, 1:2]
        if short:
            grad = jnp.where(column < here_ref[0], grad, 0.0)
        grad = grad.astype(bf16)
        grad_ref[0, :, :columns] = grad
        if columns < grad_ref.shape[2]:
            grad_ref[0, :, columns:] = jnp.zeros(
                (grad.shape[0], grad_ref.shape[2] - columns), bf16
            )
        out_ref[0] = times_back(grad, table_ref[:, :columns])

    width = table_ref.shape[1]

    @pl.when(here_ref[0] == width)
    def _():
        work(width, False)

    @pl.when(here_ref[0] != width)
    def _():
        work(round_up(last, LANES), True)


def loss_backward(states, table, targets, scales, here, rank, last):
    count, tile, deep = states.shape
    width = table.shape[1]
    return pl.pallas_call(
        partial(loss_backward_kernel, last),
        grid_spec=pltpu.PrefetchScalarGridSpec(
            num_scalar_prefetch=2,
            grid=(count,),
            in_specs=[
                pl.BlockSpec((1, tile, deep), lambda i, rank, here: (i, 0, 0)),
                pl.BlockSpec(table.shape, lambda i, rank, here: (0, 0)),
                pl.BlockSpec((1, 1, tile), lambda i, rank, here: (i, 0, 0)),
                pl.BlockSpec((1, 2, tile), lambda i, rank, here: (i ^ rank[0], 0, 0)),
            ],
            out_specs=[
                pl.BlockSpec((1, tile, width), lambda i, rank, here: (i, 0, 0)),
                pl.BlockSpec((1, tile, deep), lambda i, rank, here: (i, 0, 0)),
            ],
        ),
        out_shape=[
            jax.ShapeDtypeStruct((count, tile, width), bf16),
            jax.ShapeDtypeStruct((count, tile, deep), f32),
        ],
        name="loss_backward",
    )(rank.reshape(1), here.reshape(1), states, table, targets, scales)


def own_blocks_kernel(pieces, lines, rank_ref, *refs):
    out_ref, stage = refs[-2], refs[-1]
    count = out_ref.shape[0]

    def branch(seq_rank):
        for place in range(count):
            low = (4 * place + seq_rank) * lines
            for first, left, right in pieces:
                left_ref, right_ref = refs[left], refs[right]
                across = right_ref.shape[1] // LANES
                last = first + left_ref.shape[1] * across
                if not first <= low < last:
                    continue
                top = (low - first) // across
                bottom = -(-(low + lines - first) // across)
                skip = low - first - top * across
                got = lax.dot_general(
                    left_ref[:, top:bottom],
                    right_ref[...],
                    (((0,), (0,)), ((), ())),
                    preferred_element_type=f32,
                )
                target = stage if (bottom - top) * across != lines else out_ref.at[place]
                for column in range(across):
                    target[pl.ds(column, bottom - top, stride=across), :] = got[
                        :, column * LANES : (column + 1) * LANES
                    ]
                if target is stage:
                    out_ref[place] = stage[skip : skip + lines, :]

    for seq_rank in range(4):

        @pl.when(rank_ref[0] == seq_rank)
        def _(seq_rank=seq_rank):
            branch(seq_rank)


def own_blocks(pairs, firsts, lines, count, seq_rank):
    vmem = pl.BlockSpec(memory_space=pltpu.VMEM)
    args = [value for pair in pairs for value in pair]
    pieces = [(first, 2 * k, 2 * k + 1) for k, first in enumerate(firsts)]
    return pl.pallas_call(
        partial(own_blocks_kernel, pieces, lines),
        in_specs=[pl.BlockSpec(memory_space=pltpu.SMEM)] + [vmem] * len(args),
        out_specs=vmem,
        out_shape=jax.ShapeDtypeStruct((count, lines, LANES), f32),
        scratch_shapes=[pltpu.VMEM((lines + 64, LANES), f32)],
        name="own_blocks",
    )(seq_rank.reshape(1), *args)


def mlp_forward(stream, norm_gain, norm_shift, w_up, b_up, w_down, b_down):
    normed = layer_norm(stream, norm_gain, norm_shift).astype(bf16)
    raised = times(normed, w_up) + b_up
    active = jax.nn.gelu(raised, approximate=False).astype(bf16)
    return (stream + times(active, w_down) + b_down, normed, raised, active)


def mlp_backward(grad_stream, stream, norm_gain, norm_shift, raised, w_up, w_down):
    grad_branch = grad_stream.astype(bf16)
    grad_bdown = column_sum(grad_branch)
    grad_active = times_back(grad_branch, w_down)
    _, gelu_pull = jax.vjp(partial(jax.nn.gelu, approximate=False), raised)
    grad_raised = gelu_pull(grad_active)[0].astype(bf16)
    grad_bup = column_sum(grad_raised)
    grad_normed = times_back(grad_raised, w_up)
    grad_in, grad_gain, grad_shift = norm_back(grad_normed, stream, norm_gain, norm_shift)
    return (
        grad_stream + grad_in,
        grad_branch,
        grad_raised,
        grad_bup,
        grad_bdown,
        grad_gain,
        grad_shift,
    )


def adamw(weight_now, moment, second, gradient, factor, bias_one, bias_two):
    scaled = gradient * factor
    new_moment = beta_one * moment + (1.0 - beta_one) * scaled
    new_second = beta_two * second + (1.0 - beta_two) * scaled * scaled
    step_size = (
        new_moment / bias_one / (jnp.sqrt(new_second / bias_two) + adam_eps) + decay * weight_now
    )
    return (weight_now - rate * step_size, new_moment, new_second)


def round_up(amount, unit):
    return -(-amount // unit) * unit


def on_device(*args):
    return train_step(*args)


def train_step(
    frames,
    input_ids,
    target_ids,
    lengths,
    present,
    step_count,
    enc_params,
    enc_moment,
    enc_second,
    dec_params,
    dec_moment,
    dec_second,
    table_params,
    table_moment,
    table_second,
):
    seq_size = lax.axis_size("seq")
    grp_size = lax.axis_size("grp")
    seq_rank = lax.axis_index("seq")
    group_rank = lax.axis_index("grp")
    lead = (seq_rank == 0).astype(f32)

    frame_rows = frames.shape[1]
    rows = round_up(frame_rows, 128)
    rank = group_rank * seq_size + seq_rank
    devices = grp_size * seq_size
    enc_count = enc_params.shape[0]
    enc_lines = round_up(enc_count, 64 * LANES) // LANES
    lag = enc_lines * LANES - enc_count
    enc_here = enc_params.astype(bf16)
    enc_next = lax.ppermute(
        enc_here[: lag * devices], ("grp", "seq"), [(i + 1, i) for i in range(devices - 1)]
    )
    enc_block = lax.dynamic_slice_in_dim(
        jnp.concatenate([enc_here, enc_next]), lag * rank, enc_lines * LANES
    ).reshape(enc_lines, LANES)
    dec_lines = dec_params.shape[0] // LANES
    enc_parts = gather_near_lines(enc_block)
    frame_slots = gather_near(jnp.pad(frames[0], ((0, rows - frame_rows), (0, 0))), "seq")
    dec_parts = gather_near_lines(dec_params.astype(bf16).reshape(dec_lines, LANES))
    enc_parts = gather_far_lines(enc_parts, 0)
    enc_parts = gather_far_lines(enc_parts, 1)
    enc_came = [swap(part, "grp", 1) for part in enc_parts]
    dec_parts = gather_far_lines(dec_parts, 0)
    dec_parts = gather_far_lines(dec_parts, 1)
    dec_came = [swap(part, "grp", 1) for part in dec_parts]
    vocab = table_params.shape[1]
    width = round_up(round_up(vocab, grp_size) // grp_size, 128)
    ids_here = jnp.concatenate([input_ids, target_ids])
    ids_rows = jnp.concatenate([ids_here >> 8, ids_here & 255]).astype(bf16).reshape(1, -1)
    spare = 16 * width - ids_rows.shape[1]
    ids_rows = jnp.pad(ids_rows, ((0, 0), (0, spare))).reshape(16, width)
    table_wide = jnp.concatenate(
        [
            jnp.pad(table_params.astype(bf16), ((0, 0), (0, width * grp_size - vocab))),
            jnp.tile(ids_rows, (1, grp_size)),
        ]
    )
    chans = D // grp_size
    table_came = trade_near(
        [
            lax.dynamic_slice_in_dim(table_wide, (group_rank ^ k) * width, width, 1)
            for k in range(grp_size)
        ],
        "grp",
    )
    table = jnp.concatenate(reorder([piece[:chans] for piece in table_came], group_rank))
    vocab_first = seq_rank * vocab + group_rank * width
    vocab_here = jnp.clip(vocab - group_rank * width, 0, width)
    ids_slots = jnp.stack([piece[chans:] for piece in table_came]).reshape(grp_size, -1)
    ids_slots = ids_slots[:, : 4 * LEN].astype(jnp.int32).reshape(grp_size, 2, 2, LEN)
    ids_slots = ids_slots[:, 0] * 256 + ids_slots[:, 1]

    small = (7 + 7 + 11) * D + 2 * F
    enc_qkv, enc_wout, enc_wup, enc_wdown, positions, small_lines = lay_out(
        enc_parts,
        enc_came,
        [(h, w // LANES) for h, w in enc_layout()[:5]] + [(small // LANES, 1)],
        rank,
    )
    gains, shifts, biases, up_bias = split_flat(
        small_lines.astype(f32).reshape(-1), enc_layout()[5:]
    )
    positions = positions.astype(f32)
    span = D // seq_size

    def own(matrix, parts):
        return jnp.concatenate(
            [
                lax.dynamic_slice_in_dim(matrix, part * D + seq_rank * span, span, matrix.ndim - 1)
                for part in range(parts)
            ],
            axis=-1,
        )

    def own_bias(row):
        return lax.dynamic_slice_in_dim(biases[row], seq_rank * span, span, 0)

    half_width = D // 2
    stride = math.log(10000.0) / (half_width - 1)
    inverse = jnp.exp(-stride * jnp.arange(half_width, dtype=f32))
    x_slots = []
    for k in range(seq_size):
        offset = ((seq_rank ^ k) * frame_rows).astype(f32)
        angles = (jnp.arange(rows, dtype=f32) + offset)[:, None] * inverse[None, :]
        wave = jnp.concatenate([jnp.sin(angles), jnp.cos(angles)], axis=1)
        x_slots.append(frame_slots[k].astype(f32) + wave)
    x_all = jnp.concatenate(x_slots)
    x_enc0 = x_slots[0]
    h_enc1 = layer_norm(x_all, gains[0], shifts[0]).astype(bf16)
    own_enc_qkv = own(enc_qkv, 3)
    packed = times(h_enc1, own_enc_qkv)
    q_enc = (packed[:, :span] + own_bias(0)).astype(bf16)
    k_enc = packed[:, span : 2 * span].astype(bf16)
    v_enc = (packed[:, 2 * span :] + own_bias(1)).astype(bf16)
    frame_bias = jnp.where(jnp.arange(rows * seq_size) % rows < frame_rows, 0.0, masked_score)
    frame_bias = frame_bias.astype(f32)[:, None]
    o_own, lse_enc = attend_forward(q_enc, k_enc, v_enc, frame_bias)

    def to_rows(value):
        pieces = [value[k * rows : (k + 1) * rows] for k in range(seq_size)]
        return jnp.concatenate(reorder(trade_near(pieces, "seq"), seq_rank), axis=1)

    def to_heads(value):
        pieces = reorder([value[:, k * span : (k + 1) * span] for k in range(seq_size)], seq_rank)
        return jnp.concatenate(trade_near(pieces, "seq"), axis=0)

    def two_to_heads(first, second):
        pieces = reorder(
            [
                jnp.concatenate(
                    [first[:, k * span : (k + 1) * span], second[:, k * span : (k + 1) * span]], axis=1
                )
                for k in range(seq_size)
            ],
            seq_rank,
        )
        return jnp.concatenate(trade_near(pieces, "seq"), axis=0)

    def two_to_rows(first, second):
        both = jnp.concatenate([first, second], axis=1)
        pieces = [both[k * rows : (k + 1) * rows] for k in range(seq_size)]
        pieces = reorder(trade_near(pieces, "seq"), seq_rank)
        return jnp.concatenate(
            [piece[:, :span] for piece in pieces] + [piece[:, span:] for piece in pieces], axis=1
        )

    o_enc = to_rows(o_own)
    x_enc1 = x_enc0 + times(o_enc, enc_wout) + biases[2]
    x_enc2, h_enc2, up_enc, act_enc = mlp_forward(
        x_enc1, gains[1], shifts[1], enc_wup, up_bias[0], enc_wdown, biases[3]
    )
    enc_out = layer_norm(x_enc2, gains[2], shifts[2]).astype(bf16)
    dec_qkv, dec_wout, cross_wq, cross_wkv, cross_wout, dec_wup, dec_wdown = lay_out(
        dec_parts, dec_came, [(h, w // LANES) for h, w in dec_layout()], rank
    )
    paired = times(enc_out, cross_wkv)
    k_rows = paired[:, :D].astype(bf16)
    v_rows = (paired[:, D:] + biases[8]).astype(bf16)
    pair_cross = two_to_heads(k_rows, v_rows)
    k_cross = pair_cross[:, :span]
    v_cross = pair_cross[:, span:]

    ids = ids_slots[:, 0].reshape(-1)
    columns = jnp.arange(width)[None, :]
    inside = columns < vocab_here
    id_hot = ((ids[:, None] - vocab_first == columns) & inside).astype(bf16)
    looked = times_back(id_hot, table).astype(bf16).reshape(grp_size, LEN, D)
    part_rows = LEN // seq_size

    def share_rows(value, wire):
        pieces = [value[k * part_rows : (k + 1) * part_rows] for k in range(seq_size)]
        mine = scatter_near(reorder(pieces, seq_rank), "seq", wire)
        return jnp.concatenate(reorder(gather_near(mine.astype(wire), "seq"), seq_rank))

    token_emb = reduce_group(looked, bf16, bf16)
    token_emb = share_rows(token_emb, bf16).astype(f32)

    def all_heads(value):
        return reorder(gather_near(value, "seq"), seq_rank)

    x_dec0 = token_emb + positions
    h_dec1 = layer_norm(x_dec0, gains[3], shifts[3]).astype(bf16)
    packed = times(h_dec1, own(dec_qkv, 3))
    q_dec = (packed[:, :span] + own_bias(4)).astype(bf16)
    k_dec = packed[:, span : 2 * span].astype(bf16)
    v_dec = (packed[:, 2 * span :] + own_bias(5)).astype(bf16)
    no_bias = jnp.zeros((8, 1), f32)
    o_own_dec, lse_dec = attend_forward(q_dec, k_dec, v_dec, no_bias, True)
    o_dec = jnp.concatenate(all_heads(o_own_dec), axis=1)
    x_dec1 = x_dec0 + times(o_dec, dec_wout) + biases[6]
    h_dec2 = layer_norm(x_dec1, gains[4], shifts[4]).astype(bf16)
    q_cross = (times(h_dec2, own(cross_wq, 1)) + own_bias(7)).astype(bf16)
    o_own_cross, lse_cross = attend_forward(q_cross, k_cross, v_cross, frame_bias)
    o_cross = jnp.concatenate(all_heads(o_own_cross), axis=1)
    x_dec2 = x_dec1 + times(o_cross, cross_wout) + biases[9]
    x_dec3, h_dec3, up_dec, act_dec = mlp_forward(
        x_dec2, gains[5], shifts[5], dec_wup, up_bias[1], dec_wdown, biases[10]
    )
    states = layer_norm(x_dec3, gains[6], shifts[6]).astype(bf16)

    all_states = gather_group(states)
    target_rows = ids_slots[:, 1] - vocab_first
    target_rows = jnp.where(target_rows < vocab_here, target_rows, -1)[:, None, :]
    last = vocab - (grp_size - 1) * width
    stats = loss_forward(all_states, table, target_rows, vocab_here, group_rank, last)
    for bit in bits_of("grp"):
        stats = join_stats([stats, swap(stats, "grp", bit)])
    stats = join_stats(gather_near(stats, "seq"))
    log_total = stats[:, 0] + jnp.log(stats[:, 1])
    valid = (
        (jnp.arange(LEN)[None, :] < lengths[:, None]) & (present[:, None] > 0)
    ).astype(f32)
    token_total = jnp.sum((lengths * present).astype(f32))
    row_weight = valid / token_total
    scales = jnp.stack([log_total, row_weight], axis=1)
    loss_sum = jnp.sum((log_total - stats[:, 2]) * valid)
    grad_logits, grad_states_all = loss_backward(
        all_states, table, target_rows, scales, vocab_here, group_rank, last
    )
    grad_states = share_rows(reduce_group(grad_states_all, bf16), bf16).astype(f32)

    table_main = lax.optimization_barrier(
        over_rows(all_states.reshape(-1, D), grad_logits.reshape(-1, width))
    )

    grad_x3, grad_g6, grad_s6 = norm_back(grad_states, x_dec3, gains[6], shifts[6])
    dec_at = [0]
    for height, across in dec_layout():
        dec_at.append(dec_at[-1] + height * across // LANES)
    grad_x2, grad_down_dec, grad_up_dec, grad_dec_bup, grad_b10, grad_g5, grad_s5 = mlp_backward(
        grad_x3, x_dec2, gains[5], shifts[5], up_dec, dec_wup, dec_wdown
    )
    grad_branch = grad_x2.astype(bf16)
    grad_cross_out = grad_branch
    grad_b9 = column_sum(grad_branch)
    own_cross_wout = lax.dynamic_slice_in_dim(cross_wout, seq_rank * span, span, 0)
    grad_mixed = times_back(grad_branch, own_cross_wout).astype(bf16)
    grad_qc_own, grad_kc_own, grad_vc_own = attend_backward(
        grad_mixed, q_cross, k_cross, v_cross, lse_cross, frame_bias
    )
    grad_qc = jnp.concatenate(all_heads(grad_qc_own), axis=1)
    grad_pair = two_to_rows(grad_kc_own, grad_vc_own)
    grad_b7 = column_sum(grad_qc)
    grad_in, grad_g4, grad_s4 = norm_back(
        times_back(grad_qc, cross_wq), x_dec1, gains[4], shifts[4]
    )
    grad_x1 = grad_x2 + grad_in
    grad_branch = grad_x1.astype(bf16)
    grad_self_out = grad_branch
    grad_b6 = column_sum(grad_branch)
    own_dec_wout = lax.dynamic_slice_in_dim(dec_wout, seq_rank * span, span, 0)
    grad_mixed = times_back(grad_branch, own_dec_wout).astype(bf16)
    grad_qkv_own = attend_backward(grad_mixed, q_dec, k_dec, v_dec, lse_dec, no_bias, True)
    grad_qkv_own = jnp.concatenate(grad_qkv_own, axis=1)
    grad_qkv_all = all_heads(grad_qkv_own)
    grad_packed = jnp.concatenate(
        [
            piece[:, part * span : (part + 1) * span]
            for part in range(3)
            for piece in grad_qkv_all
        ],
        axis=1,
    )
    sums = column_sum(grad_packed)
    grad_b4 = sums[:D]
    grad_b5 = sums[2 * D :]
    grad_in, grad_g3, grad_s3 = norm_back(
        times_back(grad_packed, dec_qkv), x_dec0, gains[3], shifts[3]
    )
    grad_x0 = grad_x1 + grad_in

    grad_embed_all = gather_group(grad_x0.astype(bf16)).reshape(-1, D)
    grad_table = table_main + over_rows(grad_embed_all, id_hot)
    table_back = trade_near(
        [
            lax.dynamic_slice_in_dim(grad_table, (group_rank ^ k) * chans, chans, 0)
            for k in range(grp_size)
        ],
        "grp",
    )
    table_grad = jnp.concatenate(reorder(table_back, group_rank), axis=1)
    table_grad = table_grad[:, :vocab]

    wkv_buf = write_lines(None, enc_out, grad_pair, 2 * D * D // LANES, 0, 128)
    grad_b8 = column_sum(grad_pair[:, D:])
    grad_enc2, grad_g2, grad_s2 = norm_back(
        times_back(grad_pair, cross_wkv), x_enc2, gains[2], shifts[2]
    )

    dec_mine = own_blocks(
        [
            (h_dec1, grad_packed),
            (o_dec, grad_self_out),
            (h_dec2, grad_qc),
            (o_cross, grad_cross_out),
            (h_dec3, grad_up_dec),
            (act_dec, grad_down_dec),
        ],
        [dec_at[k] for k in (0, 1, 2, 4, 5, 6)],
        dec_lines,
        grp_size,
        seq_rank,
    )
    first_block = dec_at[3] // dec_lines
    turn = first_block % seq_size
    wkv_blocks = wkv_buf.reshape(seq_size, dec_lines, LANES)
    wkv_mine = scatter_near(
        [
            lax.dynamic_index_in_dim(wkv_blocks, (seq_rank ^ k) ^ turn, 0, False)
            for k in range(seq_size)
        ],
        "seq",
        f32,
    )
    wkv_place = (first_block + (seq_rank ^ turn)) // seq_size
    dec_mine = jnp.stack(
        [jnp.where(wkv_place == k, wkv_mine, dec_mine[k]) for k in range(grp_size)]
    )
    dec_grad = reduce_blocks(dec_mine[:, None], jnp.int32(0)).reshape(-1)

    enc_at = [0]
    for height, across in enc_layout()[:5]:
        enc_at.append(enc_at[-1] + height * across // LANES)
    enc_total = enc_lines * devices
    grad_enc1, grad_down, grad_up, grad_enc_bup, grad_b3, grad_g1, grad_s1 = mlp_backward(
        grad_enc2, x_enc1, gains[1], shifts[1], up_enc, enc_wup, enc_wdown
    )
    enc_buf = write_lines(None, act_enc, grad_down, enc_total, enc_at[3], 512)
    enc_buf = write_lines(enc_buf, h_enc2, grad_up, enc_total, enc_at[2], 128)
    grad_branch = grad_enc1.astype(bf16)
    enc_buf = write_lines(enc_buf, o_enc, grad_branch, enc_total, enc_at[1], 128)
    grad_b2 = column_sum(grad_branch)
    grad_mixed = times_back(grad_branch, enc_wout).astype(bf16)
    grad_mixed = to_heads(grad_mixed)
    grad_q, grad_k, grad_v = attend_backward(grad_mixed, q_enc, k_enc, v_enc, lse_enc, frame_bias)
    grad_packed = jnp.concatenate([grad_q, grad_k, grad_v], axis=1)
    enc_buf = write_lines(enc_buf, h_enc1, grad_packed, enc_total, 0, 128, own=seq_rank)
    sums = column_sum(grad_packed)

    def placed(values):
        return lax.dynamic_update_slice(jnp.zeros((D,), f32), values, (seq_rank * span,))

    grad_b0 = placed(sums[:span])
    grad_b1 = placed(sums[2 * span :])
    _, grad_g0, grad_s0 = norm_back(
        times_back(grad_packed, own_enc_qkv), x_all, gains[0], shifts[0]
    )
    once = lead
    grad_gains = jnp.stack(
        [grad_g0, grad_g1, grad_g2, grad_g3 * once, grad_g4 * once, grad_g5 * once, grad_g6 * once]
    )
    grad_shifts = jnp.stack(
        [grad_s0, grad_s1, grad_s2, grad_s3 * once, grad_s4 * once, grad_s5 * once, grad_s6 * once]
    )
    grad_biases = jnp.stack(
        [
            grad_b0,
            grad_b1,
            grad_b2,
            grad_b3,
            grad_b4 * once,
            grad_b5 * once,
            grad_b6 * once,
            grad_b7 * once,
            grad_b8,
            grad_b9 * once,
            grad_b10 * once,
        ]
    )
    grad_up_bias = jnp.stack([grad_enc_bup, grad_dec_bup * once])
    rest = jnp.concatenate(
        [grad_gains.reshape(-1), grad_shifts.reshape(-1), grad_biases.reshape(-1), grad_up_bias.reshape(-1)]
    ).reshape(-1, LANES)
    rest = jnp.pad(rest, ((0, enc_total - enc_at[5] - rest.shape[0]), (0, 0)))
    enc_buf = write_rest(enc_buf, grad_x0 * once, rest, enc_at[4])
    pairs = enc_buf.reshape(grp_size, 2, 2, enc_lines, LANES)
    upper = seq_rank // 2
    odd = seq_rank % 2
    away = reduce_blocks(pairs, 1 - upper)
    near = reduce_blocks(lax.optimization_barrier(pairs), upper)
    parts = [
        swap(lax.dynamic_index_in_dim(away, odd, 0, False), "seq", 2),
        swap(lax.dynamic_index_in_dim(away, 1 - odd, 0, False), "seq", 3),
    ]
    parts.append(swap(lax.dynamic_index_in_dim(near, 1 - odd, 0, False), "seq", 1))
    enc_sum = lax.dynamic_index_in_dim(near, odd, 0, False) + parts[2] + (parts[0] + parts[1])
    enc_prev = lax.ppermute(
        enc_sum[enc_lines - lag * devices // LANES :].reshape(-1),
        ("grp", "seq"),
        [(i, i + 1) for i in range(devices - 1)],
    )
    enc_grad = lax.dynamic_slice_in_dim(
        jnp.concatenate([enc_prev, enc_sum.reshape(-1)]), lag * (devices - rank), enc_count
    )

    squares = (
        jnp.sum(enc_sum * enc_sum)
        + jnp.sum(dec_grad * dec_grad)
        + jnp.sum(table_grad * table_grad)
    )
    squares = all_join(pair_join(squares.reshape(1, 1), "grp", jnp.add), "seq", jnp.add)
    mean_loss = loss_sum / token_total
    grad_norm = jnp.sqrt(squares[0, 0])
    factor = jnp.minimum(1.0, clip_limit / (grad_norm + 1e-06))
    steps_done = step_count[0].astype(f32)
    bias_one = 1.0 - beta_one**steps_done
    bias_two = 1.0 - beta_two**steps_done
    enc_new = adamw(enc_params, enc_moment, enc_second, enc_grad, factor, bias_one, bias_two)
    dec_new = adamw(dec_params, dec_moment, dec_second, dec_grad, factor, bias_one, bias_two)
    table_new = adamw(
        table_params, table_moment, table_second, table_grad, factor, bias_one, bias_two
    )
    return (mean_loss, grad_norm, *enc_new, *dec_new, *table_new)


def wide_joined_2(value, axis, join):
    pieces = jax.tree.map(lambda part: lax.all_gather(part, axis), value)
    head = jax.tree.map(lambda part: part[0], pieces)
    tail = jax.tree.map(lambda part: part[1:], pieces)
    total, _ = lax.scan(lambda total, piece: (join(total, piece), None), head, tail)
    return total


def wide_sinusoid(amount, channels, offset):
    half_width = channels // 2
    stride = math.log(10000.0) / (half_width - 1)
    inverse = jnp.exp(-stride * jnp.arange(half_width, dtype=jnp.float32))
    angles = (jnp.arange(amount, dtype=jnp.float32) + offset)[:, None] * inverse[None, :]
    return jnp.concatenate([jnp.sin(angles), jnp.cos(angles)], axis=1)


def wide_times_rows(left_side, right_side):
    return lax.dot_general(
        left_side,
        right_side,
        (((left_side.ndim - 1,), (0,)), ((), ())),
        preferred_element_type=jnp.float32,
    )


def wide_times_back(left_side, right_side):
    return lax.dot_general(
        left_side,
        right_side,
        (((left_side.ndim - 1,), (1,)), ((), ())),
        preferred_element_type=jnp.float32,
    )


def wide_over_rows(left_side, right_side):
    return lax.dot_general(
        left_side, right_side, (((0, 1), (0, 1)), ((), ())), preferred_element_type=jnp.float32
    )


def wide_column_sum(values):
    return jnp.sum(values.astype(jnp.float32), axis=(0, 1))


def wide_split_heads(values):
    return values.reshape(values.shape[0], values.shape[1], HEADS, values.shape[2] // HEADS)


def wide_score_block(query, keys, first_row):
    head_size = query.shape[2] // HEADS
    scores = jnp.einsum(
        "cqhd,ckhd->chqk", wide_split_heads(query), wide_split_heads(keys), preferred_element_type=jnp.float32
    ) * head_size ** (-0.5)
    if first_row is not None:
        allowed = (first_row + jnp.arange(query.shape[1]))[:, None] >= jnp.arange(keys.shape[1])[
            None, :
        ]
        scores = jnp.where(allowed[None, None], scores, masked_score)
    return scores


def wide_attend_forward(query, keys, values, first_row):
    scores = wide_score_block(query, keys, first_row)
    highest_score = jnp.max(scores, axis=-1, keepdims=True)
    log_total = highest_score + jnp.log(
        jnp.sum(jnp.exp(scores - highest_score), axis=-1, keepdims=True)
    )
    weights = jnp.exp(scores - log_total).astype(jnp.bfloat16)
    mixed = jnp.einsum(
        "chqk,ckhd->cqhd", weights, wide_split_heads(values), preferred_element_type=jnp.float32
    )
    return (mixed.reshape(query.shape).astype(jnp.bfloat16), log_total)


def wide_attend_backward(grad_mixed, query, keys, values, log_total, first_row):
    head_size = query.shape[2] // HEADS
    scores = wide_score_block(query, keys, first_row)
    weights = jnp.exp(scores - log_total)
    grad_heads = wide_split_heads(grad_mixed)
    grad_weights = jnp.einsum(
        "cqhd,ckhd->chqk", grad_heads, wide_split_heads(values), preferred_element_type=jnp.float32
    )
    grad_values = jnp.einsum(
        "chqk,cqhd->ckhd",
        weights.astype(jnp.bfloat16),
        grad_heads,
        preferred_element_type=jnp.float32,
    )
    inner = jnp.sum(weights * grad_weights, axis=-1, keepdims=True)
    grad_scores = (weights * (grad_weights - inner)).astype(jnp.bfloat16)
    grad_query = jnp.einsum(
        "chqk,ckhd->cqhd", grad_scores, wide_split_heads(keys), preferred_element_type=jnp.float32
    ) * head_size ** (-0.5)
    grad_keys = jnp.einsum(
        "chqk,cqhd->ckhd", grad_scores, wide_split_heads(query), preferred_element_type=jnp.float32
    ) * head_size ** (-0.5)
    return (
        grad_query.reshape(query.shape),
        grad_keys.reshape(keys.shape),
        grad_values.reshape(values.shape),
    )


def wide_mlp_forward(stream, norm_gain, norm_shift, w_up, b_up, w_down, b_down):
    normed = layer_norm(stream, norm_gain, norm_shift).astype(jnp.bfloat16)
    raised = wide_times_rows(normed, w_up) + b_up
    active = jax.nn.gelu(raised, approximate=False).astype(jnp.bfloat16)
    return (stream + wide_times_rows(active, w_down) + b_down, normed, raised, active)


def wide_mlp_backward(grad_stream, stream, norm_gain, norm_shift, normed, raised, active, w_up, w_down):
    grad_branch = grad_stream.astype(jnp.bfloat16)
    grad_wdown = wide_over_rows(active, grad_branch)
    grad_bdown = wide_column_sum(grad_branch)
    grad_active = wide_times_back(grad_branch, w_down)
    _, gelu_pull = jax.vjp(partial(jax.nn.gelu, approximate=False), raised)
    grad_raised = gelu_pull(grad_active)[0].astype(jnp.bfloat16)
    grad_wup = wide_over_rows(normed, grad_raised)
    grad_bup = wide_column_sum(grad_raised)
    grad_normed = wide_times_back(grad_raised, w_up)
    grad_in, grad_gain, grad_shift = norm_back(grad_normed, stream, norm_gain, norm_shift)
    return (
        grad_stream + grad_in,
        grad_wup,
        grad_bup,
        grad_wdown,
        grad_bdown,
        grad_gain,
        grad_shift,
    )


def wide_merge_stats(first_stats, second_stats):
    biggest = jnp.maximum(first_stats[0], second_stats[0])
    summed = first_stats[1] * jnp.exp(first_stats[0] - biggest) + second_stats[1] * jnp.exp(
        second_stats[0] - biggest
    )
    return (biggest, summed, first_stats[2] + second_stats[2])


def wide_spread_grads(grad_matrix):
    return lax.psum_scatter(grad_matrix, ("grp", "seq"), scatter_dimension=0, tiled=True)


def wide_on_device(
    frames,
    input_ids,
    target_ids,
    lengths,
    present,
    step_count,
    enc_params,
    enc_moment,
    enc_second,
    dec_params,
    dec_moment,
    dec_second,
    table_params,
    table_moment,
    table_second,
):
    enc_full, dec_full = (
        lax.all_gather(enc_params.astype(jnp.bfloat16), ("grp", "seq"), axis=0, tiled=True),
        lax.all_gather(dec_params.astype(jnp.bfloat16), ("grp", "seq"), axis=0, tiled=True),
    )
    table_local = lax.all_gather(table_params.astype(jnp.bfloat16), "grp", axis=0, tiled=True)
    enc_qkv, enc_wout, enc_wup, enc_wdown, positions, gains, shifts, biases, up_bias = split_flat(
        enc_full, enc_layout()
    )
    dec_qkv, dec_wout, cross_wq, cross_wkv, cross_wout, dec_wup, dec_wdown = split_flat(
        dec_full, dec_layout()
    )
    gains = gains.astype(jnp.float32)
    shifts = shifts.astype(jnp.float32)
    biases = biases.astype(jnp.float32)
    up_bias = up_bias.astype(jnp.float32)
    positions = positions.astype(jnp.float32)
    seq_size = lax.axis_size("seq")
    seq_rank = lax.axis_index("seq")
    group_rank = lax.axis_index("grp")
    clip_count = frames.shape[0]
    enc_rows = frames.shape[1]
    dec_rows = LEN // seq_size
    vocab_rows = table_local.shape[1]
    dec_first = seq_rank * dec_rows
    vocab_first = seq_rank * vocab_rows
    x_enc0 = (
        frames.astype(jnp.float32)
        + wide_sinusoid(enc_rows, D, (seq_rank * enc_rows).astype(jnp.float32))[None]
    )
    h_enc1 = layer_norm(x_enc0, gains[0], shifts[0]).astype(jnp.bfloat16)
    packed = wide_times_rows(h_enc1, enc_qkv)
    q_enc = (packed[..., :D] + biases[0]).astype(jnp.bfloat16)
    k_enc = packed[..., D : 2 * D].astype(jnp.bfloat16)
    v_enc = (packed[..., 2 * D :] + biases[1]).astype(jnp.bfloat16)
    keys_enc, vals_enc = (
        lax.all_gather(k_enc, "seq", axis=1, tiled=True),
        lax.all_gather(v_enc, "seq", axis=1, tiled=True),
    )
    o_enc, lse_enc = wide_attend_forward(q_enc, keys_enc, vals_enc, None)
    x_enc1 = x_enc0 + wide_times_rows(o_enc, enc_wout) + biases[2]
    x_enc2, h_enc2, up_enc, act_enc = wide_mlp_forward(
        x_enc1, gains[1], shifts[1], enc_wup, up_bias[0], enc_wdown, biases[3]
    )
    enc_out = layer_norm(x_enc2, gains[2], shifts[2]).astype(jnp.bfloat16)
    local_ids = input_ids - vocab_first
    inside = (local_ids >= 0) & (local_ids < vocab_rows)
    safe_ids = jnp.clip(local_ids, 0, vocab_rows - 1).reshape(-1)
    looked = jnp.take(table_local, safe_ids, axis=1).astype(jnp.float32).T
    looked = jnp.where(inside.reshape(-1)[:, None], looked, 0.0).reshape(clip_count, LEN, D)
    token_emb = lax.psum_scatter(
        looked.astype(jnp.bfloat16), "seq", scatter_dimension=1, tiled=True
    ).astype(jnp.float32)
    x_dec0 = token_emb + lax.dynamic_slice_in_dim(positions, dec_first, dec_rows, 0)[None]
    h_dec1 = layer_norm(x_dec0, gains[3], shifts[3]).astype(jnp.bfloat16)
    packed = wide_times_rows(h_dec1, dec_qkv)
    q_dec = (packed[..., :D] + biases[4]).astype(jnp.bfloat16)
    k_dec = packed[..., D : 2 * D].astype(jnp.bfloat16)
    v_dec = (packed[..., 2 * D :] + biases[5]).astype(jnp.bfloat16)
    paired = wide_times_rows(enc_out, cross_wkv)
    k_cross = paired[..., :D].astype(jnp.bfloat16)
    v_cross = (paired[..., D:] + biases[8]).astype(jnp.bfloat16)
    keys_dec, vals_dec, keys_cross, vals_cross = (
        lax.all_gather(k_dec, "seq", axis=1, tiled=True),
        lax.all_gather(v_dec, "seq", axis=1, tiled=True),
        lax.all_gather(k_cross, "seq", axis=1, tiled=True),
        lax.all_gather(v_cross, "seq", axis=1, tiled=True),
    )
    o_dec, lse_dec = wide_attend_forward(q_dec, keys_dec, vals_dec, dec_first)
    x_dec1 = x_dec0 + wide_times_rows(o_dec, dec_wout) + biases[6]
    h_dec2 = layer_norm(x_dec1, gains[4], shifts[4]).astype(jnp.bfloat16)
    q_cross = (wide_times_rows(h_dec2, cross_wq) + biases[7]).astype(jnp.bfloat16)
    o_cross, lse_cross = wide_attend_forward(q_cross, keys_cross, vals_cross, None)
    x_dec2 = x_dec1 + wide_times_rows(o_cross, cross_wout) + biases[9]
    x_dec3, h_dec3, up_dec, act_dec = wide_mlp_forward(
        x_dec2, gains[5], shifts[5], dec_wup, up_bias[1], dec_wdown, biases[10]
    )
    states = layer_norm(x_dec3, gains[6], shifts[6]).astype(jnp.bfloat16)
    all_states = lax.all_gather(states, "seq", axis=1, tiled=True)
    logits = wide_times_rows(all_states, table_local)
    target_local = target_ids - vocab_first
    has_target = (target_local >= 0) & (target_local < vocab_rows)
    top_local = jnp.max(logits, axis=-1)
    total_local = jnp.sum(jnp.exp(logits - top_local[..., None]), axis=-1)
    picked_local = jnp.take_along_axis(
        logits, jnp.clip(target_local, 0, vocab_rows - 1)[..., None], axis=-1
    )[..., 0]
    picked_local = jnp.where(has_target, picked_local, 0.0)
    top_all, total_all, picked_all = wide_joined_2(
        (top_local, total_local, picked_local), "seq", wide_merge_stats
    )
    log_total = top_all + jnp.log(total_all)
    my_lengths = lax.dynamic_slice_in_dim(lengths, group_rank * clip_count, clip_count)
    my_present = lax.dynamic_slice_in_dim(present, group_rank * clip_count, clip_count)
    valid = ((jnp.arange(LEN)[None, :] < my_lengths[:, None]) & (my_present[:, None] > 0)).astype(
        jnp.float32
    )
    token_total = jnp.sum((lengths * present).astype(jnp.float32))
    token_loss = (log_total - picked_all) * valid
    loss_part = jnp.sum(lax.dynamic_slice_in_dim(token_loss, dec_first, dec_rows, 1))
    row_weight = valid / token_total
    onehot = (jnp.arange(vocab_rows)[None, None, :] == target_local[..., None]).astype(jnp.float32)
    grad_logits = (
        (jnp.exp(logits - log_total[..., None]) - onehot) * row_weight[..., None]
    ).astype(jnp.bfloat16)
    grad_states_all = wide_times_back(grad_logits, table_local)
    grad_table = wide_over_rows(all_states, grad_logits)
    grad_states = lax.psum_scatter(
        grad_states_all.astype(jnp.bfloat16), "seq", scatter_dimension=1, tiled=True
    ).astype(jnp.float32)
    grad_x3, grad_g6, grad_s6 = norm_back(grad_states, x_dec3, gains[6], shifts[6])
    grad_x2, grad_dec_up, grad_dec_bup, grad_dec_down, grad_b10, grad_g5, grad_s5 = wide_mlp_backward(
        grad_x3, x_dec2, gains[5], shifts[5], h_dec3, up_dec, act_dec, dec_wup, dec_wdown
    )
    grad_branch = grad_x2.astype(jnp.bfloat16)
    grad_cross_wout = wide_over_rows(o_cross, grad_branch)
    grad_b9 = wide_column_sum(grad_branch)
    grad_mixed = wide_times_back(grad_branch, cross_wout).astype(jnp.bfloat16)
    grad_qc, grad_kc, grad_vc = wide_attend_backward(
        grad_mixed, q_cross, keys_cross, vals_cross, lse_cross, None
    )
    grad_qc = grad_qc.astype(jnp.bfloat16)
    grad_cross_wq = wide_over_rows(h_dec2, grad_qc)
    grad_b7 = wide_column_sum(grad_qc)
    grad_in, grad_g4, grad_s4 = norm_back(
        wide_times_back(grad_qc, cross_wq), x_dec1, gains[4], shifts[4]
    )
    grad_x1 = grad_x2 + grad_in
    grad_branch = grad_x1.astype(jnp.bfloat16)
    grad_dec_wout = wide_over_rows(o_dec, grad_branch)
    grad_b6 = wide_column_sum(grad_branch)
    grad_mixed = wide_times_back(grad_branch, dec_wout).astype(jnp.bfloat16)
    grad_qd, grad_kd, grad_vd = wide_attend_backward(
        grad_mixed, q_dec, keys_dec, vals_dec, lse_dec, dec_first
    )
    grad_kd, grad_vd, grad_kc, grad_vc = (
        lax.psum_scatter(
            grad_kd.astype(jnp.bfloat16), "seq", scatter_dimension=1, tiled=True
        ).astype(jnp.float32),
        lax.psum_scatter(
            grad_vd.astype(jnp.bfloat16), "seq", scatter_dimension=1, tiled=True
        ).astype(jnp.float32),
        lax.psum_scatter(
            grad_kc.astype(jnp.bfloat16), "seq", scatter_dimension=1, tiled=True
        ).astype(jnp.float32),
        lax.psum_scatter(
            grad_vc.astype(jnp.bfloat16), "seq", scatter_dimension=1, tiled=True
        ).astype(jnp.float32),
    )
    grad_qd = grad_qd.astype(jnp.bfloat16)
    grad_vd = grad_vd.astype(jnp.bfloat16)
    grad_packed = jnp.concatenate([grad_qd, grad_kd.astype(jnp.bfloat16), grad_vd], axis=-1)
    grad_dec_qkv = wide_over_rows(h_dec1, grad_packed)
    grad_b4 = wide_column_sum(grad_qd)
    grad_b5 = wide_column_sum(grad_vd)
    grad_in, grad_g3, grad_s3 = norm_back(
        wide_times_back(grad_packed, dec_qkv), x_dec0, gains[3], shifts[3]
    )
    grad_x0 = grad_x1 + grad_in
    grad_positions = lax.dynamic_update_slice_in_dim(
        jnp.zeros((LEN, D), jnp.float32), jnp.sum(grad_x0, axis=0), dec_first, 0
    )
    grad_embed_all = lax.all_gather(grad_x0.astype(jnp.bfloat16), "seq", axis=1, tiled=True).astype(
        grad_x0.dtype
    )
    grad_embed_all = jnp.where(inside.reshape(-1)[:, None], grad_embed_all.reshape(-1, D), 0.0)
    grad_table = grad_table.at[:, safe_ids].add(grad_embed_all.T)
    grad_vc = grad_vc.astype(jnp.bfloat16)
    grad_pair = jnp.concatenate([grad_kc.astype(jnp.bfloat16), grad_vc], axis=-1)
    grad_cross_wkv = wide_over_rows(enc_out, grad_pair)
    grad_b8 = wide_column_sum(grad_vc)
    grad_enc2, grad_g2, grad_s2 = norm_back(
        wide_times_back(grad_pair, cross_wkv), x_enc2, gains[2], shifts[2]
    )
    device_count = lax.axis_size(("grp", "seq"))
    dec_flat = jnp.concatenate(
        [
            grad_dec_qkv.reshape(-1),
            grad_dec_wout.reshape(-1),
            grad_cross_wq.reshape(-1),
            grad_cross_wkv.reshape(-1),
            grad_cross_wout.reshape(-1),
            grad_dec_up.reshape(-1),
            grad_dec_down.reshape(-1),
        ]
    )
    dec_matrix = dec_flat.reshape(device_count, -1)
    dec_columns = dec_matrix.shape[1]
    grad_enc1, grad_enc_up, grad_enc_bup, grad_enc_down, grad_b3, grad_g1, grad_s1 = wide_mlp_backward(
        grad_enc2, x_enc1, gains[1], shifts[1], h_enc2, up_enc, act_enc, enc_wup, enc_wdown
    )
    grad_branch = grad_enc1.astype(jnp.bfloat16)
    grad_enc_wout = wide_over_rows(o_enc, grad_branch)
    grad_b2 = wide_column_sum(grad_branch)
    grad_mixed = wide_times_back(grad_branch, enc_wout).astype(jnp.bfloat16)
    grad_qe, grad_ke, grad_ve = wide_attend_backward(
        grad_mixed, q_enc, keys_enc, vals_enc, lse_enc, None
    )
    grad_ke, grad_ve = (
        lax.psum_scatter(
            grad_ke.astype(jnp.bfloat16), "seq", scatter_dimension=1, tiled=True
        ).astype(jnp.float32),
        lax.psum_scatter(
            grad_ve.astype(jnp.bfloat16), "seq", scatter_dimension=1, tiled=True
        ).astype(jnp.float32),
    )
    grad_qe = grad_qe.astype(jnp.bfloat16)
    grad_ve = grad_ve.astype(jnp.bfloat16)
    grad_packed = jnp.concatenate([grad_qe, grad_ke.astype(jnp.bfloat16), grad_ve], axis=-1)
    grad_enc_qkv = wide_over_rows(h_enc1, grad_packed)
    grad_b0 = wide_column_sum(grad_qe)
    grad_b1 = wide_column_sum(grad_ve)
    _, grad_g0, grad_s0 = norm_back(
        wide_times_back(grad_packed, enc_qkv), x_enc0, gains[0], shifts[0]
    )
    grad_gains = jnp.stack([grad_g0, grad_g1, grad_g2, grad_g3, grad_g4, grad_g5, grad_g6])
    grad_shifts = jnp.stack([grad_s0, grad_s1, grad_s2, grad_s3, grad_s4, grad_s5, grad_s6])
    grad_biases = jnp.stack(
        [
            grad_b0,
            grad_b1,
            grad_b2,
            grad_b3,
            grad_b4,
            grad_b5,
            grad_b6,
            grad_b7,
            grad_b8,
            grad_b9,
            grad_b10,
        ]
    )
    grad_up_bias = jnp.stack([grad_enc_bup, grad_dec_bup])
    enc_flat = jnp.concatenate(
        [
            grad_enc_qkv.reshape(-1),
            grad_enc_wout.reshape(-1),
            grad_enc_up.reshape(-1),
            grad_enc_down.reshape(-1),
            grad_positions.reshape(-1),
            grad_gains.reshape(-1),
            grad_shifts.reshape(-1),
            grad_biases.reshape(-1),
            grad_up_bias.reshape(-1),
        ]
    )
    enc_matrix = enc_flat.reshape(device_count, -1)
    joined = wide_spread_grads(jnp.concatenate([dec_matrix, enc_matrix], axis=1))
    dec_grad = joined[:, :dec_columns].reshape(-1)
    enc_grad = joined[:, dec_columns:].reshape(-1)
    table_grad = lax.psum_scatter(grad_table, "grp", scatter_dimension=0, tiled=True)
    squares = (
        jnp.sum(enc_grad * enc_grad)
        + jnp.sum(dec_grad * dec_grad)
        + jnp.sum(table_grad * table_grad)
    )
    loss_sum, square_sum = lax.psum((loss_part, squares), ("grp", "seq"))
    mean_loss = loss_sum / token_total
    grad_norm = jnp.sqrt(square_sum)
    factor = jnp.minimum(1.0, clip_limit / (grad_norm + 1e-06))
    steps_done = step_count[0].astype(jnp.float32)
    bias_one = 1.0 - beta_one**steps_done
    bias_two = 1.0 - beta_two**steps_done
    enc_new = adamw(enc_params, enc_moment, enc_second, enc_grad, factor, bias_one, bias_two)
    dec_new = adamw(dec_params, dec_moment, dec_second, dec_grad, factor, bias_one, bias_two)
    table_new = adamw(
        table_params, table_moment, table_second, table_grad, factor, bias_one, bias_two
    )
    return (
        mean_loss,
        grad_norm,
        enc_new[0],
        enc_new[1],
        enc_new[2],
        dec_new[0],
        dec_new[1],
        dec_new[2],
        table_new[0],
        table_new[1],
        table_new[2],
    )


def solution(mesh):
    flat = P(("grp", "seq"))
    both = P("grp", "seq")
    in_specs = (
        P("grp", "seq", None),
        P("grp", None),
        P("grp", None),
        P(),
        P(),
        P(),
        flat,
        flat,
        flat,
        flat,
        flat,
        flat,
        both,
        both,
        both,
    )
    out_specs = (P(), P(), flat, flat, flat, flat, flat, flat, both, both, both)
    few = mesh.shape["grp"] == 8
    return jax.shard_map(
        on_device if few else wide_on_device,
        mesh=mesh,
        in_specs=in_specs,
        out_specs=out_specs,
        check_vma=False,
    )
```

```python
from functools import partial
import math

import jax
import jax.numpy as jnp
from jax import lax
from jax.experimental import pallas as pl
from jax.experimental.pallas import tpu as pltpu
from jax.sharding import PartitionSpec as P


D = 512
HEADS = 8
F = 2048
LEN = 448
HEAD = D // HEADS
LANES = 128


beta_one = 0.9
beta_two = 0.999
rate = 0.01
decay = 0.1
adam_eps = 1e-08
clip_limit = 1.0
norm_eps = 1e-05
masked_score = -1e30

bf16 = jnp.bfloat16
f32 = jnp.float32


def layer_norm(values, norm_gain, norm_shift):
    center = values - jnp.mean(values, axis=-1, keepdims=True)
    spread = jnp.mean(center * center, axis=-1, keepdims=True)
    return center * lax.rsqrt(spread + norm_eps) * norm_gain + norm_shift


def norm_back(grad_out, values, norm_gain, norm_shift):
    _, pullback = jax.vjp(layer_norm, values, norm_gain, norm_shift)
    return pullback(grad_out)


def enc_layout():
    return [(D, 3 * D), (D, D), (D, F), (F, D), (LEN, D), (7, D), (7, D), (11, D), (2, F)]


def dec_layout():
    return [(D, 3 * D), (D, D), (D, D), (D, 2 * D), (D, D), (D, F), (F, D)]


def split_flat(flat_vec, layout):
    pieces = []
    offset = 0
    for matrix_dims in layout:
        amount = matrix_dims[0] * matrix_dims[1]
        pieces.append(flat_vec[offset : offset + amount].reshape(matrix_dims))
        offset += amount
    return pieces


def times(left_side, right_side):
    return jnp.dot(left_side, right_side, preferred_element_type=f32)


def times_back(left_side, right_side):
    return lax.dot_general(
        left_side, right_side, (((1,), (1,)), ((), ())), preferred_element_type=f32
    )


def over_rows(left_side, right_side):
    return lax.dot_general(
        left_side, right_side, (((0,), (0,)), ((), ())), preferred_element_type=f32
    )


def column_sum(values):
    return jnp.sum(values.astype(f32), axis=0)


def swap(value, axis, mask):
    count = lax.axis_size(axis)
    return lax.ppermute(value, axis, [(i, i ^ mask) for i in range(count)])


def reorder(items, rank):
    items = list(items)
    bit = 1
    while bit < len(items):
        odd = (rank & bit) != 0
        items = [jnp.where(odd, items[k ^ bit], items[k]) for k in range(len(items))]
        bit *= 2
    return items


def tree_join(items, join):
    items = list(items)
    while len(items) > 1:
        items = [join(items[k], items[k + 1]) for k in range(0, len(items), 2)]
    return items[0]


def pair_join(value, axis, join):
    for bit in bits_of(axis):
        value = join(value, swap(value, axis, bit))
    return value


def all_join(value, axis, join):
    count = lax.axis_size(axis)
    return tree_join([value] + [swap(value, axis, k) for k in range(1, count)], join)


def gather_near(value, axis):
    return [value] + [swap(value, axis, k) for k in range(1, lax.axis_size(axis))]


def trade_near(items, axis):
    return [items[0]] + [swap(items[k], axis, k) for k in range(1, len(items))]


def bits_of(axis):
    count = lax.axis_size(axis)
    found = []
    bit = 1
    while bit < count:
        found.append(bit)
        bit *= 2
    return found


def group_orders():
    far = bits_of("grp")[1:]
    return far, far[::-1]


def grow(slots, bit):
    held = sorted(slots)
    sent = jnp.stack([slots[k] for k in held])
    came = swap(sent, "grp", bit)
    for place, k in enumerate(held):
        slots[k ^ bit] = came[place]
    return slots


def gather_group(value):
    half = value.shape[0] // 2
    parts = [value[:half], value[half:]]
    results = []
    for part, order in zip(parts, group_orders()):
        slots = {0: part}
        for bit in order + [1]:
            slots = grow(slots, bit)
        results.append(slots)
    count = lax.axis_size("grp")
    return jnp.stack([jnp.concatenate([r[k] for r in results]) for k in range(count)])


def reduce_group(even, odd, wire, hold=f32):
    count = lax.axis_size("grp")
    came = swap(odd.astype(wire), "grp", 1)
    held = {k: even[k // 2].astype(hold) + came[k // 2].astype(hold) for k in range(0, count, 2)}
    half = even.shape[1] // 2
    results = []
    for low, order in zip((0, half), group_orders()):
        part = {k: v[low : low + half] for k, v in held.items()}
        for bit in order:
            gone = [k for k in sorted(part) if k & bit]
            came = swap(jnp.stack([part[k] for k in gone]).astype(wire), "grp", bit)
            part = {
                k: v + came[gone.index(k ^ bit)].astype(hold)
                for k, v in part.items()
                if not k & bit
            }
        results.append(part[0])
    return jnp.concatenate(results)


def gather_near_lines(block):
    half = block.shape[0] // 2
    near = gather_near(block, "seq")
    return [jnp.stack([piece[low : low + half] for piece in near])[None] for low in (0, half)]


def gather_far_lines(parts, stage):
    return [
        jnp.concatenate([part, swap(part, "grp", order[stage])])
        for part, order in zip(parts, group_orders())
    ]


def lay_out_kernel(shapes, block, rank_ref, own_a, own_b, came_a, came_b, *refs):
    outs, (lines, wide, sems) = refs[: len(shapes)], refs[len(shapes) :]
    half = block // 2
    rank = rank_ref[0]

    def copies(index, start):
        slot = index ^ rank
        far_z = slot & 3
        mate = (slot >> 2) & 1
        far_x = (slot >> 3) & 1
        far_y = (slot >> 4) & 1
        for side, place, own_ref, came_ref in (
            (0, 2 * far_y + far_x, own_a, came_a),
            (1, 2 * far_x + far_y, own_b, came_b),
        ):
            target = lines.at[pl.ds(index * block + side * half, half), :]
            sem = sems.at[2 * index + side]
            if not start:
                pltpu.make_async_copy(own_ref.at[0, 0], target, sem).wait()
                continue

            @pl.when(mate == 0)
            def _():
                pltpu.make_async_copy(own_ref.at[place, far_z], target, sem).start()

            @pl.when(mate == 1)
            def _():
                pltpu.make_async_copy(came_ref.at[place, far_z], target, sem).start()

    lax.fori_loop(0, 32, lambda index, carry: (copies(index, True), carry)[1], 0)
    lax.fori_loop(0, 32, lambda index, carry: (copies(index, False), carry)[1], 0)
    first = 0
    for out, (height, across) in zip(outs, shapes):
        step = 64
        while height % step:
            step //= 2
        if across == 1:
            out[...] = lines[first : first + height, :]
        else:

            def unfold(index, carry, out=out, across=across, step=step, first=first):
                count = step * across
                start = pl.multiple_of(first + index * count, 16)
                wide[pl.ds(0, count), :] = lines[pl.ds(start, count), :].astype(f32)
                low = pl.multiple_of(index * step, step)
                for column in range(across):
                    out[pl.ds(low, step), column * LANES : (column + 1) * LANES] = wide[
                        pl.ds(column, step, stride=across), :
                    ].astype(bf16)
                return carry

            lax.fori_loop(0, height // step, unfold, 0)
        first += height * across


def lay_out(held, came, shapes, rank):
    block = 2 * held[0].shape[2]
    total = 8 * block * held[0].shape[1]
    vmem = pl.BlockSpec(memory_space=pltpu.VMEM)
    hbm = pl.BlockSpec(memory_space=pl.ANY)
    return pl.pallas_call(
        partial(lay_out_kernel, shapes, block),
        out_shape=[jax.ShapeDtypeStruct((h, a * LANES), bf16) for h, a in shapes],
        in_specs=[pl.BlockSpec(memory_space=pltpu.SMEM)] + [hbm] * 4,
        out_specs=[vmem] * len(shapes),
        scratch_shapes=[
            pltpu.VMEM((total, LANES), bf16),
            pltpu.VMEM((64 * 16, LANES), f32),
            pltpu.SemaphoreType.DMA((64,)),
        ],
        name="lay_out",
    )(rank.reshape(1), *held, *came)


def write_lines(buffer, left, right, total, first, step, own=None):
    tall, height = left.shape
    across = (right.shape[1] if own is None else 3 * D) // LANES
    rows = step * across
    assert first % rows == 0 and height % step == 0

    def kernel(*refs):
        left_ref, right_ref, out_ref = refs[0], refs[1], refs[-1]
        got = lax.dot_general(
            left_ref[...], right_ref[...], (((0,), (0,)), ((), ())), preferred_element_type=f32
        )
        for column in range(across):
            if own is None:
                piece = got[:, column * LANES : (column + 1) * LANES]
            else:
                per = D // LANES
                source = column // per
                piece = jnp.where(
                    refs[2][0] == column % per, got[:, source * LANES : (source + 1) * LANES], 0.0
                )
            out_ref[pl.ds(column, step, stride=across), :] = piece

    specs = [
        pl.BlockSpec((tall, step), lambda i: (0, i)),
        pl.BlockSpec(right.shape, lambda i: (0, 0)),
    ]
    args = [left, right]
    if own is not None:
        specs.append(pl.BlockSpec(memory_space=pltpu.SMEM))
        args.append(own.reshape(1))
    aliases = {}
    if buffer is not None:
        specs.append(pl.BlockSpec(memory_space=pl.ANY))
        aliases = {len(args): 0}
        args.append(buffer)
    return pl.pallas_call(
        kernel,
        grid=(height // step,),
        in_specs=specs,
        out_specs=pl.BlockSpec((rows, LANES), lambda i: (first // rows + i, 0)),
        out_shape=jax.ShapeDtypeStruct((total, LANES), f32),
        input_output_aliases=aliases,
        name="write_lines",
    )(*args)


def write_rest(buffer, matrix, rest, first):
    height = matrix.shape[0]
    across = D // LANES
    rows = height * across + rest.shape[0]

    def kernel(matrix_ref, rest_ref, buffer_ref, out_ref):
        for column in range(across):
            out_ref[pl.ds(column, height, stride=across), :] = matrix_ref[
                :, column * LANES : (column + 1) * LANES
            ]
        out_ref[height * across :, :] = rest_ref[...]

    return pl.pallas_call(
        kernel,
        grid=(1,),
        in_specs=[
            pl.BlockSpec(matrix.shape, lambda i: (0, 0)),
            pl.BlockSpec(rest.shape, lambda i: (0, 0)),
            pl.BlockSpec(memory_space=pl.ANY),
        ],
        out_specs=pl.BlockSpec((rows, LANES), lambda i: (first // rows, 0)),
        out_shape=jax.ShapeDtypeStruct(buffer.shape, f32),
        input_output_aliases={2: 0},
        name="write_rest",
    )(matrix, rest, buffer)


def reduce_blocks(blocks, pick):
    group_rank = lax.axis_index("grp")
    rest = blocks.shape[2:]
    blocks = blocks.reshape((4, 2) + blocks.shape[1:])
    mine = group_rank & 1

    def entry(core):
        zero = jnp.int32(0)
        start = (zero, core, pick) + (zero,) * len(rest)
        return lax.dynamic_slice(blocks, start, (4, 1, 1) + rest).reshape((2, 2) + rest)

    def step(value, place, bit):
        mine = (group_rank & bit) // bit
        sent = lax.dynamic_slice_in_dim(value, 1 - mine, 1, place)
        kept = lax.dynamic_slice_in_dim(value, mine, 1, place)
        return kept + swap(sent, "grp", bit)

    blocks = entry(mine) + swap(entry(1 - mine), "grp", 1)
    half = rest[-2] // 2
    results = []
    for low, order in zip((0, half), group_orders()):
        part = lax.slice_in_dim(blocks, low, low + half, axis=blocks.ndim - 2)
        for bit in order:
            part = step(part, 0 if bit == 4 else 1, bit)
        results.append(part.reshape(rest[:-2] + (half, LANES)))
    return jnp.concatenate(results, axis=-2)


def scatter_near(items, axis, wire):
    came = [swap(items[k].astype(wire), axis, k).astype(f32) for k in range(1, len(items))]
    return tree_join([items[0].astype(f32)] + came, jnp.add)


def head_scores(query_ref, key_ref, bias_ref, head, causal):
    query = query_ref[...]
    lane = lax.broadcasted_iota(jnp.int32, query.shape, 1)
    query = jnp.where(lane // HEAD == head, query * jnp.bfloat16(HEAD ** (-0.5)), jnp.bfloat16(0))
    scores = times_back(key_ref[...], query)
    if causal:
        key_at = lax.broadcasted_iota(jnp.int32, scores.shape, 0)
        query_at = lax.broadcasted_iota(jnp.int32, scores.shape, 1)
        return query, jnp.where(query_at >= key_at, scores, masked_score)
    return query, scores + bias_ref[...]


def head_rows(parts):
    row = lax.broadcasted_iota(jnp.int32, parts[0].shape, 0)
    joined = parts[-1]
    for head in range(len(parts) - 2, -1, -1):
        joined = jnp.where(row < (head + 1) * HEAD, parts[head], joined)
    return joined.T


def attend_forward_kernel(causal, query_ref, key_ref, value_ref, bias_ref, out_ref, total_ref):
    parts = []
    for head in range(query_ref.shape[1] // HEAD):
        _, scores = head_scores(query_ref, key_ref, bias_ref, head, causal)
        highest = jnp.max(scores, axis=0, keepdims=True)
        weights = jnp.exp(scores - highest)
        total = jnp.sum(weights, axis=0, keepdims=True)
        weights = (weights * (1.0 / total)).astype(bf16)
        parts.append(over_rows(value_ref[...], weights))
        total_ref[head : head + 1, :] = highest + jnp.log(total)
    out_ref[...] = head_rows(parts).astype(bf16)


def query_tile(rows):
    return 256 if rows % 256 == 0 else rows


def attend_forward(query, keys, values, bias, causal=False):
    rows, wide = query.shape
    tile = query_tile(rows)
    whole = pl.BlockSpec(keys.shape, lambda i: (0, 0))
    return pl.pallas_call(
        partial(attend_forward_kernel, causal),
        grid=(rows // tile,),
        in_specs=[
            pl.BlockSpec((tile, wide), lambda i: (i, 0)),
            whole,
            whole,
            pl.BlockSpec(bias.shape, lambda i: (0, 0)),
        ],
        out_specs=[
            pl.BlockSpec((tile, wide), lambda i: (i, 0)),
            pl.BlockSpec((wide // HEAD, tile), lambda i: (0, i)),
        ],
        out_shape=[
            jax.ShapeDtypeStruct((rows, wide), bf16),
            jax.ShapeDtypeStruct((wide // HEAD, rows), f32),
        ],
        name="attend_forward",
    )(query, keys, values, bias)


def attend_backward_kernel(
    causal,
    grad_ref,
    query_ref,
    key_ref,
    value_ref,
    total_ref,
    bias_ref,
    grad_query_ref,
    grad_key_ref,
    grad_value_ref,
    key_sum,
    value_sum,
):
    @pl.when(pl.program_id(0) == 0)
    def _():
        key_sum[...] = jnp.zeros_like(key_sum)
        value_sum[...] = jnp.zeros_like(value_sum)

    grad = grad_ref[...]
    lane = lax.broadcasted_iota(jnp.int32, grad.shape, 1)
    parts = []
    for head in range(grad.shape[1] // HEAD):
        query, scores = head_scores(query_ref, key_ref, bias_ref, head, causal)
        weights = jnp.exp(scores - total_ref[head : head + 1, :])
        grad_head = jnp.where(lane // HEAD == head, grad, jnp.bfloat16(0))
        grad_weights = times_back(value_ref[...], grad_head)
        inner = jnp.sum(weights * grad_weights, axis=0, keepdims=True)
        grad_scores = (weights * (grad_weights - inner)).astype(bf16)
        value_sum[...] += times(weights.astype(bf16), grad_head)
        key_sum[...] += times(grad_scores, query)
        parts.append(over_rows(key_ref[...], grad_scores))
    grad_query_ref[...] = (head_rows(parts) * HEAD ** (-0.5)).astype(bf16)

    @pl.when(pl.program_id(0) == pl.num_programs(0) - 1)
    def _():
        grad_key_ref[...] = key_sum[...].astype(bf16)
        grad_value_ref[...] = value_sum[...].astype(bf16)


def attend_backward(grad_mixed, query, keys, values, log_total, bias, causal=False):
    rows, wide = query.shape
    tile = query_tile(rows)
    some = pl.BlockSpec((tile, wide), lambda i: (i, 0))
    whole = pl.BlockSpec(keys.shape, lambda i: (0, 0))
    return pl.pallas_call(
        partial(attend_backward_kernel, causal),
        grid=(rows // tile,),
        in_specs=[
            some,
            some,
            whole,
            whole,
            pl.BlockSpec((wide // HEAD, tile), lambda i: (0, i)),
            pl.BlockSpec(bias.shape, lambda i: (0, 0)),
        ],
        out_specs=[some, whole, whole],
        out_shape=[
            jax.ShapeDtypeStruct((rows, wide), bf16),
            jax.ShapeDtypeStruct(keys.shape, bf16),
            jax.ShapeDtypeStruct(keys.shape, bf16),
        ],
        scratch_shapes=[pltpu.VMEM(keys.shape, f32), pltpu.VMEM(keys.shape, f32)],
        name="attend_backward",
    )(grad_mixed, query, keys, values, log_total, bias)


def stand_up(rows):
    blank = jnp.zeros((LANES - rows.shape[0], rows.shape[1]), rows.dtype)
    return jnp.concatenate([rows, blank]).T


def row_parts(rows):
    step = rows // 4 if rows % 64 == 0 else rows
    return [(low, low + step) for low in range(0, rows, step)]


def loss_forward_kernel(last, rank_ref, here_ref, states_ref, table_ref, target_ref, out_ref):
    target = stand_up(jnp.broadcast_to(target_ref[0].astype(f32), (8, target_ref.shape[2])))
    target = target[:, 0:1].astype(jnp.int32)

    def part_of(columns, short, low, high):
        logits = times(states_ref[0, low:high], table_ref[:, :columns])
        column = lax.broadcasted_iota(jnp.int32, logits.shape, 1)
        if short:
            logits = jnp.where(column < here_ref[0], logits, masked_score)
        highest = jnp.max(logits, axis=1, keepdims=True)
        total = jnp.sum(jnp.exp(logits - highest), axis=1, keepdims=True)
        picked = jnp.sum(jnp.where(column == target[low:high], logits, 0.0), axis=1, keepdims=True)
        lane = lax.broadcasted_iota(jnp.int32, (high - low, LANES), 1)
        return jnp.where(lane == 0, highest, jnp.where(lane == 1, total, picked))

    def work(columns, short):
        packed = [part_of(columns, short, low, high) for low, high in row_parts(states_ref.shape[1])]
        out_ref[0] = jnp.concatenate(packed).T[:8]

    width = table_ref.shape[1]

    @pl.when(here_ref[0] == width)
    def _():
        work(width, False)

    @pl.when(here_ref[0] != width)
    def _():
        work(round_up(last, LANES), True)


def loss_forward(states, table, targets, here, rank, last):
    count, tile, deep = states.shape
    return pl.pallas_call(
        partial(loss_forward_kernel, last),
        grid_spec=pltpu.PrefetchScalarGridSpec(
            num_scalar_prefetch=2,
            grid=(count,),
            in_specs=[
                pl.BlockSpec((1, tile, deep), lambda i, rank, here: (i, 0, 0)),
                pl.BlockSpec(table.shape, lambda i, rank, here: (0, 0)),
                pl.BlockSpec((1, 1, tile), lambda i, rank, here: (i, 0, 0)),
            ],
            out_specs=pl.BlockSpec((1, 8, tile), lambda i, rank, here: (i ^ rank[0], 0, 0)),
        ),
        out_shape=jax.ShapeDtypeStruct((count, 8, tile), f32),
        name="loss_forward",
    )(rank.reshape(1), here.reshape(1), states, table, targets)


def join_stats_kernel(*refs):
    parts, out_ref = [ref[...] for ref in refs[:-1]], refs[-1]
    while len(parts) > 1:
        pairs = []
        for first, second in zip(parts[::2], parts[1::2]):
            biggest = jnp.maximum(first[:, 0:1], second[:, 0:1])
            summed = first[:, 1:2] * jnp.exp(first[:, 0:1] - biggest) + second[:, 1:2] * jnp.exp(
                second[:, 0:1] - biggest
            )
            picked = first[:, 2:3] + second[:, 2:3]
            pairs.append(jnp.concatenate([biggest, summed, picked, first[:, 3:]], axis=1))
        parts = pairs
    out_ref[...] = parts[0]


def join_stats(parts):
    vmem = pl.BlockSpec(memory_space=pltpu.VMEM)
    return pl.pallas_call(
        join_stats_kernel,
        in_specs=[vmem] * len(parts),
        out_specs=vmem,
        out_shape=jax.ShapeDtypeStruct(parts[0].shape, f32),
        name="join_stats",
    )(*parts)


def loss_backward_kernel(
    last,
    rank_ref,
    here_ref,
    states_ref,
    table_ref,
    target_ref,
    scale_ref,
    grad_ref,
    kept_ref,
    sent_ref,
):
    target = stand_up(jnp.broadcast_to(target_ref[0].astype(f32), (8, target_ref.shape[2])))
    target = target[:, 0:1].astype(jnp.int32)
    scale = stand_up(scale_ref[0])

    odd = pl.program_id(0) % 2

    def part_of(columns, short, low, high):
        logits = times(states_ref[0, low:high], table_ref[:, :columns])
        column = lax.broadcasted_iota(jnp.int32, logits.shape, 1)
        soft = jnp.exp(logits - scale[low:high, 0:1])
        grad = jnp.where(column == target[low:high], soft - 1.0, soft) * scale[low:high, 1:2]
        if short:
            grad = jnp.where(column < here_ref[0], grad, 0.0)
        grad = grad.astype(bf16)
        grad_ref[0, low:high, :columns] = grad
        if columns < grad_ref.shape[2]:
            grad_ref[0, low:high, columns:] = jnp.zeros(
                (high - low, grad_ref.shape[2] - columns), bf16
            )
        return times_back(grad, table_ref[:, :columns])

    def work(columns, short):
        parts = [(0, states_ref.shape[1])]
        grads = [part_of(columns, short, low, high) for low, high in parts]

        @pl.when(odd == 0)
        def _():
            for (low, high), grad in zip(parts, grads):
                kept_ref[0, low:high] = grad

        @pl.when(odd == 1)
        def _():
            for (low, high), grad in zip(parts, grads):
                sent_ref[0, low:high] = grad.astype(bf16)

    width = table_ref.shape[1]

    @pl.when(here_ref[0] == width)
    def _():
        work(width, False)

    @pl.when(here_ref[0] != width)
    def _():
        work(round_up(last, LANES), True)


def loss_backward(states, table, targets, scales, here, rank, last):
    count, tile, deep = states.shape
    width = table.shape[1]
    return pl.pallas_call(
        partial(loss_backward_kernel, last),
        grid_spec=pltpu.PrefetchScalarGridSpec(
            num_scalar_prefetch=2,
            grid=(count,),
            in_specs=[
                pl.BlockSpec((1, tile, deep), lambda i, rank, here: (i, 0, 0)),
                pl.BlockSpec(table.shape, lambda i, rank, here: (0, 0)),
                pl.BlockSpec((1, 1, tile), lambda i, rank, here: (i, 0, 0)),
                pl.BlockSpec((1, 2, tile), lambda i, rank, here: (i ^ rank[0], 0, 0)),
            ],
            out_specs=[
                pl.BlockSpec((1, tile, width), lambda i, rank, here: (i, 0, 0)),
                pl.BlockSpec((1, tile, deep), lambda i, rank, here: (i // 2, 0, 0)),
                pl.BlockSpec((1, tile, deep), lambda i, rank, here: (i // 2, 0, 0)),
            ],
        ),
        out_shape=[
            jax.ShapeDtypeStruct((count, tile, width), bf16),
            jax.ShapeDtypeStruct((count // 2, tile, deep), f32),
            jax.ShapeDtypeStruct((count // 2, tile, deep), bf16),
        ],
        name="loss_backward",
    )(rank.reshape(1), here.reshape(1), states, table, targets, scales)


def own_blocks_kernel(pieces, lines, rank_ref, *refs):
    out_ref, stage = refs[-2], refs[-1]
    count = out_ref.shape[0]

    def branch(seq_rank):
        for place in range(count):
            low = (4 * place + seq_rank) * lines
            for first, left, right in pieces:
                left_ref, right_ref = refs[left], refs[right]
                across = right_ref.shape[1] // LANES
                last = first + left_ref.shape[1] * across
                if not first <= low < last:
                    continue
                top = (low - first) // across
                bottom = -(-(low + lines - first) // across)
                skip = low - first - top * across
                got = lax.dot_general(
                    left_ref[:, top:bottom],
                    right_ref[...],
                    (((0,), (0,)), ((), ())),
                    preferred_element_type=f32,
                )
                target = stage if (bottom - top) * across != lines else out_ref.at[place]
                for column in range(across):
                    target[pl.ds(column, bottom - top, stride=across), :] = got[
                        :, column * LANES : (column + 1) * LANES
                    ]
                if target is stage:
                    out_ref[place] = stage[skip : skip + lines, :]

    for seq_rank in range(4):

        @pl.when(rank_ref[0] == seq_rank)
        def _(seq_rank=seq_rank):
            branch(seq_rank)


def own_blocks(pairs, firsts, lines, count, seq_rank):
    vmem = pl.BlockSpec(memory_space=pltpu.VMEM)
    args = [value for pair in pairs for value in pair]
    pieces = [(first, 2 * k, 2 * k + 1) for k, first in enumerate(firsts)]
    return pl.pallas_call(
        partial(own_blocks_kernel, pieces, lines),
        in_specs=[pl.BlockSpec(memory_space=pltpu.SMEM)] + [vmem] * len(args),
        out_specs=vmem,
        out_shape=jax.ShapeDtypeStruct((count, lines, LANES), f32),
        scratch_shapes=[pltpu.VMEM((lines + 64, LANES), f32)],
        name="own_blocks",
    )(seq_rank.reshape(1), *args)


def mlp_forward(stream, norm_gain, norm_shift, w_up, b_up, w_down, b_down):
    normed = layer_norm(stream, norm_gain, norm_shift).astype(bf16)
    raised = times(normed, w_up) + b_up
    active = jax.nn.gelu(raised, approximate=False).astype(bf16)
    return (stream + times(active, w_down) + b_down, normed, raised, active)


def mlp_backward(grad_stream, stream, norm_gain, norm_shift, raised, w_up, w_down):
    grad_branch = grad_stream.astype(bf16)
    grad_bdown = column_sum(grad_branch)
    grad_active = times_back(grad_branch, w_down)
    _, gelu_pull = jax.vjp(partial(jax.nn.gelu, approximate=False), raised)
    grad_raised = gelu_pull(grad_active)[0].astype(bf16)
    grad_bup = column_sum(grad_raised)
    grad_normed = times_back(grad_raised, w_up)
    grad_in, grad_gain, grad_shift = norm_back(grad_normed, stream, norm_gain, norm_shift)
    return (
        grad_stream + grad_in,
        grad_branch,
        grad_raised,
        grad_bup,
        grad_bdown,
        grad_gain,
        grad_shift,
    )


def adamw(weight_now, moment, second, gradient, factor, bias_one, bias_two):
    scaled = gradient * factor
    new_moment = beta_one * moment + (1.0 - beta_one) * scaled
    new_second = beta_two * second + (1.0 - beta_two) * scaled * scaled
    step_size = (
        new_moment / bias_one / (jnp.sqrt(new_second / bias_two) + adam_eps) + decay * weight_now
    )
    return (weight_now - rate * step_size, new_moment, new_second)


def round_up(amount, unit):
    return -(-amount // unit) * unit


def on_device(*args):
    return train_step(*args)


def train_step(
    frames,
    input_ids,
    target_ids,
    lengths,
    present,
    step_count,
    enc_params,
    enc_moment,
    enc_second,
    dec_params,
    dec_moment,
    dec_second,
    table_params,
    table_moment,
    table_second,
):
    seq_size = lax.axis_size("seq")
    grp_size = lax.axis_size("grp")
    seq_rank = lax.axis_index("seq")
    group_rank = lax.axis_index("grp")
    lead = (seq_rank == 0).astype(f32)

    frame_rows = frames.shape[1]
    rows = round_up(frame_rows, 128)
    rank = group_rank * seq_size + seq_rank
    devices = grp_size * seq_size
    enc_count = enc_params.shape[0]
    enc_lines = round_up(enc_count, 64 * LANES) // LANES
    lag = enc_lines * LANES - enc_count
    enc_here = enc_params.astype(bf16)
    enc_next = lax.ppermute(
        enc_here[: lag * devices], ("grp", "seq"), [(i + 1, i) for i in range(devices - 1)]
    )
    enc_block = lax.dynamic_slice_in_dim(
        jnp.concatenate([enc_here, enc_next]), lag * rank, enc_lines * LANES
    ).reshape(enc_lines, LANES)
    dec_lines = dec_params.shape[0] // LANES
    enc_parts = gather_near_lines(enc_block)
    frame_slots = gather_near(jnp.pad(frames[0], ((0, rows - frame_rows), (0, 0))), "seq")
    dec_parts = gather_near_lines(dec_params.astype(bf16).reshape(dec_lines, LANES))
    enc_parts = gather_far_lines(enc_parts, 0)
    enc_parts = gather_far_lines(enc_parts, 1)
    enc_came = [swap(part, "grp", 1) for part in enc_parts]
    dec_parts = gather_far_lines(dec_parts, 0)
    dec_parts = gather_far_lines(dec_parts, 1)
    dec_came = [swap(part, "grp", 1) for part in dec_parts]
    vocab = table_params.shape[1]
    width = round_up(round_up(vocab, grp_size) // grp_size, 128)
    ids_here = jnp.concatenate([input_ids, target_ids])
    ids_rows = jnp.concatenate([ids_here >> 8, ids_here & 255]).astype(bf16).reshape(1, -1)
    spare = 16 * width - ids_rows.shape[1]
    ids_rows = jnp.pad(ids_rows, ((0, 0), (0, spare))).reshape(16, width)
    table_wide = jnp.concatenate(
        [
            jnp.pad(table_params.astype(bf16), ((0, 0), (0, width * grp_size - vocab))),
            jnp.tile(ids_rows, (1, grp_size)),
        ]
    )
    chans = D // grp_size
    table_came = trade_near(
        [
            lax.dynamic_slice_in_dim(table_wide, (group_rank ^ k) * width, width, 1)
            for k in range(grp_size)
        ],
        "grp",
    )
    table = jnp.concatenate(reorder([piece[:chans] for piece in table_came], group_rank))
    vocab_first = seq_rank * vocab + group_rank * width
    vocab_here = jnp.clip(vocab - group_rank * width, 0, width)
    ids_rows = round_up(4 * LEN, width) // width
    ids_slots = jnp.stack([piece[chans : chans + ids_rows] for piece in table_came])
    ids_slots = ids_slots.reshape(grp_size, -1)[:, : 4 * LEN].astype(jnp.int32)
    ids_slots = ids_slots.reshape(grp_size, 2, 2, LEN)
    ids_slots = ids_slots[:, 0] * 256 + ids_slots[:, 1]

    small = (7 + 7 + 11) * D + 2 * F
    enc_qkv, enc_wout, enc_wup, enc_wdown, positions, small_lines = lay_out(
        enc_parts,
        enc_came,
        [(h, w // LANES) for h, w in enc_layout()[:5]] + [(small // LANES, 1)],
        rank,
    )
    gains, shifts, biases, up_bias = split_flat(
        small_lines.astype(f32).reshape(-1), enc_layout()[5:]
    )
    positions = positions.astype(f32)
    span = D // seq_size

    def own(matrix, parts):
        return jnp.concatenate(
            [
                lax.dynamic_slice_in_dim(matrix, part * D + seq_rank * span, span, matrix.ndim - 1)
                for part in range(parts)
            ],
            axis=-1,
        )

    def own_bias(row):
        return lax.dynamic_slice_in_dim(biases[row], seq_rank * span, span, 0)

    half_width = D // 2
    stride = math.log(10000.0) / (half_width - 1)
    inverse = jnp.exp(-stride * jnp.arange(half_width, dtype=f32))
    x_slots = []
    for k in range(seq_size):
        offset = ((seq_rank ^ k) * frame_rows).astype(f32)
        angles = (jnp.arange(rows, dtype=f32) + offset)[:, None] * inverse[None, :]
        wave = jnp.concatenate([jnp.sin(angles), jnp.cos(angles)], axis=1)
        x_slots.append(frame_slots[k].astype(f32) + wave)
    x_all = jnp.concatenate(x_slots)
    x_enc0 = x_slots[0]
    h_enc1 = layer_norm(x_all, gains[0], shifts[0]).astype(bf16)
    own_enc_qkv = own(enc_qkv, 3)
    packed = times(h_enc1, own_enc_qkv)
    q_enc = (packed[:, :span] + own_bias(0)).astype(bf16)
    k_enc = packed[:, span : 2 * span].astype(bf16)
    v_enc = (packed[:, 2 * span :] + own_bias(1)).astype(bf16)
    frame_bias = jnp.where(jnp.arange(rows * seq_size) % rows < frame_rows, 0.0, masked_score)
    frame_bias = frame_bias.astype(f32)[:, None]
    o_own, lse_enc = attend_forward(q_enc, k_enc, v_enc, frame_bias)

    def to_rows(value):
        pieces = [value[k * rows : (k + 1) * rows] for k in range(seq_size)]
        return jnp.concatenate(reorder(trade_near(pieces, "seq"), seq_rank), axis=1)

    def to_heads(value):
        pieces = reorder([value[:, k * span : (k + 1) * span] for k in range(seq_size)], seq_rank)
        return jnp.concatenate(trade_near(pieces, "seq"), axis=0)

    def two_to_heads(first, second):
        pieces = reorder(
            [
                jnp.concatenate(
                    [first[:, k * span : (k + 1) * span], second[:, k * span : (k + 1) * span]], axis=1
                )
                for k in range(seq_size)
            ],
            seq_rank,
        )
        return jnp.concatenate(trade_near(pieces, "seq"), axis=0)

    def two_to_rows(first, second):
        both = jnp.concatenate([first, second], axis=1)
        pieces = [both[k * rows : (k + 1) * rows] for k in range(seq_size)]
        pieces = reorder(trade_near(pieces, "seq"), seq_rank)
        return jnp.concatenate(
            [piece[:, :span] for piece in pieces] + [piece[:, span:] for piece in pieces], axis=1
        )

    o_enc = to_rows(o_own)
    x_enc1 = x_enc0 + times(o_enc, enc_wout) + biases[2]
    x_enc2, h_enc2, up_enc, act_enc = mlp_forward(
        x_enc1, gains[1], shifts[1], enc_wup, up_bias[0], enc_wdown, biases[3]
    )
    enc_out = layer_norm(x_enc2, gains[2], shifts[2]).astype(bf16)
    dec_qkv, dec_wout, cross_wq, cross_wkv, cross_wout, dec_wup, dec_wdown = lay_out(
        dec_parts, dec_came, [(h, w // LANES) for h, w in dec_layout()], rank
    )
    paired = times(enc_out, cross_wkv)
    k_rows = paired[:, :D].astype(bf16)
    v_rows = (paired[:, D:] + biases[8]).astype(bf16)
    pair_cross = two_to_heads(k_rows, v_rows)
    k_cross = pair_cross[:, :span]
    v_cross = pair_cross[:, span:]

    ids = ids_slots[:, 0].reshape(-1)
    columns = jnp.arange(width)[None, :]
    inside = columns < vocab_here
    id_hot = ((ids[:, None] - vocab_first == columns) & inside).astype(bf16)
    looked = times_back(id_hot, table).astype(bf16).reshape(grp_size, LEN, D)
    part_rows = LEN // seq_size

    def share_rows(value, wire):
        pieces = [value[k * part_rows : (k + 1) * part_rows] for k in range(seq_size)]
        mine = scatter_near(reorder(pieces, seq_rank), "seq", wire)
        return jnp.concatenate(reorder(gather_near(mine.astype(wire), "seq"), seq_rank))

    token_emb = reduce_group(looked[::2], looked[1::2], bf16, bf16)
    token_emb = share_rows(token_emb, bf16).astype(f32)

    def all_heads(value):
        return reorder(gather_near(value, "seq"), seq_rank)

    x_dec0 = token_emb + positions
    h_dec1 = layer_norm(x_dec0, gains[3], shifts[3]).astype(bf16)
    packed = times(h_dec1, own(dec_qkv, 3))
    q_dec = (packed[:, :span] + own_bias(4)).astype(bf16)
    k_dec = packed[:, span : 2 * span].astype(bf16)
    v_dec = (packed[:, 2 * span :] + own_bias(5)).astype(bf16)
    no_bias = jnp.zeros((8, 1), f32)
    o_own_dec, lse_dec = attend_forward(q_dec, k_dec, v_dec, no_bias, True)
    o_dec = jnp.concatenate(all_heads(o_own_dec), axis=1)
    x_dec1 = x_dec0 + times(o_dec, dec_wout) + biases[6]
    h_dec2 = layer_norm(x_dec1, gains[4], shifts[4]).astype(bf16)
    q_cross = (times(h_dec2, own(cross_wq, 1)) + own_bias(7)).astype(bf16)
    o_own_cross, lse_cross = attend_forward(q_cross, k_cross, v_cross, frame_bias)
    o_cross = jnp.concatenate(all_heads(o_own_cross), axis=1)
    x_dec2 = x_dec1 + times(o_cross, cross_wout) + biases[9]
    x_dec3, h_dec3, up_dec, act_dec = mlp_forward(
        x_dec2, gains[5], shifts[5], dec_wup, up_bias[1], dec_wdown, biases[10]
    )
    states = layer_norm(x_dec3, gains[6], shifts[6]).astype(bf16)

    all_states = gather_group(states)
    target_rows = ids_slots[:, 1] - vocab_first
    target_rows = jnp.where(target_rows < vocab_here, target_rows, -1)[:, None, :]
    last = vocab - (grp_size - 1) * width
    stats = loss_forward(all_states, table, target_rows, vocab_here, group_rank, last)
    for bit in bits_of("grp"):
        stats = join_stats([stats, swap(stats, "grp", bit)])
    stats = join_stats(gather_near(stats, "seq"))
    log_total = stats[:, 0] + jnp.log(stats[:, 1])
    valid = (
        (jnp.arange(LEN)[None, :] < lengths[:, None]) & (present[:, None] > 0)
    ).astype(f32)
    token_total = jnp.sum((lengths * present).astype(f32))
    row_weight = valid / token_total
    scales = jnp.stack([log_total, row_weight], axis=1)
    loss_sum = jnp.sum((log_total - stats[:, 2]) * valid)
    grad_logits, states_kept, states_sent = loss_backward(
        all_states, table, target_rows, scales, vocab_here, group_rank, last
    )
    grad_states = share_rows(reduce_group(states_kept, states_sent, bf16), bf16).astype(f32)

    table_main = lax.optimization_barrier(
        over_rows(all_states.reshape(-1, D), grad_logits.reshape(-1, width))
    )

    grad_x3, grad_g6, grad_s6 = norm_back(grad_states, x_dec3, gains[6], shifts[6])
    dec_at = [0]
    for height, across in dec_layout():
        dec_at.append(dec_at[-1] + height * across // LANES)
    grad_x2, grad_down_dec, grad_up_dec, grad_dec_bup, grad_b10, grad_g5, grad_s5 = mlp_backward(
        grad_x3, x_dec2, gains[5], shifts[5], up_dec, dec_wup, dec_wdown
    )
    grad_branch = grad_x2.astype(bf16)
    grad_cross_out = grad_branch
    grad_b9 = column_sum(grad_branch)
    own_cross_wout = lax.dynamic_slice_in_dim(cross_wout, seq_rank * span, span, 0)
    grad_mixed = times_back(grad_branch, own_cross_wout).astype(bf16)
    grad_qc_own, grad_kc_own, grad_vc_own = attend_backward(
        grad_mixed, q_cross, k_cross, v_cross, lse_cross, frame_bias
    )
    grad_qc = jnp.concatenate(all_heads(grad_qc_own), axis=1)
    grad_pair = two_to_rows(grad_kc_own, grad_vc_own)
    grad_b7 = column_sum(grad_qc)
    grad_in, grad_g4, grad_s4 = norm_back(
        times_back(grad_qc, cross_wq), x_dec1, gains[4], shifts[4]
    )
    grad_x1 = grad_x2 + grad_in
    grad_branch = grad_x1.astype(bf16)
    grad_self_out = grad_branch
    grad_b6 = column_sum(grad_branch)
    own_dec_wout = lax.dynamic_slice_in_dim(dec_wout, seq_rank * span, span, 0)
    grad_mixed = times_back(grad_branch, own_dec_wout).astype(bf16)
    grad_qkv_own = attend_backward(grad_mixed, q_dec, k_dec, v_dec, lse_dec, no_bias, True)
    grad_qkv_own = jnp.concatenate(grad_qkv_own, axis=1)
    grad_qkv_all = all_heads(grad_qkv_own)
    grad_packed = jnp.concatenate(
        [
            piece[:, part * span : (part + 1) * span]
            for part in range(3)
            for piece in grad_qkv_all
        ],
        axis=1,
    )
    sums = column_sum(grad_packed)
    grad_b4 = sums[:D]
    grad_b5 = sums[2 * D :]
    grad_in, grad_g3, grad_s3 = norm_back(
        times_back(grad_packed, dec_qkv), x_dec0, gains[3], shifts[3]
    )
    grad_x0 = grad_x1 + grad_in

    grad_embed_all = gather_group(grad_x0.astype(bf16)).reshape(-1, D)
    grad_table = table_main + over_rows(grad_embed_all, id_hot)
    table_back = trade_near(
        [
            lax.dynamic_slice_in_dim(grad_table, (group_rank ^ k) * chans, chans, 0)
            for k in range(grp_size)
        ],
        "grp",
    )
    table_grad = jnp.concatenate(reorder(table_back, group_rank), axis=1)
    table_grad = table_grad[:, :vocab]

    wkv_buf = write_lines(None, enc_out, grad_pair, 2 * D * D // LANES, 0, 128)
    grad_b8 = column_sum(grad_pair[:, D:])
    grad_enc2, grad_g2, grad_s2 = norm_back(
        times_back(grad_pair, cross_wkv), x_enc2, gains[2], shifts[2]
    )

    dec_mine = own_blocks(
        [
            (h_dec1, grad_packed),
            (o_dec, grad_self_out),
            (h_dec2, grad_qc),
            (o_cross, grad_cross_out),
            (h_dec3, grad_up_dec),
            (act_dec, grad_down_dec),
        ],
        [dec_at[k] for k in (0, 1, 2, 4, 5, 6)],
        dec_lines,
        grp_size,
        seq_rank,
    )
    first_block = dec_at[3] // dec_lines
    turn = first_block % seq_size
    wkv_blocks = wkv_buf.reshape(seq_size, dec_lines, LANES)
    wkv_mine = scatter_near(
        [
            lax.dynamic_index_in_dim(wkv_blocks, (seq_rank ^ k) ^ turn, 0, False)
            for k in range(seq_size)
        ],
        "seq",
        f32,
    )
    wkv_place = (first_block + (seq_rank ^ turn)) // seq_size
    dec_mine = jnp.stack(
        [jnp.where(wkv_place == k, wkv_mine, dec_mine[k]) for k in range(grp_size)]
    )
    dec_grad = reduce_blocks(dec_mine[:, None], jnp.int32(0)).reshape(-1)

    enc_at = [0]
    for height, across in enc_layout()[:5]:
        enc_at.append(enc_at[-1] + height * across // LANES)
    enc_total = enc_lines * devices
    grad_enc1, grad_down, grad_up, grad_enc_bup, grad_b3, grad_g1, grad_s1 = mlp_backward(
        grad_enc2, x_enc1, gains[1], shifts[1], up_enc, enc_wup, enc_wdown
    )
    enc_buf = write_lines(None, act_enc, grad_down, enc_total, enc_at[3], 512)
    enc_buf = write_lines(enc_buf, h_enc2, grad_up, enc_total, enc_at[2], 128)
    grad_branch = grad_enc1.astype(bf16)
    enc_buf = write_lines(enc_buf, o_enc, grad_branch, enc_total, enc_at[1], 128)
    grad_b2 = column_sum(grad_branch)
    grad_mixed = times_back(grad_branch, enc_wout).astype(bf16)
    grad_mixed = to_heads(grad_mixed)
    grad_q, grad_k, grad_v = attend_backward(grad_mixed, q_enc, k_enc, v_enc, lse_enc, frame_bias)
    grad_packed = jnp.concatenate([grad_q, grad_k, grad_v], axis=1)
    enc_buf = write_lines(enc_buf, h_enc1, grad_packed, enc_total, 0, 128, own=seq_rank)
    sums = column_sum(grad_packed)

    def placed(values):
        return lax.dynamic_update_slice(jnp.zeros((D,), f32), values, (seq_rank * span,))

    grad_b0 = placed(sums[:span])
    grad_b1 = placed(sums[2 * span :])
    _, grad_g0, grad_s0 = norm_back(
        times_back(grad_packed, own_enc_qkv), x_all, gains[0], shifts[0]
    )
    once = lead
    grad_gains = jnp.stack(
        [grad_g0, grad_g1, grad_g2, grad_g3 * once, grad_g4 * once, grad_g5 * once, grad_g6 * once]
    )
    grad_shifts = jnp.stack(
        [grad_s0, grad_s1, grad_s2, grad_s3 * once, grad_s4 * once, grad_s5 * once, grad_s6 * once]
    )
    grad_biases = jnp.stack(
        [
            grad_b0,
            grad_b1,
            grad_b2,
            grad_b3,
            grad_b4 * once,
            grad_b5 * once,
            grad_b6 * once,
            grad_b7 * once,
            grad_b8,
            grad_b9 * once,
            grad_b10 * once,
        ]
    )
    grad_up_bias = jnp.stack([grad_enc_bup, grad_dec_bup * once])
    rest = jnp.concatenate(
        [grad_gains.reshape(-1), grad_shifts.reshape(-1), grad_biases.reshape(-1), grad_up_bias.reshape(-1)]
    ).reshape(-1, LANES)
    rest = jnp.pad(rest, ((0, enc_total - enc_at[5] - rest.shape[0]), (0, 0)))
    enc_buf = write_rest(enc_buf, grad_x0 * once, rest, enc_at[4])
    pairs = enc_buf.reshape(grp_size, 2, 2, enc_lines, LANES)
    upper = seq_rank // 2
    odd = seq_rank % 2
    away = reduce_blocks(pairs, 1 - upper)
    near = reduce_blocks(lax.optimization_barrier(pairs), upper)
    parts = [
        swap(lax.dynamic_index_in_dim(away, odd, 0, False), "seq", 2),
        swap(lax.dynamic_index_in_dim(away, 1 - odd, 0, False), "seq", 3),
    ]
    parts.append(swap(lax.dynamic_index_in_dim(near, 1 - odd, 0, False), "seq", 1))
    enc_sum = lax.dynamic_index_in_dim(near, odd, 0, False) + parts[2] + (parts[0] + parts[1])
    enc_prev = lax.ppermute(
        enc_sum[enc_lines - lag * devices // LANES :].reshape(-1),
        ("grp", "seq"),
        [(i, i + 1) for i in range(devices - 1)],
    )
    enc_grad = lax.dynamic_slice_in_dim(
        jnp.concatenate([enc_prev, enc_sum.reshape(-1)]), lag * (devices - rank), enc_count
    )

    squares = (
        jnp.sum(enc_sum * enc_sum)
        + jnp.sum(dec_grad * dec_grad)
        + jnp.sum(table_grad * table_grad)
    )
    squares = all_join(pair_join(squares.reshape(1, 1), "grp", jnp.add), "seq", jnp.add)
    mean_loss = loss_sum / token_total
    grad_norm = jnp.sqrt(squares[0, 0])
    factor = jnp.minimum(1.0, clip_limit / (grad_norm + 1e-06))
    steps_done = step_count[0].astype(f32)
    bias_one = 1.0 - beta_one**steps_done
    bias_two = 1.0 - beta_two**steps_done
    enc_new = adamw(enc_params, enc_moment, enc_second, enc_grad, factor, bias_one, bias_two)
    dec_new = adamw(dec_params, dec_moment, dec_second, dec_grad, factor, bias_one, bias_two)
    table_new = adamw(
        table_params, table_moment, table_second, table_grad, factor, bias_one, bias_two
    )
    return (mean_loss, grad_norm, *enc_new, *dec_new, *table_new)


def wide_joined_2(value, axis, join):
    pieces = jax.tree.map(lambda part: lax.all_gather(part, axis), value)
    head = jax.tree.map(lambda part: part[0], pieces)
    tail = jax.tree.map(lambda part: part[1:], pieces)
    total, _ = lax.scan(lambda total, piece: (join(total, piece), None), head, tail)
    return total


def wide_sinusoid(amount, channels, offset):
    half_width = channels // 2
    stride = math.log(10000.0) / (half_width - 1)
    inverse = jnp.exp(-stride * jnp.arange(half_width, dtype=jnp.float32))
    angles = (jnp.arange(amount, dtype=jnp.float32) + offset)[:, None] * inverse[None, :]
    return jnp.concatenate([jnp.sin(angles), jnp.cos(angles)], axis=1)


def wide_times_rows(left_side, right_side):
    return lax.dot_general(
        left_side,
        right_side,
        (((left_side.ndim - 1,), (0,)), ((), ())),
        preferred_element_type=jnp.float32,
    )


def wide_times_back(left_side, right_side):
    return lax.dot_general(
        left_side,
        right_side,
        (((left_side.ndim - 1,), (1,)), ((), ())),
        preferred_element_type=jnp.float32,
    )


def wide_over_rows(left_side, right_side):
    return lax.dot_general(
        left_side, right_side, (((0, 1), (0, 1)), ((), ())), preferred_element_type=jnp.float32
    )


def wide_column_sum(values):
    return jnp.sum(values.astype(jnp.float32), axis=(0, 1))


def wide_split_heads(values):
    return values.reshape(values.shape[0], values.shape[1], HEADS, values.shape[2] // HEADS)


def wide_score_block(query, keys, first_row):
    head_size = query.shape[2] // HEADS
    scores = jnp.einsum(
        "cqhd,ckhd->chqk", wide_split_heads(query), wide_split_heads(keys), preferred_element_type=jnp.float32
    ) * head_size ** (-0.5)
    if first_row is not None:
        allowed = (first_row + jnp.arange(query.shape[1]))[:, None] >= jnp.arange(keys.shape[1])[
            None, :
        ]
        scores = jnp.where(allowed[None, None], scores, masked_score)
    return scores


def wide_attend_forward(query, keys, values, first_row):
    scores = wide_score_block(query, keys, first_row)
    highest_score = jnp.max(scores, axis=-1, keepdims=True)
    log_total = highest_score + jnp.log(
        jnp.sum(jnp.exp(scores - highest_score), axis=-1, keepdims=True)
    )
    weights = jnp.exp(scores - log_total).astype(jnp.bfloat16)
    mixed = jnp.einsum(
        "chqk,ckhd->cqhd", weights, wide_split_heads(values), preferred_element_type=jnp.float32
    )
    return (mixed.reshape(query.shape).astype(jnp.bfloat16), log_total)


def wide_attend_backward(grad_mixed, query, keys, values, log_total, first_row):
    head_size = query.shape[2] // HEADS
    scores = wide_score_block(query, keys, first_row)
    weights = jnp.exp(scores - log_total)
    grad_heads = wide_split_heads(grad_mixed)
    grad_weights = jnp.einsum(
        "cqhd,ckhd->chqk", grad_heads, wide_split_heads(values), preferred_element_type=jnp.float32
    )
    grad_values = jnp.einsum(
        "chqk,cqhd->ckhd",
        weights.astype(jnp.bfloat16),
        grad_heads,
        preferred_element_type=jnp.float32,
    )
    inner = jnp.sum(weights * grad_weights, axis=-1, keepdims=True)
    grad_scores = (weights * (grad_weights - inner)).astype(jnp.bfloat16)
    grad_query = jnp.einsum(
        "chqk,ckhd->cqhd", grad_scores, wide_split_heads(keys), preferred_element_type=jnp.float32
    ) * head_size ** (-0.5)
    grad_keys = jnp.einsum(
        "chqk,cqhd->ckhd", grad_scores, wide_split_heads(query), preferred_element_type=jnp.float32
    ) * head_size ** (-0.5)
    return (
        grad_query.reshape(query.shape),
        grad_keys.reshape(keys.shape),
        grad_values.reshape(values.shape),
    )


def wide_mlp_forward(stream, norm_gain, norm_shift, w_up, b_up, w_down, b_down):
    normed = layer_norm(stream, norm_gain, norm_shift).astype(jnp.bfloat16)
    raised = wide_times_rows(normed, w_up) + b_up
    active = jax.nn.gelu(raised, approximate=False).astype(jnp.bfloat16)
    return (stream + wide_times_rows(active, w_down) + b_down, normed, raised, active)


def wide_mlp_backward(grad_stream, stream, norm_gain, norm_shift, normed, raised, active, w_up, w_down):
    grad_branch = grad_stream.astype(jnp.bfloat16)
    grad_wdown = wide_over_rows(active, grad_branch)
    grad_bdown = wide_column_sum(grad_branch)
    grad_active = wide_times_back(grad_branch, w_down)
    _, gelu_pull = jax.vjp(partial(jax.nn.gelu, approximate=False), raised)
    grad_raised = gelu_pull(grad_active)[0].astype(jnp.bfloat16)
    grad_wup = wide_over_rows(normed, grad_raised)
    grad_bup = wide_column_sum(grad_raised)
    grad_normed = wide_times_back(grad_raised, w_up)
    grad_in, grad_gain, grad_shift = norm_back(grad_normed, stream, norm_gain, norm_shift)
    return (
        grad_stream + grad_in,
        grad_wup,
        grad_bup,
        grad_wdown,
        grad_bdown,
        grad_gain,
        grad_shift,
    )


def wide_merge_stats(first_stats, second_stats):
    biggest = jnp.maximum(first_stats[0], second_stats[0])
    summed = first_stats[1] * jnp.exp(first_stats[0] - biggest) + second_stats[1] * jnp.exp(
        second_stats[0] - biggest
    )
    return (biggest, summed, first_stats[2] + second_stats[2])


def wide_spread_grads(grad_matrix):
    return lax.psum_scatter(grad_matrix, ("grp", "seq"), scatter_dimension=0, tiled=True)


def wide_on_device(
    frames,
    input_ids,
    target_ids,
    lengths,
    present,
    step_count,
    enc_params,
    enc_moment,
    enc_second,
    dec_params,
    dec_moment,
    dec_second,
    table_params,
    table_moment,
    table_second,
):
    enc_full, dec_full = (
        lax.all_gather(enc_params.astype(jnp.bfloat16), ("grp", "seq"), axis=0, tiled=True),
        lax.all_gather(dec_params.astype(jnp.bfloat16), ("grp", "seq"), axis=0, tiled=True),
    )
    table_local = lax.all_gather(table_params.astype(jnp.bfloat16), "grp", axis=0, tiled=True)
    enc_qkv, enc_wout, enc_wup, enc_wdown, positions, gains, shifts, biases, up_bias = split_flat(
        enc_full, enc_layout()
    )
    dec_qkv, dec_wout, cross_wq, cross_wkv, cross_wout, dec_wup, dec_wdown = split_flat(
        dec_full, dec_layout()
    )
    gains = gains.astype(jnp.float32)
    shifts = shifts.astype(jnp.float32)
    biases = biases.astype(jnp.float32)
    up_bias = up_bias.astype(jnp.float32)
    positions = positions.astype(jnp.float32)
    seq_size = lax.axis_size("seq")
    seq_rank = lax.axis_index("seq")
    group_rank = lax.axis_index("grp")
    clip_count = frames.shape[0]
    enc_rows = frames.shape[1]
    dec_rows = LEN // seq_size
    vocab_rows = table_local.shape[1]
    dec_first = seq_rank * dec_rows
    vocab_first = seq_rank * vocab_rows
    x_enc0 = (
        frames.astype(jnp.float32)
        + wide_sinusoid(enc_rows, D, (seq_rank * enc_rows).astype(jnp.float32))[None]
    )
    h_enc1 = layer_norm(x_enc0, gains[0], shifts[0]).astype(jnp.bfloat16)
    packed = wide_times_rows(h_enc1, enc_qkv)
    q_enc = (packed[..., :D] + biases[0]).astype(jnp.bfloat16)
    k_enc = packed[..., D : 2 * D].astype(jnp.bfloat16)
    v_enc = (packed[..., 2 * D :] + biases[1]).astype(jnp.bfloat16)
    keys_enc, vals_enc = (
        lax.all_gather(k_enc, "seq", axis=1, tiled=True),
        lax.all_gather(v_enc, "seq", axis=1, tiled=True),
    )
    o_enc, lse_enc = wide_attend_forward(q_enc, keys_enc, vals_enc, None)
    x_enc1 = x_enc0 + wide_times_rows(o_enc, enc_wout) + biases[2]
    x_enc2, h_enc2, up_enc, act_enc = wide_mlp_forward(
        x_enc1, gains[1], shifts[1], enc_wup, up_bias[0], enc_wdown, biases[3]
    )
    enc_out = layer_norm(x_enc2, gains[2], shifts[2]).astype(jnp.bfloat16)
    local_ids = input_ids - vocab_first
    inside = (local_ids >= 0) & (local_ids < vocab_rows)
    safe_ids = jnp.clip(local_ids, 0, vocab_rows - 1).reshape(-1)
    looked = jnp.take(table_local, safe_ids, axis=1).astype(jnp.float32).T
    looked = jnp.where(inside.reshape(-1)[:, None], looked, 0.0).reshape(clip_count, LEN, D)
    token_emb = lax.psum_scatter(
        looked.astype(jnp.bfloat16), "seq", scatter_dimension=1, tiled=True
    ).astype(jnp.float32)
    x_dec0 = token_emb + lax.dynamic_slice_in_dim(positions, dec_first, dec_rows, 0)[None]
    h_dec1 = layer_norm(x_dec0, gains[3], shifts[3]).astype(jnp.bfloat16)
    packed = wide_times_rows(h_dec1, dec_qkv)
    q_dec = (packed[..., :D] + biases[4]).astype(jnp.bfloat16)
    k_dec = packed[..., D : 2 * D].astype(jnp.bfloat16)
    v_dec = (packed[..., 2 * D :] + biases[5]).astype(jnp.bfloat16)
    paired = wide_times_rows(enc_out, cross_wkv)
    k_cross = paired[..., :D].astype(jnp.bfloat16)
    v_cross = (paired[..., D:] + biases[8]).astype(jnp.bfloat16)
    keys_dec, vals_dec, keys_cross, vals_cross = (
        lax.all_gather(k_dec, "seq", axis=1, tiled=True),
        lax.all_gather(v_dec, "seq", axis=1, tiled=True),
        lax.all_gather(k_cross, "seq", axis=1, tiled=True),
        lax.all_gather(v_cross, "seq", axis=1, tiled=True),
    )
    o_dec, lse_dec = wide_attend_forward(q_dec, keys_dec, vals_dec, dec_first)
    x_dec1 = x_dec0 + wide_times_rows(o_dec, dec_wout) + biases[6]
    h_dec2 = layer_norm(x_dec1, gains[4], shifts[4]).astype(jnp.bfloat16)
    q_cross = (wide_times_rows(h_dec2, cross_wq) + biases[7]).astype(jnp.bfloat16)
    o_cross, lse_cross = wide_attend_forward(q_cross, keys_cross, vals_cross, None)
    x_dec2 = x_dec1 + wide_times_rows(o_cross, cross_wout) + biases[9]
    x_dec3, h_dec3, up_dec, act_dec = wide_mlp_forward(
        x_dec2, gains[5], shifts[5], dec_wup, up_bias[1], dec_wdown, biases[10]
    )
    states = layer_norm(x_dec3, gains[6], shifts[6]).astype(jnp.bfloat16)
    all_states = lax.all_gather(states, "seq", axis=1, tiled=True)
    logits = wide_times_rows(all_states, table_local)
    target_local = target_ids - vocab_first
    has_target = (target_local >= 0) & (target_local < vocab_rows)
    top_local = jnp.max(logits, axis=-1)
    total_local = jnp.sum(jnp.exp(logits - top_local[..., None]), axis=-1)
    picked_local = jnp.take_along_axis(
        logits, jnp.clip(target_local, 0, vocab_rows - 1)[..., None], axis=-1
    )[..., 0]
    picked_local = jnp.where(has_target, picked_local, 0.0)
    top_all, total_all, picked_all = wide_joined_2(
        (top_local, total_local, picked_local), "seq", wide_merge_stats
    )
    log_total = top_all + jnp.log(total_all)
    my_lengths = lax.dynamic_slice_in_dim(lengths, group_rank * clip_count, clip_count)
    my_present = lax.dynamic_slice_in_dim(present, group_rank * clip_count, clip_count)
    valid = ((jnp.arange(LEN)[None, :] < my_lengths[:, None]) & (my_present[:, None] > 0)).astype(
        jnp.float32
    )
    token_total = jnp.sum((lengths * present).astype(jnp.float32))
    token_loss = (log_total - picked_all) * valid
    loss_part = jnp.sum(lax.dynamic_slice_in_dim(token_loss, dec_first, dec_rows, 1))
    row_weight = valid / token_total
    onehot = (jnp.arange(vocab_rows)[None, None, :] == target_local[..., None]).astype(jnp.float32)
    grad_logits = (
        (jnp.exp(logits - log_total[..., None]) - onehot) * row_weight[..., None]
    ).astype(jnp.bfloat16)
    grad_states_all = wide_times_back(grad_logits, table_local)
    grad_table = wide_over_rows(all_states, grad_logits)
    grad_states = lax.psum_scatter(
        grad_states_all.astype(jnp.bfloat16), "seq", scatter_dimension=1, tiled=True
    ).astype(jnp.float32)
    grad_x3, grad_g6, grad_s6 = norm_back(grad_states, x_dec3, gains[6], shifts[6])
    grad_x2, grad_dec_up, grad_dec_bup, grad_dec_down, grad_b10, grad_g5, grad_s5 = wide_mlp_backward(
        grad_x3, x_dec2, gains[5], shifts[5], h_dec3, up_dec, act_dec, dec_wup, dec_wdown
    )
    grad_branch = grad_x2.astype(jnp.bfloat16)
    grad_cross_wout = wide_over_rows(o_cross, grad_branch)
    grad_b9 = wide_column_sum(grad_branch)
    grad_mixed = wide_times_back(grad_branch, cross_wout).astype(jnp.bfloat16)
    grad_qc, grad_kc, grad_vc = wide_attend_backward(
        grad_mixed, q_cross, keys_cross, vals_cross, lse_cross, None
    )
    grad_qc = grad_qc.astype(jnp.bfloat16)
    grad_cross_wq = wide_over_rows(h_dec2, grad_qc)
    grad_b7 = wide_column_sum(grad_qc)
    grad_in, grad_g4, grad_s4 = norm_back(
        wide_times_back(grad_qc, cross_wq), x_dec1, gains[4], shifts[4]
    )
    grad_x1 = grad_x2 + grad_in
    grad_branch = grad_x1.astype(jnp.bfloat16)
    grad_dec_wout = wide_over_rows(o_dec, grad_branch)
    grad_b6 = wide_column_sum(grad_branch)
    grad_mixed = wide_times_back(grad_branch, dec_wout).astype(jnp.bfloat16)
    grad_qd, grad_kd, grad_vd = wide_attend_backward(
        grad_mixed, q_dec, keys_dec, vals_dec, lse_dec, dec_first
    )
    grad_kd, grad_vd, grad_kc, grad_vc = (
        lax.psum_scatter(
            grad_kd.astype(jnp.bfloat16), "seq", scatter_dimension=1, tiled=True
        ).astype(jnp.float32),
        lax.psum_scatter(
            grad_vd.astype(jnp.bfloat16), "seq", scatter_dimension=1, tiled=True
        ).astype(jnp.float32),
        lax.psum_scatter(
            grad_kc.astype(jnp.bfloat16), "seq", scatter_dimension=1, tiled=True
        ).astype(jnp.float32),
        lax.psum_scatter(
            grad_vc.astype(jnp.bfloat16), "seq", scatter_dimension=1, tiled=True
        ).astype(jnp.float32),
    )
    grad_qd = grad_qd.astype(jnp.bfloat16)
    grad_vd = grad_vd.astype(jnp.bfloat16)
    grad_packed = jnp.concatenate([grad_qd, grad_kd.astype(jnp.bfloat16), grad_vd], axis=-1)
    grad_dec_qkv = wide_over_rows(h_dec1, grad_packed)
    grad_b4 = wide_column_sum(grad_qd)
    grad_b5 = wide_column_sum(grad_vd)
    grad_in, grad_g3, grad_s3 = norm_back(
        wide_times_back(grad_packed, dec_qkv), x_dec0, gains[3], shifts[3]
    )
    grad_x0 = grad_x1 + grad_in
    grad_positions = lax.dynamic_update_slice_in_dim(
        jnp.zeros((LEN, D), jnp.float32), jnp.sum(grad_x0, axis=0), dec_first, 0
    )
    grad_embed_all = lax.all_gather(grad_x0.astype(jnp.bfloat16), "seq", axis=1, tiled=True).astype(
        grad_x0.dtype
    )
    grad_embed_all = jnp.where(inside.reshape(-1)[:, None], grad_embed_all.reshape(-1, D), 0.0)
    grad_table = grad_table.at[:, safe_ids].add(grad_embed_all.T)
    grad_vc = grad_vc.astype(jnp.bfloat16)
    grad_pair = jnp.concatenate([grad_kc.astype(jnp.bfloat16), grad_vc], axis=-1)
    grad_cross_wkv = wide_over_rows(enc_out, grad_pair)
    grad_b8 = wide_column_sum(grad_vc)
    grad_enc2, grad_g2, grad_s2 = norm_back(
        wide_times_back(grad_pair, cross_wkv), x_enc2, gains[2], shifts[2]
    )
    device_count = lax.axis_size(("grp", "seq"))
    dec_flat = jnp.concatenate(
        [
            grad_dec_qkv.reshape(-1),
            grad_dec_wout.reshape(-1),
            grad_cross_wq.reshape(-1),
            grad_cross_wkv.reshape(-1),
            grad_cross_wout.reshape(-1),
            grad_dec_up.reshape(-1),
            grad_dec_down.reshape(-1),
        ]
    )
    dec_matrix = dec_flat.reshape(device_count, -1)
    dec_columns = dec_matrix.shape[1]
    grad_enc1, grad_enc_up, grad_enc_bup, grad_enc_down, grad_b3, grad_g1, grad_s1 = wide_mlp_backward(
        grad_enc2, x_enc1, gains[1], shifts[1], h_enc2, up_enc, act_enc, enc_wup, enc_wdown
    )
    grad_branch = grad_enc1.astype(jnp.bfloat16)
    grad_enc_wout = wide_over_rows(o_enc, grad_branch)
    grad_b2 = wide_column_sum(grad_branch)
    grad_mixed = wide_times_back(grad_branch, enc_wout).astype(jnp.bfloat16)
    grad_qe, grad_ke, grad_ve = wide_attend_backward(
        grad_mixed, q_enc, keys_enc, vals_enc, lse_enc, None
    )
    grad_ke, grad_ve = (
        lax.psum_scatter(
            grad_ke.astype(jnp.bfloat16), "seq", scatter_dimension=1, tiled=True
        ).astype(jnp.float32),
        lax.psum_scatter(
            grad_ve.astype(jnp.bfloat16), "seq", scatter_dimension=1, tiled=True
        ).astype(jnp.float32),
    )
    grad_qe = grad_qe.astype(jnp.bfloat16)
    grad_ve = grad_ve.astype(jnp.bfloat16)
    grad_packed = jnp.concatenate([grad_qe, grad_ke.astype(jnp.bfloat16), grad_ve], axis=-1)
    grad_enc_qkv = wide_over_rows(h_enc1, grad_packed)
    grad_b0 = wide_column_sum(grad_qe)
    grad_b1 = wide_column_sum(grad_ve)
    _, grad_g0, grad_s0 = norm_back(
        wide_times_back(grad_packed, enc_qkv), x_enc0, gains[0], shifts[0]
    )
    grad_gains = jnp.stack([grad_g0, grad_g1, grad_g2, grad_g3, grad_g4, grad_g5, grad_g6])
    grad_shifts = jnp.stack([grad_s0, grad_s1, grad_s2, grad_s3, grad_s4, grad_s5, grad_s6])
    grad_biases = jnp.stack(
        [
            grad_b0,
            grad_b1,
            grad_b2,
            grad_b3,
            grad_b4,
            grad_b5,
            grad_b6,
            grad_b7,
            grad_b8,
            grad_b9,
            grad_b10,
        ]
    )
    grad_up_bias = jnp.stack([grad_enc_bup, grad_dec_bup])
    enc_flat = jnp.concatenate(
        [
            grad_enc_qkv.reshape(-1),
            grad_enc_wout.reshape(-1),
            grad_enc_up.reshape(-1),
            grad_enc_down.reshape(-1),
            grad_positions.reshape(-1),
            grad_gains.reshape(-1),
            grad_shifts.reshape(-1),
            grad_biases.reshape(-1),
            grad_up_bias.reshape(-1),
        ]
    )
    enc_matrix = enc_flat.reshape(device_count, -1)
    joined = wide_spread_grads(jnp.concatenate([dec_matrix, enc_matrix], axis=1))
    dec_grad = joined[:, :dec_columns].reshape(-1)
    enc_grad = joined[:, dec_columns:].reshape(-1)
    table_grad = lax.psum_scatter(grad_table, "grp", scatter_dimension=0, tiled=True)
    squares = (
        jnp.sum(enc_grad * enc_grad)
        + jnp.sum(dec_grad * dec_grad)
        + jnp.sum(table_grad * table_grad)
    )
    loss_sum, square_sum = lax.psum((loss_part, squares), ("grp", "seq"))
    mean_loss = loss_sum / token_total
    grad_norm = jnp.sqrt(square_sum)
    factor = jnp.minimum(1.0, clip_limit / (grad_norm + 1e-06))
    steps_done = step_count[0].astype(jnp.float32)
    bias_one = 1.0 - beta_one**steps_done
    bias_two = 1.0 - beta_two**steps_done
    enc_new = adamw(enc_params, enc_moment, enc_second, enc_grad, factor, bias_one, bias_two)
    dec_new = adamw(dec_params, dec_moment, dec_second, dec_grad, factor, bias_one, bias_two)
    table_new = adamw(
        table_params, table_moment, table_second, table_grad, factor, bias_one, bias_two
    )
    return (
        mean_loss,
        grad_norm,
        enc_new[0],
        enc_new[1],
        enc_new[2],
        dec_new[0],
        dec_new[1],
        dec_new[2],
        table_new[0],
        table_new[1],
        table_new[2],
    )


def solution(mesh):
    flat = P(("grp", "seq"))
    both = P("grp", "seq")
    in_specs = (
        P("grp", "seq", None),
        P("grp", None),
        P("grp", None),
        P(),
        P(),
        P(),
        flat,
        flat,
        flat,
        flat,
        flat,
        flat,
        both,
        both,
        both,
    )
    out_specs = (P(), P(), flat, flat, flat, flat, flat, flat, both, both, both)
    few = mesh.shape["grp"] == 8
    return jax.shard_map(
        on_device if few else wide_on_device,
        mesh=mesh,
        in_specs=in_specs,
        out_specs=out_specs,
        check_vma=False,
    )
```
